512 devices in a mesh: pb: 128 (over z, x, core), vert: 4 (over y).
Axes of the slice: x: 4, y: 4, z: 16, core: 2. Of those that a mesh axis runs over, the one named last changes fastest.
Arguments:
- orbitals: bfloat16 [256, 32, 1024], P('pb', None, 'vert'), may hold values from -6 to 6
- transition: float32 [256, 256], P('pb'), may hold values from -0.9 to 0.9
- trial: float32 [8, 256, 256], P('vert', 'pb'), may hold values from -6 to 6
- screened: bfloat16 [256, 1024, 1024], P('pb', None, 'vert'), may hold values from -0.00030517578 to 0.00030517578
- bare: bfloat16 [1024, 1024], replicated, may hold values from -6.1035156e-05 to 6.1035156e-05
- cheb: float32 [3], replicated, may hold values from 0.5 to 1.5
- pair_k: int32 [384], P('pb'), may hold values from 0 to 255
- pair_slot: int32 [384], P('pb'), may hold values from 0 to 1
- k_order: int32 [256], replicated, may hold values from 0 to 255, each once
Outputs:
- filtered: float32 [8, 256, 256], P('vert', 'pb')
The draws below stay inside these ranges and needn't reach their ends.
Inputs may be any that keep to these rules, and one draw needn't show every extreme that they name: The pair i lies with the owner of its momentum transfer 2 * (i // 3) + pair_slot[i]. `k_order`: A permutation of the k-points.
All inputs are finite; a program needn't handle non-finite values.
Results may differ from the reference program's by a relative error of at most 0.0075.
Values may be sent and summed in bfloat16 or wider, within the bound.
No kernel may reach another device: no remote copies, remote signals or barrier semaphores. Data moves between devices by JAX's collectives and lax.ppermute only.
A program may use at most 64 MiB of HBM per device.

```python
import math
import jax
import jax.numpy as jnp
import numpy as np
from jax import lax

NV = 16
NC = 16
NP = 1024
K_DEV = 2
NVEC = 8
PAIRS_DEV = 3
NK = 256
PAIRS = 384
NB = 32
VC = 256


def place_ends(entries, rng, smallest, high):
    dims = entries.shape
    index_at = [jax.random.randint(jax.random.fold_in(rng, axis), (), 0, dims[axis]) for axis in range(len(dims))]
    entries = entries.at[tuple(index_at)].set(smallest)
    longest = dims.index(max(dims))
    index_at[longest] = (index_at[longest] + 1) % dims[longest]
    return entries.at[tuple(index_at)].set(high)


def block_levels(stream_key, extent, split, smallest, top_value):
    level, own = 1.0, jax.random.fold_in(stream_key, 6)
    for position, blocks in split:
        steps = jnp.exp(jax.random.uniform(jax.random.fold_in(own, position), (blocks,), jnp.float32, smallest / len(split), top_value / len(split)))
        level = level * jnp.repeat(steps, extent[position] // blocks).reshape([-1 if axis == position else 1 for axis in range(len(extent))])
    return level


def rank_bounds(number_of, lean):
    portions = [(1 << 20) // math.isqrt(grade ** lean) + 1 for grade in range(1, number_of + 1)]
    spread = 1 + sum(portions) // (1 << 30)
    return np.cumsum(np.array([max(1, weight // spread) for weight in portions]))


def skewed_ids(own_key, extent, count, slope):
    listing = rank_bounds(count, slope)
    lot = jax.random.randint(jax.random.fold_in(own_key, 1), extent, 0, int(listing[count - 1]))
    standing = jnp.searchsorted(jnp.asarray(listing, jnp.int32), lot, side="right")
    return jax.random.permutation(jax.random.fold_in(own_key, 2), count)[standing].astype(jnp.int32)


def scatter_about(key, dims, spread, most, cuts=(), kind=jnp.bfloat16):
    result = jax.random.normal(key, dims, jnp.float32) * spread
    if len(cuts) > 0:
        result = block_levels(key, dims, cuts, -0.22, 0.18) * result
    return jnp.clip(result, min=-most, max=most).astype(kind)


def setup_inputs(seed: int = 0) -> dict:
    splits = jax.random.split(jax.random.key(seed), 10)
    orbitals = scatter_about(splits[0], (NK, NB, NP), 1.0, 6.0, ((0, 128), (2, 4)))
    transition = jnp.clip(jax.random.uniform(splits[1], (NK, VC), jnp.float32, -0.9, 0.9) * block_levels(splits[1], (NK, VC), ((0, 128),), -0.4, 0.0), -0.9, 0.9)
    trial = scatter_about(splits[2], (NVEC, NK, VC), 1.0, 6.0, ((0, 4), (1, 128)), jnp.float32)
    screened = scatter_about(splits[3], (NK, NP, NP), (1.0 / (48 * NP)), 0.00030517578, ((0, 128), (2, 4)))
    bare = scatter_about(splits[4], (NP, NP), (1.0 / (256 * NP)), 6.103515625e-05)
    cheb = jnp.clip(jax.random.uniform(splits[5], (3,), jnp.float32, 0.5, 1.5), 0.5, 1.5)
    pair_k = place_ends(skewed_ids(splits[6], (PAIRS,), NK, 2), jax.random.fold_in(splits[6], 3), 0, NK - 1).astype(jnp.int32)
    pair_slot = place_ends(jax.random.randint(splits[7], (PAIRS,), 0, K_DEV), jax.random.fold_in(splits[7], 1), 0, K_DEV - 1).astype(jnp.int32)
    k_order = jax.random.permutation(splits[8], NK).astype(jnp.int32)
    return {"orbitals": orbitals, "transition": transition, "trial": trial, "screened": screened, "bare": bare, "cheb": cheb, "pair_k": pair_k, "pair_slot": pair_slot, "k_order": k_order}


def reference(orbitals, transition, trial, screened, bare, cheb, pair_k, pair_slot, k_order):
    storage = jnp.zeros((NK,), jnp.int32).at[k_order].set(jnp.arange(NK, dtype=jnp.int32))
    transfer = ((jnp.arange(PAIRS, dtype=jnp.int32) // PAIRS_DEV) * K_DEV + pair_slot).astype(jnp.int32)
    partner = jnp.mod(pair_k - transfer, NK).astype(jnp.int32)
    row_first = storage[pair_k]
    row_second = storage[partner]
    pair_width = NV * NC

    def build_block(pair_index):
        orb_first = orbitals[row_first[pair_index]].astype(jnp.float32)
        orb_second = orbitals[row_second[pair_index]].astype(jnp.float32)
        left_pair = (orb_first[:NV, None, :] * orb_second[None, :NV, :]).reshape(NV * NV, NP).astype(jnp.bfloat16)
        right_pair = (orb_first[NV:, None, :] * orb_second[None, NV:, :]).reshape(NC * NC, NP).astype(jnp.bfloat16)
        half_product = jnp.dot(left_pair, screened[transfer[pair_index]], preferred_element_type=jnp.float32).astype(jnp.bfloat16)
        block_full = jnp.dot(half_product, right_pair.T, preferred_element_type=jnp.float32)
        return block_full.reshape(NV, NV, NC, NC).transpose(0, 2, 1, 3).reshape(pair_width, pair_width)

    blocks = lax.map(build_block, jnp.arange(PAIRS, dtype=jnp.int32))
    orb_all = orbitals.astype(jnp.float32)
    products = (orb_all[:, :NV, None, :] * orb_all[:, None, NV:, :]).reshape(NK, pair_width, NP).astype(jnp.bfloat16)
    hp = lax.Precision.HIGHEST

    def apply_kernel(current):
        gathered_first = current[:, row_first].astype(jnp.float32)
        gathered_second = current[:, row_second].astype(jnp.float32)
        toward_first = jnp.einsum("pij,npj->npi", blocks, gathered_second, precision=hp)
        toward_second = jnp.einsum("pij,npi->npj", blocks, gathered_first, precision=hp)
        screened_term = jnp.zeros((NVEC, NK, pair_width), jnp.float32)
        screened_term = screened_term.at[:, row_first].add(toward_first).at[:, row_second].add(toward_second)
        density = jnp.einsum("nkj,kjm->nm", current.astype(jnp.float32), products.astype(jnp.float32), precision=hp).astype(jnp.bfloat16)
        potential = jnp.dot(density, bare.T, preferred_element_type=jnp.float32).astype(jnp.bfloat16)
        bare_term = jnp.einsum("kjm,nm->nkj", products.astype(jnp.float32), potential.astype(jnp.float32), precision=hp)
        return transition[None] * current.astype(jnp.float32) + 2.0 * bare_term - screened_term

    first_step = apply_kernel(trial.astype(jnp.bfloat16))
    second_step = 2.0 * apply_kernel(first_step.astype(jnp.bfloat16)) - trial
    return cheb[0] * trial + cheb[1] * first_step + cheb[2] * second_step
```

```python
import functools

import jax
import jax.numpy as jnp
from jax import lax
from jax.experimental import pallas as pl
from jax.experimental.pallas import tpu as pltpu
from jax.sharding import Mesh
from jax.sharding import PartitionSpec as P

BF = jnp.bfloat16
F32 = jnp.float32
NV = 16
LAST = (((1,), (1,)), ((), ()))
PB = ("z", "x", "c")
PLANE = ("x", "c")
BLOCK = ("x", "c", "y")


def exchange(blocks, axis):
    return lax.all_to_all(blocks, axis, 0, 0, tiled=True)


def to_everyone(shard, axis):
    count = lax.axis_size(axis)
    return exchange(jnp.broadcast_to(shard[None], (count, *shard.shape)), axis)


def dot(a, b):
    return jnp.dot(a, b, preferred_element_type=F32)


def dot_t(a, b):
    return lax.dot_general(a, b, LAST, preferred_element_type=F32)


def call(kernel, outs, smem, scratch=()):
    def run(*args):
        specs = [
            pl.BlockSpec(memory_space=pltpu.SMEM if k in smem else pltpu.VMEM)
            for k in range(len(args))
        ]
        return pl.pallas_call(
            kernel,
            out_shape=[jax.ShapeDtypeStruct(s, d) for s, d in outs],
            in_specs=specs,
            out_specs=[pl.BlockSpec(memory_space=pltpu.VMEM) for _ in outs],
            scratch_shapes=list(scratch),
        )(*args)

    return run


def lanes(rows, width):
    return lax.broadcasted_iota(jnp.int32, (rows, width), 1)


def products_of(own_ref, s, part):
    val = own_ref[part, s, 0:16, :].astype(F32)
    cond = own_ref[part, s, 16:32, :].astype(F32)
    pieces = [(val[v : v + 1, :] * cond).astype(BF) for v in range(16)]
    return jnp.concatenate(pieces, axis=0)


def density_of(own_ref, rows_bf):
    parts = []
    for part in range(4):
        total = dot(rows_bf[0], products_of(own_ref, 0, part))
        total = total + dot(rows_bf[1], products_of(own_ref, 1, part))
        parts.append(total)
    return parts


def bare_of(own_ref, bare_ref, dens):
    pots = []
    for out in range(4):
        total = jnp.zeros((2, 256), F32)
        for part in range(4):
            total = total + dot_t(
                dens[part].astype(BF),
                bare_ref[out * 256 : (out + 1) * 256, part * 256 : (part + 1) * 256],
            )
        pots.append(total.astype(BF))
    terms = []
    for s in range(2):
        total = jnp.zeros((2, 256), F32)
        for part in range(4):
            total = total + dot_t(pots[part], products_of(own_ref, s, part))
        terms.append(total)
    return terms


def pack_kernel(info_ref, orb_ref, trial_ref, own_ref, out_ref, tail_ref):
    out_ref[0:64, :] = orb_ref[...].reshape(64, 256)
    rows = [trial_ref[:, s, :].astype(BF) for s in range(2)]
    parts = density_of(own_ref, rows)
    tail_ref[...] = jnp.zeros((16, 256), F32)
    for s in range(2):
        tail_ref[2 * s : 2 * s + 2, :] = rows[s].astype(F32)
    for part in range(4):
        tail_ref[4 + 2 * part : 6 + 2 * part, :] = parts[part]
    kind = lax.rem(lanes(1, 256), 16) // 2
    ids = jnp.zeros((1, 256), jnp.int32)
    for e in range(8):
        ids = jnp.where(kind == e, info_ref[e], ids)
    tail_ref[12:13, :] = ids.astype(F32)
    out_ref[64:80, :] = tail_ref[...].astype(BF)


def select_kernel(plane_ref, gat_ref, out_ref, pick_ref):
    lane = lanes(1, 256)
    pick_ref[...] = jnp.zeros((256, 256), F32)
    for peer in range(8):
        for e in range(6):
            row = plane_ref[peer * 8 + e]
            z = row // 16
            s = lax.rem(row, 2)
            for n in range(2):
                at = peer * 32 + 2 * e + n
                pick_ref[at : at + 1, :] = (lane == z * 16 + 2 * s + n).astype(F32)

            @pl.when(s == 0)
            def _():
                out_ref[peer, 32 * e : 32 * e + 32, :] = gat_ref[z, 0:32, :]

            @pl.when(s == 1)
            def _():
                out_ref[peer, 32 * e : 32 * e + 32, :] = gat_ref[z, 32:64, :]

        for d in range(8):
            at = peer * 32 + 16 + d
            pick_ref[at : at + 1, :] = (lax.rem(lane, 16) == 4 + d).astype(F32)
    tails = gat_ref[:, 64:80, :].reshape(256, 256)
    picked = dot(pick_ref[...].astype(BF), tails).astype(BF)
    out_ref[:, 192:224, :] = picked.reshape(8, 32, 256)


def accept_kernel(info_ref, got_ref, val_ref, cond_ref, dens_ref, tail_ref):
    for e in range(6):
        column = lax.rem(info_ref[e] // 2, 8)
        val_ref[16 * e : 16 * e + 16, :] = got_ref[column, 32 * e : 32 * e + 16, :]
        cond_ref[e] = got_ref[column, 32 * e + 16 : 32 * e + 32, :]
        part = got_ref[column, 192:208, :].astype(F32)
        tail_ref[2 * e : 2 * e + 2, :] = part[2 * e : 2 * e + 2, :]
    tail_ref[12:16, :] = jnp.zeros((4, 256), F32)
    val_ref[96:112, :] = tail_ref[...].astype(BF)
    total = got_ref[0, 208:224, :].astype(F32)
    for peer in range(1, 8):
        total = total + got_ref[peer, 208:224, :].astype(F32)
    dens_ref[...] = total[0:8, :]


def base_kernel(
    info_ref, plane_ref, dens_ref, gat_ref, own_ref, bare_ref, trans_ref, trial_ref,
    base_ref, route_ref, back_ref, base_s, route_s,
):
    dens = [dens_ref[2 * part : 2 * part + 2, :] for part in range(4)]
    terms = bare_of(own_ref, bare_ref, dens)
    for s in range(2):
        x = trial_ref[:, s, :].astype(BF).astype(F32)
        base_s[2 * s : 2 * s + 2, :] = trans_ref[s : s + 1, :] * x + 2.0 * terms[s]
    base_ref[...] = base_s[...]

    lane = lanes(1, 256)
    held = jnp.zeros((1, 256), F32)
    for z in range(16):
        row = gat_ref[z, 64:80, :].astype(F32)[12:13, :]
        held = jnp.where(lane // 16 == z, row, held)
    held = held.astype(jnp.int32)
    sign = jnp.where(lax.rem(lane, 16) < 12, -1.0, 1.0)
    parity = lax.rem(lane, 2)
    z_me = info_ref[8]
    q_me = info_ref[9]
    for peer in range(8):
        for k in range(8):
            row = plane_ref[peer * 8 + k] if k < 6 else z_me * 16 + peer * 2 + (k - 6)
            for n in range(2):
                at = peer * 16 + 2 * k + n
                hit = (held == row) & (parity == n)
                route_s[at : at + 1, :] = jnp.where(hit, sign, 0.0)
    route_ref[...] = route_s[...].astype(BF)

    wide = lanes(1, 512)
    sent = jnp.full((1, 512), -1, jnp.int32)
    for peer in range(8):
        for e in range(6):
            here = (wide // 64 == peer) & (lax.rem(wide, 16) // 2 == e)
            sent = jnp.where(here, plane_ref[peer * 8 + e], sent)
    row = lax.broadcasted_iota(jnp.int32, (64, 512), 0)
    target = (row // 4) * 16 + q_me * 2 + lax.rem(row, 4) // 2
    hit = (sent == target) & (lax.rem(row, 2) == lax.rem(lanes(64, 512), 2))
    back_ref[...] = jnp.where(hit, -1.0, 0.0).astype(BF)


def spread(x):
    rows = jnp.concatenate([x] * 16, axis=0)
    group = lax.broadcasted_iota(jnp.int32, (128, 256), 0) // 8
    return jnp.where(group == lanes(128, 256) // 16, rows, 0.0).astype(BF)


def gathered(full):
    group = lax.broadcasted_iota(jnp.int32, (128, 256), 0) // 8
    kept = jnp.where(group == lanes(128, 256) // 16, full, 0.0)
    total = kept[0:8, :]
    for v in range(1, 16):
        total = total + kept[8 * v : 8 * v + 8, :]
    return total


def apply_pair(i, half_ref, cond_ref, xs_ref, ys_ref, t_ref, u_ref):
    tile_a = jnp.concatenate([cond_ref[2 * i]] * 16, axis=0)
    tile_c = jnp.concatenate([cond_ref[2 * i + 1]] * 16, axis=0)
    t_ref[0] = dot(spread(xs_ref[2 * i]), tile_a)
    t_ref[1] = dot(spread(xs_ref[2 * i + 1]), tile_c)
    u_ref[1] = jnp.zeros((128, 256), F32)

    def over_first(v, carry):
        at = pl.multiple_of(v * 8, 8)
        t_a = t_ref[0, pl.ds(at, 8), :]
        total = jnp.zeros((8, 256), F32)
        for w in range(16):
            h = jnp.broadcast_to(half_ref[i, pl.ds(v * 16 + w, 1), :], (8, 256))
            total = total + h * t_ref[1, 8 * w : 8 * w + 8, :]
            u_ref[1, 8 * w : 8 * w + 8, :] += h * t_a
        u_ref[0, pl.ds(at, 8), :] = total
        return carry

    lax.fori_loop(0, 16, over_first, 0)
    ys_ref[2 * i] = gathered(dot_t(u_ref[0].astype(BF), tile_a))
    ys_ref[2 * i + 1] = gathered(dot_t(u_ref[1].astype(BF), tile_c))


def first_kernel(
    info_ref, wide_ref, cond_ref, scr_ref, base_ref, half_ref, res_ref,
    xs_ref, ys_ref, t_ref, u_ref, rs_ref,
):
    for part in range(4):
        tail = wide_ref[part, 96:112, :].astype(F32)
        for e in range(6):
            xs_ref[e, 2 * part : 2 * part + 2, :] = tail[2 * e : 2 * e + 2, :]

    def one(i, carry):
        slot = info_ref[11 + i]
        total = jnp.zeros((256, 256), F32)
        for part in range(4):
            at = pl.multiple_of(i * 32, 16)
            a = wide_ref[part, pl.ds(at, 16), :].astype(F32)
            b = wide_ref[part, pl.ds(at + 16, 16), :].astype(F32)
            left = jnp.concatenate(
                [(a[v : v + 1, :] * b).astype(BF) for v in range(16)], axis=0
            )
            total = total + dot(left, scr_ref[slot, part * 256 : (part + 1) * 256, :])
        half_ref[i] = total.astype(BF).astype(F32)
        apply_pair(i, half_ref, cond_ref, xs_ref, ys_ref, t_ref, u_ref)
        return carry

    lax.fori_loop(0, 3, one, 0)
    for part in range(4):
        for e in range(6):
            rs_ref[part, 2 * e : 2 * e + 2, :] = ys_ref[e, 2 * part : 2 * part + 2, :]
        mine = (info_ref[10] == part).astype(F32)
        rs_ref[part, 12:16, :] = base_ref[...] * mine
    res_ref[...] = rs_ref[...].astype(BF)


def middle_kernel(route_ref, col_ref, out_ref):
    full = dot(route_ref[...], col_ref[...].reshape(256, 256)).astype(BF)
    for peer in range(8):
        for part in range(4):
            out_ref[4 * peer + part] = full[16 * peer : 16 * peer + 16, :]


def second_kernel(
    info_ref, got_ref, half_ref, cond_ref, own_ref, out_ref, own_x_ref,
    xs_ref, ys_ref, t_ref, u_ref, rs_ref, ds_ref,
):
    for part in range(4):
        total = got_ref[part].astype(F32)
        for peer in range(1, 8):
            total = total + got_ref[4 * peer + part].astype(F32)
        for e in range(6):
            xs_ref[e, 2 * part : 2 * part + 2, :] = total[2 * e : 2 * e + 2, :]
    y_me = info_ref[10]
    total = got_ref[y_me].astype(F32)
    for peer in range(1, 8):
        total = total + got_ref[4 * peer + y_me].astype(F32)
    own_x_ref[...] = total[12:16, :]
    rows = [total[12 + 2 * s : 14 + 2 * s, :].astype(BF) for s in range(2)]
    parts = density_of(own_ref, rows)
    for part in range(4):
        for h in range(2):
            at = 4 * part + 2 * h
            ds_ref[at : at + 2, :] = parts[part][:, 128 * h : 128 * h + 128]

    def one(i, carry):
        apply_pair(i, half_ref, cond_ref, xs_ref, ys_ref, t_ref, u_ref)
        return carry

    lax.fori_loop(0, 3, one, 0)
    rs_ref[...] = jnp.zeros((4, 16, 256), F32)
    for part in range(4):
        for e in range(6):
            rs_ref[part, 2 * e : 2 * e + 2, :] = ys_ref[e, 2 * part : 2 * part + 2, :]
    for peer in range(8):
        for part in range(4):
            out_ref[4 * peer + part, :, 0:256] = rs_ref[part].astype(BF)
            out_ref[4 * peer + part, :, 256:384] = ds_ref[...].astype(BF)


def return_kernel(info_ref, back_ref, got_ref, out_ref, buf_ref):
    full = dot(back_ref[...], got_ref[:, :, 0:256].reshape(512, 256))
    y_me = info_ref[10]
    total = got_ref[y_me, :, 256:384].astype(F32)
    for peer in range(1, 8):
        total = total + got_ref[4 * peer + y_me, :, 256:384].astype(F32)
    buf_ref[...] = jnp.zeros((16, 16, 256), F32)
    for part in range(4):
        for h in range(2):
            at = 4 * part + 2 * h
            buf_ref[0, 4 + 2 * part : 6 + 2 * part, 128 * h : 128 * h + 128] = total[at : at + 2, :]
    for z in range(16):
        if z:
            buf_ref[z, 4:12, :] = buf_ref[0, 4:12, :]
        buf_ref[z, 0:4, :] = full[4 * z : 4 * z + 4, :]
    out_ref[...] = buf_ref[...].astype(BF)


def last_kernel(cheb_ref, got_ref, own_ref, bare_ref, trans_ref, trial_ref, own_x_ref, out_ref):
    total = got_ref[0].astype(F32)
    for z in range(1, 16):
        total = total + got_ref[z].astype(F32)
    dens = [total[4 + 2 * part : 6 + 2 * part, :] for part in range(4)]
    terms = bare_of(own_ref, bare_ref, dens)
    for s in range(2):
        x = own_x_ref[2 * s : 2 * s + 2, :]
        t = trial_ref[:, s, :]
        applied = (
            trans_ref[s : s + 1, :] * x.astype(BF).astype(F32)
            + 2.0 * terms[s]
            + total[2 * s : 2 * s + 2, :]
        )
        second = 2.0 * applied - t
        out_ref[:, s, :] = cheb_ref[0] * t + cheb_ref[1] * x + cheb_ref[2] * second


def body(orbitals, transition, trial, screened, bare, cheb, pair_k, pair_slot, k_order):
    k_total = k_order.shape[0]
    position = lax.axis_index(PB)
    momentum = position * 2 + pair_slot
    partner = jnp.mod(pair_k - momentum, k_total)
    ends = jnp.stack([pair_k, partner], axis=1).reshape(-1)
    rows = jnp.arange(k_total, dtype=jnp.int32)
    dest = jnp.sum(jnp.where(ends[:, None] == k_order[None, :], rows[None, :], 0), axis=1)
    own_rows = position * 2 + jnp.arange(2, dtype=jnp.int32)
    where = jnp.stack([lax.axis_index("z"), lax.axis_index(PLANE), lax.axis_index("y")])
    info = jnp.concatenate([dest, own_rows, where, pair_slot, jnp.zeros((2,), jnp.int32)])

    plane = to_everyone(info[0:8], PLANE).reshape(64)
    own = to_everyone(orbitals, "y")
    (packed,) = call(pack_kernel, [((80, 256), BF)], (0,), [pltpu.VMEM((16, 256), F32)])(
        info, orbitals, trial, own
    )
    gat = lax.all_gather(packed, "z")
    (chosen,) = call(select_kernel, [((8, 224, 256), BF)], (0,), [pltpu.VMEM((256, 256), F32)])(
        plane, gat
    )
    got = exchange(chosen, PLANE)
    val, cond, dens = call(
        accept_kernel,
        [((112, 256), BF), ((6, 16, 256), BF), ((8, 256), F32)],
        (0,),
        [pltpu.VMEM((16, 256), F32)],
    )(info, got)
    wide = to_everyone(val, "y")
    base, route, back = call(
        base_kernel,
        [((4, 256), F32), ((128, 256), BF), ((64, 512), BF)],
        (0, 1),
        [pltpu.VMEM((4, 256), F32), pltpu.VMEM((128, 256), F32)],
    )(info, plane, dens, gat, own, bare, transition, trial)
    work = [
        pltpu.VMEM((6, 8, 256), F32),
        pltpu.VMEM((6, 8, 256), F32),
        pltpu.VMEM((2, 128, 256), F32),
        pltpu.VMEM((2, 128, 256), F32),
        pltpu.VMEM((4, 16, 256), F32),
    ]
    half, res = call(
        first_kernel, [((3, 256, 256), F32), ((4, 16, 256), BF)], (0,), work
    )(info, wide, cond, screened, base)
    parts = exchange(res, "y")
    column = jnp.sum(parts.astype(F32), axis=0).astype(BF)
    columns = to_everyone(column, "z")
    (middle,) = call(middle_kernel, [((32, 16, 256), BF)], ())(route, columns)
    arrived = exchange(middle, BLOCK)
    out2, own_x = call(
        second_kernel,
        [((32, 16, 384), BF), ((4, 256), F32)],
        (0,),
        work + [pltpu.VMEM((16, 128), F32)],
    )(info, arrived, half, cond, own)
    returned = exchange(out2, BLOCK)
    (final,) = call(
        return_kernel, [((16, 16, 256), BF)], (0,), [pltpu.VMEM((16, 16, 256), F32)]
    )(info, back, returned)
    last = exchange(final, "z")
    (result,) = call(last_kernel, [(trial.shape, F32)], (0,))(
        cheb, last, own, bare, transition, trial, own_x
    )
    return result


def solution(mesh):
    split = Mesh(mesh.devices.reshape(16, 4, 2, mesh.shape["vert"]), ("z", "x", "c", "y"))
    in_specs = (
        P(PB, None, "y"),
        P(PB, None),
        P("y", PB, None),
        P(PB, None, "y"),
        P(),
        P(),
        P(PB),
        P(PB),
        P(),
    )
    out_specs = P("y", PB, None)
    return jax.shard_map(body, mesh=split, in_specs=in_specs, out_specs=out_specs, check_vma=False)
```

```python
import functools

import jax
import jax.numpy as jnp
from jax import lax
from jax.experimental import pallas as pl
from jax.experimental.pallas import tpu as pltpu
from jax.sharding import Mesh
from jax.sharding import PartitionSpec as P

BF = jnp.bfloat16
F32 = jnp.float32
NV = 16
LAST = (((1,), (1,)), ((), ()))
PB = ("z", "x", "c")
PLANE = ("x", "c")
BLOCK = ("x", "c", "y")
LIMIT = 12 << 20


def exchange(blocks, axis):
    return lax.all_to_all(blocks, axis, 0, 0, tiled=True)


def dot(a, b):
    return jnp.dot(a, b, preferred_element_type=F32)


def dot_t(a, b):
    return lax.dot_general(a, b, LAST, preferred_element_type=F32)


def call(kernel, outs, smem, scratch=()):
    def run(*args):
        specs = [
            pl.BlockSpec(memory_space=pltpu.SMEM if k in smem else pltpu.VMEM)
            for k in range(len(args))
        ]
        return pl.pallas_call(
            kernel,
            out_shape=[jax.ShapeDtypeStruct(s, d) for s, d in outs],
            in_specs=specs,
            out_specs=[
                pl.BlockSpec(memory_space=pltpu.SMEM if len(s) == 1 else pltpu.VMEM)
                for s, _ in outs
            ],
            scratch_shapes=list(scratch),
            name=kernel.__name__,
            compiler_params=pltpu.CompilerParams(vmem_limit_bytes=LIMIT),
        )(*args)

    return run


def lanes(rows, width):
    return lax.broadcasted_iota(jnp.int32, (rows, width), 1)


def products_of(own_ref, s, part):
    val = own_ref[part, s, 0:16, :].astype(F32)
    cond = own_ref[part, s, 16:32, :].astype(F32)
    pieces = [(val[v : v + 1, :] * cond).astype(BF) for v in range(16)]
    return jnp.concatenate(pieces, axis=0)


def density_of(own_ref, rows_bf):
    parts = []
    for part in range(4):
        total = dot(rows_bf[0], products_of(own_ref, 0, part))
        total = total + dot(rows_bf[1], products_of(own_ref, 1, part))
        parts.append(total)
    return parts


def bare_of(own_ref, bare_ref, dens):
    pots = []
    for out in range(4):
        total = jnp.zeros((2, 256), F32)
        for part in range(4):
            total = total + dot_t(
                dens[part].astype(BF),
                bare_ref[out * 256 : (out + 1) * 256, part * 256 : (part + 1) * 256],
            )
        pots.append(total.astype(BF))
    terms = []
    for s in range(2):
        total = jnp.zeros((2, 256), F32)
        for part in range(4):
            total = total + dot_t(pots[part], products_of(own_ref, s, part))
        terms.append(total)
    return terms


def info_kernel(pair_ref, slot_ref, order_ref, orb_ref, info_ref, ids_ref, own_ref):
    position = lax.axis_index(PB)
    lane = lanes(1, 256)
    short = lanes(1, 128)
    order = order_ref[...]
    ids = jnp.where(short == 6, position * 2, jnp.where(short == 7, position * 2 + 1, 0))
    for i in range(3):
        first = pair_ref[i]
        second = first - position * 2 - slot_ref[i]
        second = jnp.where(second < 0, second + 256, second)
        for h, k in enumerate((first, second)):
            row = jnp.sum(jnp.where(order == k, lane, 0))
            info_ref[2 * i + h] = row
            ids = jnp.where(short == 2 * i + h, row, ids)
        info_ref[11 + i] = slot_ref[i]
    info_ref[6] = position * 2
    info_ref[7] = position * 2 + 1
    info_ref[8] = lax.axis_index("z")
    info_ref[9] = lax.axis_index(PLANE)
    info_ref[10] = lax.axis_index("y")
    info_ref[14] = 0
    info_ref[15] = 0
    for peer in range(8):
        ids_ref[peer] = ids
    for part in range(4):
        own_ref[part] = orb_ref[...]


def pack_kernel(info_ref, orb_ref, trial_ref, own_ref, out_ref, tail_ref):
    out_ref[0:64, :] = orb_ref[...].reshape(64, 256)
    rows = [trial_ref[:, s, :].astype(BF) for s in range(2)]
    parts = density_of(own_ref, rows)
    tail_ref[...] = jnp.zeros((16, 256), F32)
    for s in range(2):
        tail_ref[2 * s : 2 * s + 2, :] = rows[s].astype(F32)
    for part in range(4):
        tail_ref[4 + 2 * part : 6 + 2 * part, :] = parts[part]
    kind = lax.rem(lanes(1, 256), 16) // 2
    ids = jnp.zeros((1, 256), jnp.int32)
    for e in range(8):
        ids = jnp.where(kind == e, info_ref[e], ids)
    tail_ref[12:13, :] = ids.astype(F32)
    out_ref[64:80, :] = tail_ref[...].astype(BF)


def select_kernel(plane_ref, gat_ref, out_ref, pick_ref):
    lane = lanes(1, 256)
    pick_ref[...] = jnp.zeros((256, 256), F32)
    for peer in range(8):
        for e in range(6):
            row = plane_ref[peer, 0, e]
            z = row // 16
            s = lax.rem(row, 2)
            for n in range(2):
                at = peer * 32 + 2 * e + n
                pick_ref[at : at + 1, :] = (lane == z * 16 + 2 * s + n).astype(F32)
            at = pl.multiple_of(s * 32, 32)
            out_ref[peer, 32 * e : 32 * e + 32, :] = gat_ref[z, pl.ds(at, 32), :]

        for d in range(8):
            at = peer * 32 + 16 + d
            pick_ref[at : at + 1, :] = (lax.rem(lane, 16) == 4 + d).astype(F32)
    tails = gat_ref[:, 64:80, :].reshape(256, 256)
    picked = dot(pick_ref[...].astype(BF), tails).astype(BF)
    out_ref[:, 192:224, :] = picked.reshape(8, 32, 256)


def accept_kernel(info_ref, got_ref, val_ref, cond_ref, dens_ref, tail_ref):
    for e in range(6):
        column = lax.rem(info_ref[e] // 2, 8)
        val = got_ref[column, 32 * e : 32 * e + 16, :]
        for part in range(4):
            val_ref[part, 16 * e : 16 * e + 16, :] = val
        cond_ref[e] = got_ref[column, 32 * e + 16 : 32 * e + 32, :]
        part = got_ref[column, 192:208, :].astype(F32)
        tail_ref[2 * e : 2 * e + 2, :] = part[2 * e : 2 * e + 2, :]
    tail_ref[12:16, :] = jnp.zeros((4, 256), F32)
    for part in range(4):
        val_ref[part, 96:112, :] = tail_ref[...].astype(BF)
    total = got_ref[0, 208:224, :].astype(F32)
    for peer in range(1, 8):
        total = total + got_ref[peer, 208:224, :].astype(F32)
    dens_ref[...] = total[0:8, :]


def base_kernel(
    info_ref, plane_ref, dens_ref, gat_ref, own_ref, bare_ref, trans_ref, trial_ref,
    base_ref, route_ref, back_ref, base_s, route_s,
):
    dens = [dens_ref[2 * part : 2 * part + 2, :] for part in range(4)]
    terms = bare_of(own_ref, bare_ref, dens)
    for s in range(2):
        x = trial_ref[:, s, :].astype(BF).astype(F32)
        base_s[2 * s : 2 * s + 2, :] = trans_ref[s : s + 1, :] * x + 2.0 * terms[s]
    base_ref[...] = base_s[...]

    lane = lanes(1, 256)
    held = jnp.zeros((1, 256), F32)
    for z in range(16):
        row = gat_ref[z, 64:80, :].astype(F32)[12:13, :]
        held = jnp.where(lane // 16 == z, row, held)
    held = held.astype(jnp.int32)
    sign = jnp.where(lax.rem(lane, 16) < 12, -1.0, 1.0)
    parity = lax.rem(lane, 2)
    z_me = info_ref[8]
    q_me = info_ref[9]
    for peer in range(8):
        for k in range(8):
            row = plane_ref[peer, 0, k] if k < 6 else z_me * 16 + peer * 2 + (k - 6)
            for n in range(2):
                at = peer * 16 + 2 * k + n
                hit = (held == row) & (parity == n)
                route_s[at : at + 1, :] = jnp.where(hit, sign, 0.0)
    route_ref[...] = route_s[...].astype(BF)

    wide = lanes(1, 512)
    sent = jnp.full((1, 512), -1, jnp.int32)
    for peer in range(8):
        for e in range(6):
            here = (wide // 64 == peer) & (lax.rem(wide, 16) // 2 == e)
            sent = jnp.where(here, plane_ref[peer, 0, e], sent)
    row = lax.broadcasted_iota(jnp.int32, (64, 512), 0)
    target = (row // 4) * 16 + q_me * 2 + lax.rem(row, 4) // 2
    hit = (sent == target) & (lax.rem(row, 2) == lax.rem(lanes(64, 512), 2))
    back_ref[...] = jnp.where(hit, -1.0, 0.0).astype(BF)


def spread(x):
    rows = jnp.concatenate([x] * 16, axis=0)
    group = lax.broadcasted_iota(jnp.int32, (128, 256), 0) // 8
    return jnp.where(group == lanes(128, 256) // 16, rows, 0.0).astype(BF)


def gathered(full):
    group = lax.broadcasted_iota(jnp.int32, (128, 256), 0) // 8
    kept = jnp.where(group == lanes(128, 256) // 16, full, 0.0)
    total = kept[0:8, :]
    for v in range(1, 16):
        total = total + kept[8 * v : 8 * v + 8, :]
    return total


def apply_pair(i, half_ref, cond_ref, xs_ref, ys_ref, t_ref, u_ref):
    tile_a = jnp.concatenate([cond_ref[2 * i]] * 16, axis=0)
    tile_c = jnp.concatenate([cond_ref[2 * i + 1]] * 16, axis=0)
    t_ref[0] = dot(spread(xs_ref[2 * i]), tile_a)
    t_ref[1] = dot(spread(xs_ref[2 * i + 1]), tile_c)
    for part in range(2):
        at = slice(128 * part, 128 * part + 128)
        t_c = [t_ref[1, 8 * w : 8 * w + 8, at] for w in range(16)]

        def over_first(v, u_c):
            row = pl.multiple_of(v * 8, 8)
            t_a = t_ref[0, pl.ds(row, 8), at]
            sums = [jnp.zeros((8, 128), F32)] * 2
            new = []
            for w in range(16):
                h = jnp.broadcast_to(half_ref[2 * i + part, pl.ds(v * 16 + w, 1), :], (8, 128))
                sums[w % 2] = sums[w % 2] + h * t_c[w]
                new.append(u_c[w] + h * t_a)
            u_ref[0, pl.ds(row, 8), at] = sums[0] + sums[1]
            return tuple(new)

        u_c = lax.fori_loop(0, 16, over_first, (jnp.zeros((8, 128), F32),) * 16)
        for w in range(16):
            u_ref[1, 8 * w : 8 * w + 8, at] = u_c[w]
    ys_ref[2 * i] = gathered(dot_t(u_ref[0].astype(BF), tile_a))
    ys_ref[2 * i + 1] = gathered(dot_t(u_ref[1].astype(BF), tile_c))


def first_kernel(
    info_ref, wide_ref, cond_ref, scr_ref, base_ref, half_ref, res_ref,
    xs_ref, ys_ref, t_ref, u_ref, rs_ref,
):
    for part in range(4):
        tail = wide_ref[part, 96:112, :].astype(F32)
        for e in range(6):
            xs_ref[e, 2 * part : 2 * part + 2, :] = tail[2 * e : 2 * e + 2, :]

    def one(i, carry):
        slot = info_ref[11 + i]
        total = jnp.zeros((256, 256), F32)
        for part in range(4):
            at = pl.multiple_of(i * 32, 16)
            a = wide_ref[part, pl.ds(at, 16), :].astype(F32)
            b = wide_ref[part, pl.ds(at + 16, 16), :].astype(F32)
            left = jnp.concatenate(
                [(a[v : v + 1, :] * b).astype(BF) for v in range(16)], axis=0
            )
            total = total + dot(left, scr_ref[slot, part * 256 : (part + 1) * 256, :])
        total = total.astype(BF).astype(F32)
        half_ref[2 * i] = total[:, 0:128]
        half_ref[2 * i + 1] = total[:, 128:256]
        apply_pair(i, half_ref, cond_ref, xs_ref, ys_ref, t_ref, u_ref)
        return carry

    lax.fori_loop(0, 3, one, 0)
    for part in range(4):
        for e in range(6):
            rs_ref[part, 2 * e : 2 * e + 2, :] = ys_ref[e, 2 * part : 2 * part + 2, :]
        mine = (info_ref[10] == part).astype(F32)
        rs_ref[part, 12:16, :] = base_ref[...] * mine
    res_ref[...] = rs_ref[...].astype(BF)


def column_kernel(got_ref, out_ref):
    total = got_ref[0].astype(F32)
    for part in range(1, 4):
        total = total + got_ref[part].astype(F32)
    for z in range(16):
        out_ref[z] = total.astype(BF)


def middle_kernel(route_ref, col_ref, out_ref):
    full = dot(route_ref[...], col_ref[...].reshape(256, 256)).astype(BF)
    for peer in range(8):
        for part in range(4):
            out_ref[4 * peer + part] = full[16 * peer : 16 * peer + 16, :]


def second_kernel(
    info_ref, got_ref, half_ref, cond_ref, own_ref, out_ref, own_x_ref,
    xs_ref, ys_ref, t_ref, u_ref, rs_ref, ds_ref,
):
    for part in range(4):
        total = got_ref[part].astype(F32)
        for peer in range(1, 8):
            total = total + got_ref[4 * peer + part].astype(F32)
        for e in range(6):
            xs_ref[e, 2 * part : 2 * part + 2, :] = total[2 * e : 2 * e + 2, :]
    y_me = info_ref[10]
    total = got_ref[y_me].astype(F32)
    for peer in range(1, 8):
        total = total + got_ref[4 * peer + y_me].astype(F32)
    own_x_ref[...] = total[12:16, :]
    rows = [total[12 + 2 * s : 14 + 2 * s, :].astype(BF) for s in range(2)]
    parts = density_of(own_ref, rows)
    for part in range(4):
        for h in range(2):
            at = 4 * part + 2 * h
            ds_ref[at : at + 2, :] = parts[part][:, 128 * h : 128 * h + 128]

    def one(i, carry):
        apply_pair(i, half_ref, cond_ref, xs_ref, ys_ref, t_ref, u_ref)
        return carry

    lax.fori_loop(0, 3, one, 0)
    rs_ref[...] = jnp.zeros((4, 16, 256), F32)
    for part in range(4):
        for e in range(6):
            rs_ref[part, 2 * e : 2 * e + 2, :] = ys_ref[e, 2 * part : 2 * part + 2, :]
    for peer in range(8):
        for part in range(4):
            out_ref[4 * peer + part, :, 0:256] = rs_ref[part].astype(BF)
            out_ref[4 * peer + part, :, 256:384] = ds_ref[...].astype(BF)


def return_kernel(info_ref, back_ref, got_ref, out_ref, buf_ref):
    full = dot(back_ref[...], got_ref[:, :, 0:256].reshape(512, 256))
    y_me = info_ref[10]
    total = got_ref[y_me, :, 256:384].astype(F32)
    for peer in range(1, 8):
        total = total + got_ref[4 * peer + y_me, :, 256:384].astype(F32)
    buf_ref[...] = jnp.zeros((16, 16, 256), F32)
    for part in range(4):
        for h in range(2):
            at = 4 * part + 2 * h
            buf_ref[0, 4 + 2 * part : 6 + 2 * part, 128 * h : 128 * h + 128] = total[at : at + 2, :]
    for z in range(16):
        if z:
            buf_ref[z, 4:12, :] = buf_ref[0, 4:12, :]
        buf_ref[z, 0:4, :] = full[4 * z : 4 * z + 4, :]
    out_ref[...] = buf_ref[...].astype(BF)


def last_kernel(cheb_ref, got_ref, own_ref, bare_ref, trans_ref, trial_ref, own_x_ref, out_ref):
    total = got_ref[0].astype(F32)
    for z in range(1, 16):
        total = total + got_ref[z].astype(F32)
    dens = [total[4 + 2 * part : 6 + 2 * part, :] for part in range(4)]
    terms = bare_of(own_ref, bare_ref, dens)
    for s in range(2):
        x = own_x_ref[2 * s : 2 * s + 2, :]
        t = trial_ref[:, s, :]
        applied = (
            trans_ref[s : s + 1, :] * x.astype(BF).astype(F32)
            + 2.0 * terms[s]
            + total[2 * s : 2 * s + 2, :]
        )
        second = 2.0 * applied - t
        out_ref[:, s, :] = cheb_ref[0] * t + cheb_ref[1] * x + cheb_ref[2] * second


def body(orbitals, transition, trial, screened, bare, cheb, pair_k, pair_slot, k_order):
    info, ids, copies = call(
        info_kernel,
        [((16,), jnp.int32), ((8, 1, 128), jnp.int32), ((4, 2, 32, 256), BF)],
        (0, 1),
    )(pair_k, pair_slot, k_order.reshape(1, -1), orbitals)
    own = exchange(copies, "y")
    plane = exchange(ids, PLANE)
    (packed,) = call(pack_kernel, [((80, 256), BF)], (0,), [pltpu.VMEM((16, 256), F32)])(
        info, orbitals, trial, own
    )
    gat = lax.all_gather(packed, "z")
    (chosen,) = call(select_kernel, [((8, 224, 256), BF)], (0,), [pltpu.VMEM((256, 256), F32)])(
        plane, gat
    )
    got = exchange(chosen, PLANE)
    val, cond, dens = call(
        accept_kernel,
        [((4, 112, 256), BF), ((6, 16, 256), BF), ((8, 256), F32)],
        (0,),
        [pltpu.VMEM((16, 256), F32)],
    )(info, got)
    wide = exchange(val, "y")
    base, route, back = call(
        base_kernel,
        [((4, 256), F32), ((128, 256), BF), ((64, 512), BF)],
        (0, 1),
        [pltpu.VMEM((4, 256), F32), pltpu.VMEM((128, 256), F32)],
    )(info, plane, dens, gat, own, bare, transition, trial)
    work = [
        pltpu.VMEM((6, 8, 256), F32),
        pltpu.VMEM((6, 8, 256), F32),
        pltpu.VMEM((2, 128, 256), F32),
        pltpu.VMEM((2, 128, 256), F32),
        pltpu.VMEM((4, 16, 256), F32),
    ]
    half, res = call(
        first_kernel, [((6, 256, 128), F32), ((4, 16, 256), BF)], (0,), work
    )(info, wide, cond, screened, base)
    parts = exchange(res, "y")
    (column,) = call(column_kernel, [((16, 16, 256), BF)], ())(parts)
    columns = exchange(column, "z")
    (middle,) = call(middle_kernel, [((32, 16, 256), BF)], ())(route, columns)
    arrived = exchange(middle, BLOCK)
    out2, own_x = call(
        second_kernel,
        [((32, 16, 384), BF), ((4, 256), F32)],
        (0,),
        work + [pltpu.VMEM((16, 128), F32)],
    )(info, arrived, half, cond, own)
    returned = exchange(out2, BLOCK)
    (final,) = call(
        return_kernel, [((16, 16, 256), BF)], (0,), [pltpu.VMEM((16, 16, 256), F32)]
    )(info, back, returned)
    last = exchange(final, "z")
    (result,) = call(last_kernel, [(trial.shape, F32)], (0,))(
        cheb, last, own, bare, transition, trial, own_x
    )
    return result


def solution(mesh):
    split = Mesh(mesh.devices.reshape(16, 4, 2, mesh.shape["vert"]), ("z", "x", "c", "y"))
    in_specs = (
        P(PB, None, "y"),
        P(PB, None),
        P("y", PB, None),
        P(PB, None, "y"),
        P(),
        P(),
        P(PB),
        P(PB),
        P(),
    )
    out_specs = P("y", PB, None)
    return jax.shard_map(body, mesh=split, in_specs=in_specs, out_specs=out_specs, check_vma=False)
```

```python
import jax
import jax.numpy as jnp
from jax import lax
from jax.experimental import pallas as pl
from jax.experimental.pallas import tpu as pltpu
from jax.sharding import Mesh
from jax.sharding import PartitionSpec as P


BF = jnp.bfloat16
F32 = jnp.float32
LAST = (((1,), (1,)), ((), ()))
PB = ("z", "x", "c")
PLANE = ("x", "c")
BLOCK = ("x", "c", "y")
SHEET = ("x", "y")
LIMIT = 12 << 20


def exchange(blocks, axis):
    return lax.all_to_all(blocks, axis, 0, 0, tiled=True)


def swap(shard):
    return lax.ppermute(shard, "c", [(0, 1), (1, 0)])


def dot(a, b):
    return jnp.dot(a, b, preferred_element_type=F32)


def dot_t(a, b):
    return lax.dot_general(a, b, LAST, preferred_element_type=F32)


def call(kernel, outs, smem, scratch=(), far=(), limit=LIMIT):
    def space(k):
        return pltpu.SMEM if k in smem else pltpu.HBM if k in far else pltpu.VMEM

    def run(*args):
        specs = [pl.BlockSpec(memory_space=space(k)) for k in range(len(args))]
        return pl.pallas_call(
            kernel,
            out_shape=[jax.ShapeDtypeStruct(s, d) for s, d in outs],
            in_specs=specs,
            out_specs=[
                pl.BlockSpec(memory_space=pltpu.SMEM if len(s) == 1 else pltpu.VMEM)
                for s, _ in outs
            ],
            scratch_shapes=list(scratch),
            compiler_params=pltpu.CompilerParams(vmem_limit_bytes=limit),
            cost_estimate=pl.CostEstimate(flops=0, transcendentals=0, bytes_accessed=4 << 20),
        )(*args)

    return run


def lanes(rows, width):
    return lax.broadcasted_iota(jnp.int32, (rows, width), 1)


def products_of(own_ref, s, part):
    val = own_ref[part, s, 0:16, :].astype(F32)
    cond = own_ref[part, s, 16:32, :].astype(F32)
    pieces = [(val[v : v + 1, :] * cond).astype(BF) for v in range(16)]
    return jnp.concatenate(pieces, axis=0)


def density_of(own_ref, rows_bf):
    parts = []
    for part in range(4):
        total = dot(rows_bf[0], products_of(own_ref, 0, part))
        total = total + dot(rows_bf[1], products_of(own_ref, 1, part))
        parts.append(total)
    return parts


def bare_of(own_ref, bare_ref, dens):
    pots = []
    for out in range(4):
        total = jnp.zeros((2, 256), F32)
        for part in range(4):
            total = total + dot_t(
                dens[part].astype(BF),
                bare_ref[out * 256 : (out + 1) * 256, part * 256 : (part + 1) * 256],
            )
        pots.append(total.astype(BF))
    terms = []
    for s in range(2):
        total = jnp.zeros((2, 256), F32)
        for part in range(4):
            total = total + dot_t(pots[part], products_of(own_ref, s, part))
        terms.append(total)
    return terms


def info_kernel(
    pair_hbm, slot_hbm, order_hbm, orb_hbm, trial_hbm, trans_hbm,
    info_ref, ids_ref, own_ref, held_ref, pair_ref, slot_ref, order_ref, trial_ref, trans_ref, sem,
):
    moves = [
        (pair_hbm, pair_ref), (slot_hbm, slot_ref), (order_hbm, order_ref),
        (trial_hbm, trial_ref), (trans_hbm, trans_ref),
    ] + [(orb_hbm, own_ref.at[part]) for part in range(4)]
    copies = [pltpu.make_async_copy(a, b, sem.at[k]) for k, (a, b) in enumerate(moves)]
    for copy in copies:
        copy.start()
    for copy in copies[:3]:
        copy.wait()
    position = lax.axis_index(PB)
    lane = lanes(1, 256)
    short = lanes(1, 128)
    order = order_ref[...]
    ids = jnp.where(short == 6, position * 2, jnp.where(short == 7, position * 2 + 1, 0))
    for i in range(3):
        first = pair_ref[i]
        second = first - position * 2 - slot_ref[i]
        second = jnp.where(second < 0, second + 256, second)
        for h, k in enumerate((first, second)):
            row = jnp.sum(jnp.where(order == k, lane, 0))
            info_ref[2 * i + h] = row
            ids = jnp.where(short == 2 * i + h, row, ids)
        info_ref[11 + i] = slot_ref[i]
    info_ref[6] = position * 2
    info_ref[7] = position * 2 + 1
    info_ref[8] = lax.axis_index("z")
    info_ref[9] = lax.axis_index(PLANE)
    info_ref[10] = lax.axis_index("y")
    info_ref[14] = 0
    info_ref[15] = 0
    for peer in range(8):
        ids_ref[peer] = ids
    for copy in copies[3:]:
        copy.wait()
    held_ref[...] = jnp.zeros((8, 256), F32)
    for s in range(2):
        held_ref[2 * s : 2 * s + 2, :] = trial_ref[:, s, :]
    held_ref[4:6, :] = trans_ref[...]


def pack_kernel(info_ref, held_ref, own_ref, out_ref, tail_ref):
    out_ref[0:64, :] = own_ref[info_ref[10]].reshape(64, 256)
    rows = [held_ref[2 * s : 2 * s + 2, :].astype(BF) for s in range(2)]
    parts = density_of(own_ref, rows)
    tail_ref[...] = jnp.zeros((16, 256), F32)
    for s in range(2):
        tail_ref[2 * s : 2 * s + 2, :] = rows[s].astype(F32)
    for part in range(4):
        tail_ref[4 + 2 * part : 6 + 2 * part, :] = parts[part]
    kind = lax.rem(lanes(1, 256), 16) // 2
    ids = jnp.zeros((1, 256), jnp.int32)
    for e in range(8):
        ids = jnp.where(kind == e, info_ref[e], ids)
    tail_ref[12:13, :] = ids.astype(F32)
    out_ref[64:80, :] = tail_ref[...].astype(BF)


def select_kernel(info_ref, plane_ref, gat_ref, twin_ref, out_ref, pick_ref):
    lane = lanes(1, 512)
    core = lax.rem(info_ref[9], 2)
    pick_ref[...] = jnp.zeros((128, 512), F32)
    for peer in range(4):
        for e in range(6):
            row = plane_ref[2 * peer + core, 0, e]
            z = row // 16
            s = lax.rem(row, 2)
            ours = lax.rem(row // 2, 2) == core
            first = z * 16 + 2 * s + jnp.where(ours, 0, 256)
            for n in range(2):
                at = peer * 32 + 2 * e + n
                pick_ref[at : at + 1, :] = (lane == first + n).astype(F32)
            at = pl.multiple_of(s * 32, 32)

            @pl.when(ours)
            def _():
                out_ref[peer, 32 * e : 32 * e + 32, :] = gat_ref[z, pl.ds(at, 32), :]

            @pl.when(jnp.logical_not(ours))
            def _():
                out_ref[peer, 32 * e : 32 * e + 32, :] = twin_ref[z, pl.ds(at, 32), :]

        for d in range(8):
            at = peer * 32 + 16 + d
            pick_ref[at : at + 1, :] = (lax.rem(lane, 16) == 4 + d).astype(F32)
    pick = pick_ref[...].astype(BF)
    picked = dot(pick[:, 0:256], gat_ref[:, 64:80, :].reshape(256, 256))
    picked = picked + dot(pick[:, 256:512], twin_ref[:, 64:80, :].reshape(256, 256))
    out_ref[:, 192:224, :] = picked.astype(BF).reshape(4, 32, 256)


def accept_kernel(info_ref, got_ref, val_ref, cond_ref, dens_ref, tail_ref):
    for e in range(6):
        column = lax.rem(info_ref[e] // 4, 4)
        val = got_ref[column, 32 * e : 32 * e + 16, :]
        for part in range(4):
            val_ref[part, 16 * e : 16 * e + 16, :] = val
        cond_ref[e] = got_ref[column, 32 * e + 16 : 32 * e + 32, :]
        part = got_ref[column, 192:208, :].astype(F32)
        tail_ref[2 * e : 2 * e + 2, :] = part[2 * e : 2 * e + 2, :]
    tail_ref[12:16, :] = jnp.zeros((4, 256), F32)
    for part in range(4):
        val_ref[part, 96:112, :] = tail_ref[...].astype(BF)
    total = got_ref[0, 208:224, :].astype(F32)
    for peer in range(1, 4):
        total = total + got_ref[peer, 208:224, :].astype(F32)
    dens_ref[...] = total[0:8, :]


def base_kernel(
    info_ref, plane_ref, dens_ref, gat_ref, own_ref, bare_ref, held_ref,
    base_ref, route_ref, back_ref, base_s, route_s,
):
    dens = [dens_ref[2 * part : 2 * part + 2, :] for part in range(4)]
    terms = bare_of(own_ref, bare_ref, dens)
    for s in range(2):
        x = held_ref[2 * s : 2 * s + 2, :].astype(BF).astype(F32)
        base_s[2 * s : 2 * s + 2, :] = held_ref[4 + s : 5 + s, :] * x + 2.0 * terms[s]
    base_ref[...] = base_s[...]

    lane = lanes(1, 256)
    held = jnp.zeros((1, 256), F32)
    for z in range(16):
        row = gat_ref[z, 64:80, :].astype(F32)[12:13, :]
        held = jnp.where(lane // 16 == z, row, held)
    held = held.astype(jnp.int32)
    sign = jnp.where(lax.rem(lane, 16) < 12, -1.0, 1.0)
    parity = lax.rem(lane, 2)
    z_me = info_ref[8]
    q_me = info_ref[9]
    for peer in range(8):
        for k in range(8):
            row = plane_ref[peer, 0, k] if k < 6 else z_me * 16 + peer * 2 + (k - 6)
            for n in range(2):
                at = peer * 16 + 2 * k + n
                hit = (held == row) & (parity == n)
                route_s[at : at + 1, :] = jnp.where(hit, sign, 0.0)
    route_ref[...] = route_s[...].astype(BF)

    sent = jnp.full((1, 256), -1, jnp.int32)
    core = lax.rem(q_me, 2)
    for peer in range(4):
        for e in range(6):
            here = (lane // 64 == peer) & (lax.rem(lane, 16) // 2 == e)
            sent = jnp.where(here, plane_ref[2 * peer + core, 0, e], sent)
    row = lax.broadcasted_iota(jnp.int32, (128, 256), 0)
    target = (row // 8) * 16 + (q_me // 2) * 4 + lax.rem(row, 8) // 2
    hit = (sent == target) & (lax.rem(row, 2) == lax.rem(lanes(128, 256), 2))
    back_ref[...] = jnp.where(hit, -1.0, 0.0).astype(BF)


def spread(x):
    rows = jnp.concatenate([x] * 16, axis=0)
    group = lax.broadcasted_iota(jnp.int32, (128, 256), 0) // 8
    return jnp.where(group == lanes(128, 256) // 16, rows, 0.0).astype(BF)


def gathered(full):
    group = lax.broadcasted_iota(jnp.int32, (128, 256), 0) // 8
    kept = jnp.where(group == lanes(128, 256) // 16, full, 0.0)
    total = kept[0:8, :]
    for v in range(1, 16):
        total = total + kept[8 * v : 8 * v + 8, :]
    return total


def apply_pair(i, half_ref, cond_ref, xs_ref, ys_ref, t_ref, u_ref):
    tile_a = jnp.concatenate([cond_ref[2 * i]] * 16, axis=0)
    tile_c = jnp.concatenate([cond_ref[2 * i + 1]] * 16, axis=0)
    t_ref[0] = dot(spread(xs_ref[2 * i]), tile_a)
    t_ref[1] = dot(spread(xs_ref[2 * i + 1]), tile_c)
    for part in range(2):
        at = slice(128 * part, 128 * part + 128)
        t_c = [t_ref[1, 8 * w : 8 * w + 8, at] for w in range(16)]

        def over_first(v, u_c):
            row = pl.multiple_of(v * 8, 8)
            t_a = t_ref[0, pl.ds(row, 8), at]
            sums = [jnp.zeros((8, 128), F32)] * 2
            new = []
            for w in range(16):
                h = jnp.broadcast_to(half_ref[2 * i + part, pl.ds(v * 16 + w, 1), :], (8, 128))
                sums[w % 2] = sums[w % 2] + h * t_c[w]
                new.append(u_c[w] + h * t_a)
            u_ref[0, pl.ds(row, 8), at] = sums[0] + sums[1]
            return tuple(new)

        u_c = lax.fori_loop(0, 16, over_first, (jnp.zeros((8, 128), F32),) * 16)
        for w in range(16):
            u_ref[1, 8 * w : 8 * w + 8, at] = u_c[w]
    ys_ref[2 * i] = gathered(dot_t(u_ref[0].astype(BF), tile_a))
    ys_ref[2 * i + 1] = gathered(dot_t(u_ref[1].astype(BF), tile_c))


def first_kernel(
    info_ref, wide_ref, cond_ref, scr_ref, base_ref, half_ref, res_ref,
    xs_ref, ys_ref, t_ref, u_ref, rs_ref,
):
    for part in range(4):
        tail = wide_ref[part, 96:112, :].astype(F32)
        for e in range(6):
            xs_ref[e, 2 * part : 2 * part + 2, :] = tail[2 * e : 2 * e + 2, :]

    def one(i, carry):
        slot = info_ref[11 + i]
        total = jnp.zeros((256, 256), F32)
        for part in range(4):
            at = pl.multiple_of(i * 32, 16)
            a = wide_ref[part, pl.ds(at, 16), :].astype(F32)
            b = wide_ref[part, pl.ds(at + 16, 16), :].astype(F32)
            left = jnp.concatenate(
                [(a[v : v + 1, :] * b).astype(BF) for v in range(16)], axis=0
            )
            total = total + dot(left, scr_ref[slot, part * 256 : (part + 1) * 256, :])
        total = total.astype(BF).astype(F32)
        half_ref[2 * i] = total[:, 0:128]
        half_ref[2 * i + 1] = total[:, 128:256]
        apply_pair(i, half_ref, cond_ref, xs_ref, ys_ref, t_ref, u_ref)
        return carry

    lax.fori_loop(0, 3, one, 0)
    for part in range(4):
        for e in range(6):
            rs_ref[part, 2 * e : 2 * e + 2, :] = ys_ref[e, 2 * part : 2 * part + 2, :]
        mine = (info_ref[10] == part).astype(F32)
        rs_ref[part, 12:16, :] = base_ref[...] * mine
    res_ref[...] = rs_ref[...].astype(BF)


def column_kernel(got_ref, out_ref):
    total = got_ref[0].astype(F32)
    for part in range(1, 4):
        total = total + got_ref[part].astype(F32)
    for z in range(16):
        out_ref[z] = total.astype(BF)


def middle_kernel(route_ref, col_ref, out_ref):
    full = dot(route_ref[...], col_ref[...].reshape(256, 256)).astype(BF)
    for peer in range(8):
        for part in range(4):
            out_ref[4 * peer + part] = full[16 * peer : 16 * peer + 16, :]


def second_kernel(
    info_ref, got_ref, half_ref, cond_ref, own_ref, out_ref, own_x_ref,
    xs_ref, ys_ref, t_ref, u_ref, rs_ref, ds_ref,
):
    for part in range(4):
        total = got_ref[part].astype(F32)
        for peer in range(1, 8):
            total = total + got_ref[4 * peer + part].astype(F32)
        for e in range(6):
            xs_ref[e, 2 * part : 2 * part + 2, :] = total[2 * e : 2 * e + 2, :]
    y_me = info_ref[10]
    total = got_ref[y_me].astype(F32)
    for peer in range(1, 8):
        total = total + got_ref[4 * peer + y_me].astype(F32)
    own_x_ref[...] = total[12:16, :]
    rows = [total[12 + 2 * s : 14 + 2 * s, :].astype(BF) for s in range(2)]
    parts = density_of(own_ref, rows)
    for part in range(4):
        for h in range(2):
            at = 4 * part + 2 * h
            ds_ref[at : at + 2, :] = parts[part][:, 128 * h : 128 * h + 128]

    def one(i, carry):
        apply_pair(i, half_ref, cond_ref, xs_ref, ys_ref, t_ref, u_ref)
        return carry

    lax.fori_loop(0, 3, one, 0)
    rs_ref[...] = jnp.zeros((4, 16, 256), F32)
    for part in range(4):
        for e in range(6):
            rs_ref[part, 2 * e : 2 * e + 2, :] = ys_ref[e, 2 * part : 2 * part + 2, :]
    for peer in range(4):
        for part in range(4):
            out_ref[4 * peer + part, :, 0:256] = rs_ref[part].astype(BF)
            out_ref[4 * peer + part, :, 256:384] = ds_ref[...].astype(BF)


def return_kernel(info_ref, back_ref, got_ref, out_ref, buf_ref):
    full = dot(back_ref[...], got_ref[:, :, 0:256].reshape(256, 256))
    y_me = info_ref[10]
    total = got_ref[y_me, :, 256:384].astype(F32)
    for peer in range(1, 4):
        total = total + got_ref[4 * peer + y_me, :, 256:384].astype(F32)
    for part in range(4):
        for h in range(2):
            at = 4 * part + 2 * h
            buf_ref[2 * part : 2 * part + 2, 128 * h : 128 * h + 128] = total[at : at + 2, :]
    for z in range(16):
        rows = jnp.concatenate([full[8 * z : 8 * z + 8, :], buf_ref[...]], axis=0)
        out_ref[z] = rows.astype(BF)


def cross_kernel(info_ref, got_ref, keep_ref, send_ref, buf_ref):
    total = got_ref[0].astype(F32)
    for z in range(1, 16):
        total = total + got_ref[z].astype(F32)
    mine = lax.rem(info_ref[9], 2) == 0
    buf_ref[0:4, :] = jnp.where(mine, total[0:4, :], total[4:8, :])
    buf_ref[4:12, :] = total[8:16, :]
    buf_ref[12:16, :] = jnp.zeros((4, 256), F32)
    keep_ref[...] = buf_ref[...]
    buf_ref[0:4, :] = jnp.where(mine, total[4:8, :], total[0:4, :])
    send_ref[...] = buf_ref[...].astype(BF)


def last_kernel(cheb_ref, keep_ref, got_ref, own_ref, bare_ref, held_ref, own_x_ref, out_ref):
    total = keep_ref[...] + got_ref[...].astype(F32)
    dens = [total[4 + 2 * part : 6 + 2 * part, :] for part in range(4)]
    terms = bare_of(own_ref, bare_ref, dens)
    for s in range(2):
        x = own_x_ref[2 * s : 2 * s + 2, :]
        t = held_ref[2 * s : 2 * s + 2, :]
        applied = (
            held_ref[4 + s : 5 + s, :] * x.astype(BF).astype(F32)
            + 2.0 * terms[s]
            + total[2 * s : 2 * s + 2, :]
        )
        second = 2.0 * applied - t
        out_ref[:, s, :] = cheb_ref[0] * t + cheb_ref[1] * x + cheb_ref[2] * second


def body(orbitals, transition, trial, screened, bare, cheb, pair_k, pair_slot, k_order):
    info, ids, copies, held = call(
        info_kernel,
        [
            ((16,), jnp.int32), ((8, 1, 128), jnp.int32), ((4, 2, 32, 256), BF), ((8, 256), F32),
        ],
        (),
        [
            pltpu.SMEM((3,), jnp.int32),
            pltpu.SMEM((3,), jnp.int32),
            pltpu.VMEM((1, 256), jnp.int32),
            pltpu.VMEM((2, 2, 256), F32),
            pltpu.VMEM((2, 256), F32),
            pltpu.SemaphoreType.DMA((9,)),
        ],
        range(6),
        66600000,
    )(pair_k, pair_slot, k_order.reshape(1, -1), orbitals, trial, transition)
    own = exchange(copies, "y")
    plane = exchange(ids, PLANE)
    (packed,) = call(pack_kernel, [((80, 256), BF)], (0,), [pltpu.VMEM((16, 256), F32)])(
        info, held, own
    )
    gat = lax.all_gather(packed, "z")
    twin = swap(gat)
    (chosen,) = call(select_kernel, [((4, 224, 256), BF)], (0, 1), [pltpu.VMEM((128, 512), F32)])(
        info, plane, gat, twin
    )
    got = exchange(chosen, "x")
    val, cond, dens = call(
        accept_kernel,
        [((4, 112, 256), BF), ((6, 16, 256), BF), ((8, 256), F32)],
        (0,),
        [pltpu.VMEM((16, 256), F32)],
    )(info, got)
    wide = exchange(val, "y")
    base, route, back = call(
        base_kernel,
        [((4, 256), F32), ((128, 256), BF), ((128, 256), BF)],
        (0, 1),
        [pltpu.VMEM((4, 256), F32), pltpu.VMEM((128, 256), F32)],
    )(info, plane, dens, gat, own, bare, held)
    work = [
        pltpu.VMEM((6, 8, 256), F32),
        pltpu.VMEM((6, 8, 256), F32),
        pltpu.VMEM((2, 128, 256), F32),
        pltpu.VMEM((2, 128, 256), F32),
        pltpu.VMEM((4, 16, 256), F32),
    ]
    half, res = call(
        first_kernel, [((6, 256, 128), F32), ((4, 16, 256), BF)], (0,), work
    )(info, wide, cond, screened, base)
    parts = exchange(res, "y")
    (column,) = call(column_kernel, [((16, 16, 256), BF)], ())(parts)
    columns = exchange(column, "z")
    (middle,) = call(middle_kernel, [((32, 16, 256), BF)], ())(route, columns)
    arrived = exchange(middle, BLOCK)
    out2, own_x = call(
        second_kernel,
        [((16, 16, 384), BF), ((4, 256), F32)],
        (0,),
        work + [pltpu.VMEM((16, 128), F32)],
    )(info, arrived, half, cond, own)
    returned = exchange(out2, SHEET)
    (final,) = call(return_kernel, [((16, 16, 256), BF)], (0,), [pltpu.VMEM((8, 256), F32)])(
        info, back, returned
    )
    keep, send = call(
        cross_kernel, [((16, 256), F32), ((16, 256), BF)], (0,), [pltpu.VMEM((16, 256), F32)]
    )(info, exchange(final, "z"))
    (result,) = call(last_kernel, [(trial.shape, F32)], (0,))(
        cheb, keep, swap(send), own, bare, held, own_x
    )
    return result


def solution(mesh):
    split = Mesh(mesh.devices.reshape(16, 4, 2, mesh.shape["vert"]), ("z", "x", "c", "y"))
    in_specs = (
        P(PB, None, "y"),
        P(PB, None),
        P("y", PB, None),
        P(PB, None, "y"),
        P(),
        P(),
        P(PB),
        P(PB),
        P(),
    )
    out_specs = P("y", PB, None)
    return jax.shard_map(body, mesh=split, in_specs=in_specs, out_specs=out_specs, check_vma=False)
```

```python
import jax
import jax.numpy as jnp
from jax import lax
from jax.experimental import pallas as pl
from jax.experimental.pallas import tpu as pltpu
from jax.sharding import Mesh
from jax.sharding import PartitionSpec as P


BF = jnp.bfloat16
F32 = jnp.float32
LAST = (((1,), (1,)), ((), ()))
PB = ("z", "x", "c")
PLANE = ("x", "c")
BLOCK = ("x", "c", "y")
LIMIT = 12 << 20


def exchange(blocks, axis):
    return lax.all_to_all(blocks, axis, 0, 0, tiled=True)


def swap(shard):
    return lax.ppermute(shard, "c", [(0, 1), (1, 0)])


def dot(a, b):
    return jnp.dot(a, b, preferred_element_type=F32)


def dot_t(a, b):
    return lax.dot_general(a, b, LAST, preferred_element_type=F32)


def call(kernel, outs, smem, scratch=(), far=(), limit=LIMIT):
    def space(k):
        return pltpu.SMEM if k in smem else pltpu.HBM if k in far else pltpu.VMEM

    def run(*args):
        specs = [pl.BlockSpec(memory_space=space(k)) for k in range(len(args))]
        return pl.pallas_call(
            kernel,
            out_shape=[jax.ShapeDtypeStruct(s, d) for s, d in outs],
            in_specs=specs,
            out_specs=[
                pl.BlockSpec(memory_space=pltpu.SMEM if len(s) == 1 else pltpu.VMEM)
                for s, _ in outs
            ],
            scratch_shapes=list(scratch),
            compiler_params=pltpu.CompilerParams(vmem_limit_bytes=limit),
            cost_estimate=pl.CostEstimate(flops=0, transcendentals=0, bytes_accessed=4 << 20),
        )(*args)

    return run


def lanes(rows, width):
    return lax.broadcasted_iota(jnp.int32, (rows, width), 1)


def products_of(own_ref, s, part):
    val = own_ref[part, s, 0:16, :].astype(F32)
    cond = own_ref[part, s, 16:32, :].astype(F32)
    pieces = [(val[v : v + 1, :] * cond).astype(BF) for v in range(16)]
    return jnp.concatenate(pieces, axis=0)


def density_of(own_ref, rows_bf):
    parts = []
    for part in range(4):
        total = dot(rows_bf[0], products_of(own_ref, 0, part))
        total = total + dot(rows_bf[1], products_of(own_ref, 1, part))
        parts.append(total)
    return parts


def bare_of(own_ref, bare_ref, dens):
    pots = []
    for out in range(4):
        total = jnp.zeros((2, 256), F32)
        for part in range(4):
            total = total + dot_t(
                dens[part].astype(BF),
                bare_ref[out * 256 : (out + 1) * 256, part * 256 : (part + 1) * 256],
            )
        pots.append(total.astype(BF))
    terms = []
    for s in range(2):
        total = jnp.zeros((2, 256), F32)
        for part in range(4):
            total = total + dot_t(pots[part], products_of(own_ref, s, part))
        terms.append(total)
    return terms


def info_kernel(
    pair_hbm, slot_hbm, order_hbm, orb_hbm, trial_hbm, trans_hbm,
    info_ref, ids_ref, own_ref, held_ref, pair_ref, slot_ref, order_ref, trial_ref, trans_ref, sem,
):
    moves = [
        (pair_hbm, pair_ref), (slot_hbm, slot_ref), (order_hbm, order_ref),
        (trial_hbm, trial_ref), (trans_hbm, trans_ref),
    ] + [(orb_hbm, own_ref.at[part]) for part in range(4)]
    copies = [pltpu.make_async_copy(a, b, sem.at[k]) for k, (a, b) in enumerate(moves)]
    for copy in copies:
        copy.start()
    for copy in copies[:3]:
        copy.wait()
    position = lax.axis_index(PB)
    lane = lanes(1, 256)
    short = lanes(1, 128)
    order = order_ref[...]
    ids = jnp.where(short == 6, position * 2, jnp.where(short == 7, position * 2 + 1, 0))
    for i in range(3):
        first = pair_ref[i]
        second = first - position * 2 - slot_ref[i]
        second = jnp.where(second < 0, second + 256, second)
        for h, k in enumerate((first, second)):
            row = jnp.sum(jnp.where(order == k, lane, 0))
            info_ref[2 * i + h] = row
            ids = jnp.where(short == 2 * i + h, row, ids)
        info_ref[11 + i] = slot_ref[i]
    info_ref[6] = position * 2
    info_ref[7] = position * 2 + 1
    info_ref[8] = lax.axis_index("z")
    info_ref[9] = lax.axis_index(PLANE)
    info_ref[10] = lax.axis_index("y")
    info_ref[14] = 0
    info_ref[15] = 0
    for peer in range(8):
        ids_ref[peer] = ids
    for copy in copies[3:]:
        copy.wait()
    held_ref[...] = jnp.zeros((8, 256), F32)
    for s in range(2):
        held_ref[2 * s : 2 * s + 2, :] = trial_ref[:, s, :]
    held_ref[4:6, :] = trans_ref[...]


def pack_kernel(info_ref, held_ref, own_ref, out_ref, tail_ref):
    out_ref[0:64, :] = own_ref[info_ref[10]].reshape(64, 256)
    rows = [held_ref[2 * s : 2 * s + 2, :].astype(BF) for s in range(2)]
    parts = density_of(own_ref, rows)
    tail_ref[...] = jnp.zeros((16, 256), F32)
    for s in range(2):
        tail_ref[2 * s : 2 * s + 2, :] = rows[s].astype(F32)
    for part in range(4):
        tail_ref[4 + 2 * part : 6 + 2 * part, :] = parts[part]
    kind = lax.rem(lanes(1, 256), 16) // 2
    ids = jnp.zeros((1, 256), jnp.int32)
    for e in range(8):
        ids = jnp.where(kind == e, info_ref[e], ids)
    tail_ref[12:13, :] = ids.astype(F32)
    out_ref[64:80, :] = tail_ref[...].astype(BF)


def select_kernel(info_ref, plane_ref, gat_ref, twin_ref, out_ref, pick_ref):
    lane = lanes(1, 512)
    core = lax.rem(info_ref[9], 2)
    pick_ref[...] = jnp.zeros((128, 512), F32)
    for peer in range(4):
        for e in range(6):
            row = plane_ref[2 * peer + core, 0, e]
            z = row // 16
            s = lax.rem(row, 2)
            ours = lax.rem(row // 2, 2) == core
            first = z * 16 + 2 * s + jnp.where(ours, 0, 256)
            for n in range(2):
                at = peer * 32 + 2 * e + n
                pick_ref[at : at + 1, :] = (lane == first + n).astype(F32)
            at = pl.multiple_of(s * 32, 32)

            @pl.when(ours)
            def _():
                out_ref[peer, 32 * e : 32 * e + 32, :] = gat_ref[z, pl.ds(at, 32), :]

            @pl.when(jnp.logical_not(ours))
            def _():
                out_ref[peer, 32 * e : 32 * e + 32, :] = twin_ref[z, pl.ds(at, 32), :]

        for d in range(8):
            at = peer * 32 + 16 + d
            pick_ref[at : at + 1, :] = (lax.rem(lane, 16) == 4 + d).astype(F32)
    pick = pick_ref[...].astype(BF)
    picked = dot(pick[:, 0:256], gat_ref[:, 64:80, :].reshape(256, 256))
    picked = picked + dot(pick[:, 256:512], twin_ref[:, 64:80, :].reshape(256, 256))
    out_ref[:, 192:224, :] = picked.astype(BF).reshape(4, 32, 256)


def accept_kernel(info_ref, got_ref, val_ref, cond_ref, dens_ref, tail_ref):
    for e in range(6):
        column = lax.rem(info_ref[e] // 4, 4)
        val = got_ref[column, 32 * e : 32 * e + 16, :]
        for part in range(4):
            val_ref[part, 16 * e : 16 * e + 16, :] = val
        cond_ref[e] = got_ref[column, 32 * e + 16 : 32 * e + 32, :]
        part = got_ref[column, 192:208, :].astype(F32)
        tail_ref[2 * e : 2 * e + 2, :] = part[2 * e : 2 * e + 2, :]
    tail_ref[12:16, :] = jnp.zeros((4, 256), F32)
    for part in range(4):
        val_ref[part, 96:112, :] = tail_ref[...].astype(BF)
    total = got_ref[0, 208:224, :].astype(F32)
    for peer in range(1, 4):
        total = total + got_ref[peer, 208:224, :].astype(F32)
    dens_ref[...] = total[0:8, :]


def base_kernel(
    info_ref, plane_ref, dens_ref, gat_ref, own_ref, bare_ref, held_ref,
    base_ref, route_ref, back_ref, base_s, route_s,
):
    dens = [dens_ref[2 * part : 2 * part + 2, :] for part in range(4)]
    terms = bare_of(own_ref, bare_ref, dens)
    for s in range(2):
        x = held_ref[2 * s : 2 * s + 2, :].astype(BF).astype(F32)
        base_s[2 * s : 2 * s + 2, :] = held_ref[4 + s : 5 + s, :] * x + 2.0 * terms[s]
    base_ref[...] = base_s[...]

    lane = lanes(1, 256)
    held = jnp.zeros((1, 256), F32)
    for z in range(16):
        row = gat_ref[z, 64:80, :].astype(F32)[12:13, :]
        held = jnp.where(lane // 16 == z, row, held)
    held = held.astype(jnp.int32)
    parity = lax.rem(lane, 2)
    z_me = info_ref[8]
    q_me = info_ref[9]
    for peer in range(8):
        for k in range(8):
            row = plane_ref[peer, 0, k] if k < 6 else z_me * 16 + peer * 2 + (k - 6)
            for n in range(2):
                at = peer * 16 + 2 * k + n
                hit = (held == row) & (parity == n)
                route_s[at : at + 1, :] = jnp.where(hit, -1.0 if k < 6 else 1.0, 0.0)
    route_ref[...] = jnp.transpose(route_s[...]).astype(BF)

    wide = lanes(1, 512)
    sent = jnp.full((1, 512), -1, jnp.int32)
    for peer in range(8):
        for e in range(6):
            here = (wide // 64 == peer) & (lax.rem(wide, 16) // 2 == e)
            sent = jnp.where(here, plane_ref[peer, 0, e], sent)
    row = lax.broadcasted_iota(jnp.int32, (64, 512), 0)
    target = (row // 4) * 16 + q_me * 2 + lax.rem(row, 4) // 2
    hit = (sent == target) & (lax.rem(row, 2) == lax.rem(lanes(64, 512), 2))
    back_ref[...] = jnp.where(hit, -1.0, 0.0).astype(BF)


def spread(x):
    rows = jnp.concatenate([x] * 16, axis=0)
    group = lax.broadcasted_iota(jnp.int32, (128, 256), 0) // 8
    return jnp.where(group == lanes(128, 256) // 16, rows, 0.0).astype(BF)


def gathered(full):
    group = lax.broadcasted_iota(jnp.int32, (128, 256), 0) // 8
    kept = jnp.where(group == lanes(128, 256) // 16, full, 0.0)
    total = kept[0:8, :]
    for v in range(1, 16):
        total = total + kept[8 * v : 8 * v + 8, :]
    return total


def apply_pair(i, half_ref, cond_ref, xs_ref, ys_ref, t_ref, u_ref):
    tile_a = jnp.concatenate([cond_ref[2 * i]] * 16, axis=0)
    tile_c = jnp.concatenate([cond_ref[2 * i + 1]] * 16, axis=0)
    t_ref[0] = dot(spread(xs_ref[2 * i]), tile_a)
    t_ref[1] = dot(spread(xs_ref[2 * i + 1]), tile_c)
    for part in range(2):
        at = slice(128 * part, 128 * part + 128)
        t_c = [t_ref[1, 8 * w : 8 * w + 8, at] for w in range(16)]
        u_c = [None] * 16
        for v in range(16):
            t_a = t_ref[0, 8 * v : 8 * v + 8, at]
            sums = [None] * 2
            for w in range(16):
                row = 16 * v + w
                h = jnp.broadcast_to(half_ref[2 * i + part, row : row + 1, :], (8, 128))
                one, two = h * t_c[w], h * t_a
                sums[w % 2] = one if w < 2 else sums[w % 2] + one
                u_c[w] = two if v == 0 else u_c[w] + two
            u_ref[0, 8 * v : 8 * v + 8, at] = sums[0] + sums[1]
        for w in range(16):
            u_ref[1, 8 * w : 8 * w + 8, at] = u_c[w]
    ys_ref[2 * i] = gathered(dot_t(u_ref[0].astype(BF), tile_a))
    ys_ref[2 * i + 1] = gathered(dot_t(u_ref[1].astype(BF), tile_c))


def first_kernel(
    info_ref, wide_ref, cond_ref, scr_ref, base_ref, half_ref, res_ref,
    xs_ref, ys_ref, t_ref, u_ref, rs_ref,
):
    for part in range(4):
        tail = wide_ref[part, 96:112, :].astype(F32)
        for e in range(6):
            xs_ref[e, 2 * part : 2 * part + 2, :] = tail[2 * e : 2 * e + 2, :]

    def one(i, carry):
        slot = info_ref[11 + i]
        total = jnp.zeros((256, 256), F32)
        for part in range(4):
            at = pl.multiple_of(i * 32, 16)
            a = wide_ref[part, pl.ds(at, 16), :].astype(F32)
            b = wide_ref[part, pl.ds(at + 16, 16), :].astype(F32)
            left = jnp.concatenate(
                [(a[v : v + 1, :] * b).astype(BF) for v in range(16)], axis=0
            )
            total = total + dot(left, scr_ref[slot, part * 256 : (part + 1) * 256, :])
        total = total.astype(BF).astype(F32)
        half_ref[2 * i] = total[:, 0:128]
        half_ref[2 * i + 1] = total[:, 128:256]
        apply_pair(i, half_ref, cond_ref, xs_ref, ys_ref, t_ref, u_ref)
        return carry

    lax.fori_loop(0, 3, one, 0)
    for part in range(4):
        for e in range(6):
            rs_ref[part, 2 * e : 2 * e + 2, :] = ys_ref[e, 2 * part : 2 * part + 2, :]
        mine = (info_ref[10] == part).astype(F32)
        rs_ref[part, 12:16, :] = base_ref[...] * mine
    for peer in range(8):
        for part in range(4):
            res_ref[4 * peer + part] = rs_ref[part].astype(BF)


def middle_kernel(route_ref, got_ref, out_ref):
    peers = []
    for peer in range(8):
        total = got_ref[4 * peer].astype(F32)
        for part in range(1, 4):
            total = total + got_ref[4 * peer + part].astype(F32)
        peers.append(total.astype(BF))
    full = dot(route_ref[...], jnp.concatenate(peers, axis=0))
    out_ref[...] = full.astype(BF).reshape(16, 16, 256)


def step_kernel(got_ref, out_ref, own_x_ref):
    total = got_ref[0].astype(F32)
    for z in range(1, 16):
        total = total + got_ref[z].astype(F32)
    own_x_ref[...] = total[12:16, :]
    for part in range(4):
        out_ref[part] = total.astype(BF)


def density_kernel(own_x_ref, own_ref, out_ref, ds_ref):
    rows = [own_x_ref[2 * s : 2 * s + 2, :].astype(BF) for s in range(2)]
    parts = density_of(own_ref, rows)
    for part in range(4):
        for h in range(2):
            at = 4 * part + 2 * h
            ds_ref[at : at + 2, :] = parts[part][:, 128 * h : 128 * h + 128]
    out_ref[...] = ds_ref[...].astype(BF)


def second_kernel(
    got_ref, ds_ref, half_ref, cond_ref, out_ref, xs_ref, ys_ref, t_ref, u_ref, rs_ref,
):
    for part in range(4):
        total = got_ref[part].astype(F32)
        for e in range(6):
            xs_ref[e, 2 * part : 2 * part + 2, :] = total[2 * e : 2 * e + 2, :]

    def one(i, carry):
        apply_pair(i, half_ref, cond_ref, xs_ref, ys_ref, t_ref, u_ref)
        return carry

    lax.fori_loop(0, 3, one, 0)
    rs_ref[...] = jnp.zeros((4, 16, 256), F32)
    for part in range(4):
        for e in range(6):
            rs_ref[part, 2 * e : 2 * e + 2, :] = ys_ref[e, 2 * part : 2 * part + 2, :]
    for peer in range(8):
        for part in range(4):
            out_ref[4 * peer + part, :, 0:256] = rs_ref[part].astype(BF)
            out_ref[4 * peer + part, :, 256:384] = ds_ref[...]


def return_kernel(info_ref, back_ref, got_ref, out_ref, buf_ref):
    full = dot(back_ref[...], got_ref[:, :, 0:256].reshape(512, 256))
    y_me = info_ref[10]
    total = got_ref[y_me, :, 256:384].astype(F32)
    for peer in range(1, 8):
        total = total + got_ref[4 * peer + y_me, :, 256:384].astype(F32)
    buf_ref[...] = jnp.zeros((16, 16, 256), F32)
    for part in range(4):
        for h in range(2):
            at = 4 * part + 2 * h
            buf_ref[0, 4 + 2 * part : 6 + 2 * part, 128 * h : 128 * h + 128] = total[at : at + 2, :]
    for z in range(16):
        if z:
            buf_ref[z, 4:12, :] = buf_ref[0, 4:12, :]
        buf_ref[z, 0:4, :] = full[4 * z : 4 * z + 4, :]
    out_ref[...] = buf_ref[...].astype(BF)


def last_kernel(cheb_ref, got_ref, own_ref, bare_ref, held_ref, own_x_ref, out_ref):
    total = got_ref[0].astype(F32)
    for z in range(1, 16):
        total = total + got_ref[z].astype(F32)
    dens = [total[4 + 2 * part : 6 + 2 * part, :] for part in range(4)]
    terms = bare_of(own_ref, bare_ref, dens)
    for s in range(2):
        x = own_x_ref[2 * s : 2 * s + 2, :]
        t = held_ref[2 * s : 2 * s + 2, :]
        applied = (
            held_ref[4 + s : 5 + s, :] * x.astype(BF).astype(F32)
            + 2.0 * terms[s]
            + total[2 * s : 2 * s + 2, :]
        )
        second = 2.0 * applied - t
        out_ref[:, s, :] = cheb_ref[0] * t + cheb_ref[1] * x + cheb_ref[2] * second


def body(orbitals, transition, trial, screened, bare, cheb, pair_k, pair_slot, k_order):
    info, ids, copies, held = call(
        info_kernel,
        [
            ((16,), jnp.int32), ((8, 1, 128), jnp.int32), ((4, 2, 32, 256), BF), ((8, 256), F32),
        ],
        (),
        [
            pltpu.SMEM((3,), jnp.int32),
            pltpu.SMEM((3,), jnp.int32),
            pltpu.VMEM((1, 256), jnp.int32),
            pltpu.VMEM((2, 2, 256), F32),
            pltpu.VMEM((2, 256), F32),
            pltpu.SemaphoreType.DMA((9,)),
        ],
        range(6),
        66600000,
    )(pair_k, pair_slot, k_order.reshape(1, -1), orbitals, trial, transition)
    own = exchange(copies, "y")
    plane = exchange(ids, PLANE)
    (packed,) = call(pack_kernel, [((80, 256), BF)], (0,), [pltpu.VMEM((16, 256), F32)])(
        info, held, own
    )
    gat = lax.all_gather(packed, "z")
    twin = swap(gat)
    (chosen,) = call(select_kernel, [((4, 224, 256), BF)], (0, 1), [pltpu.VMEM((128, 512), F32)])(
        info, plane, gat, twin
    )
    got = exchange(chosen, "x")
    val, cond, dens = call(
        accept_kernel,
        [((4, 112, 256), BF), ((6, 16, 256), BF), ((8, 256), F32)],
        (0,),
        [pltpu.VMEM((16, 256), F32)],
    )(info, got)
    wide = exchange(val, "y")
    base, route, back = call(
        base_kernel,
        [((4, 256), F32), ((256, 128), BF), ((64, 512), BF)],
        (0, 1),
        [pltpu.VMEM((4, 256), F32), pltpu.VMEM((128, 256), F32)],
    )(info, plane, dens, gat, own, bare, held)
    work = [
        pltpu.VMEM((6, 8, 256), F32),
        pltpu.VMEM((6, 8, 256), F32),
        pltpu.VMEM((2, 128, 256), F32),
        pltpu.VMEM((2, 128, 256), F32),
        pltpu.VMEM((4, 16, 256), F32),
    ]
    half, res = call(
        first_kernel, [((6, 256, 128), F32), ((32, 16, 256), BF)], (0,), work
    )(info, wide, cond, screened, base)
    (middle,) = call(middle_kernel, [((16, 16, 256), BF)], ())(route, exchange(res, BLOCK))
    step, own_x = call(step_kernel, [((4, 16, 256), BF), ((4, 256), F32)], ())(
        exchange(middle, "z")
    )
    (dens2,) = call(density_kernel, [((16, 128), BF)], (), [pltpu.VMEM((16, 128), F32)])(
        own_x, own
    )
    (out2,) = call(second_kernel, [((32, 16, 384), BF)], (), work)(
        exchange(step, "y"), dens2, half, cond
    )
    (final,) = call(
        return_kernel, [((16, 16, 256), BF)], (0,), [pltpu.VMEM((16, 16, 256), F32)]
    )(info, back, exchange(out2, BLOCK))
    last = exchange(final, "z")
    (result,) = call(last_kernel, [(trial.shape, F32)], (0,))(
        cheb, last, own, bare, held, own_x
    )
    return result


def solution(mesh):
    split = Mesh(mesh.devices.reshape(16, 4, 2, mesh.shape["vert"]), ("z", "x", "c", "y"))
    in_specs = (
        P(PB, None, "y"),
        P(PB, None),
        P("y", PB, None),
        P(PB, None, "y"),
        P(),
        P(),
        P(PB),
        P(PB),
        P(),
    )
    out_specs = P("y", PB, None)
    return jax.shard_map(body, mesh=split, in_specs=in_specs, out_specs=out_specs, check_vma=False)
```

```python
import jax
import jax.numpy as jnp
from jax import lax
from jax.experimental import pallas as pl
from jax.experimental.pallas import tpu as pltpu
from jax.sharding import Mesh
from jax.sharding import PartitionSpec as P


BF = jnp.bfloat16
F32 = jnp.float32
LAST = (((1,), (1,)), ((), ()))
PB = ("z", "x", "c")
PLANE = ("x", "c")
BLOCK = ("x", "c", "y")
LIMIT = 12 << 20


def exchange(blocks, axis):
    return lax.all_to_all(blocks, axis, 0, 0, tiled=True)


def swap(shard):
    return lax.ppermute(shard, "c", [(0, 1), (1, 0)])


def shift(shard, by):
    count = lax.axis_size("y")
    return lax.ppermute(shard, "y", [(k, (k + by) % count) for k in range(count)])


def dot(a, b):
    return jnp.dot(a, b, preferred_element_type=F32)


def dot_t(a, b):
    return lax.dot_general(a, b, LAST, preferred_element_type=F32)


def call(kernel, outs, smem, scratch=(), far=(), limit=LIMIT):
    def space(k):
        return pltpu.SMEM if k in smem else pltpu.HBM if k in far else pltpu.VMEM

    def run(*args):
        specs = [pl.BlockSpec(memory_space=space(k)) for k in range(len(args))]
        return pl.pallas_call(
            kernel,
            out_shape=[jax.ShapeDtypeStruct(s, d) for s, d in outs],
            in_specs=specs,
            out_specs=[
                pl.BlockSpec(memory_space=pltpu.SMEM if len(s) == 1 else pltpu.VMEM)
                for s, _ in outs
            ],
            scratch_shapes=list(scratch),
            compiler_params=pltpu.CompilerParams(vmem_limit_bytes=limit),
            cost_estimate=pl.CostEstimate(flops=0, transcendentals=0, bytes_accessed=4 << 20),
        )(*args)

    return run


def lanes(rows, width):
    return lax.broadcasted_iota(jnp.int32, (rows, width), 1)


def products_of(own_ref, s, part):
    val = own_ref[part, s, 0:16, :].astype(F32)
    cond = own_ref[part, s, 16:32, :].astype(F32)
    pieces = [(val[v : v + 1, :] * cond).astype(BF) for v in range(16)]
    return jnp.concatenate(pieces, axis=0)


def density_of(own_ref, rows_bf):
    parts = []
    for part in range(4):
        total = dot(rows_bf[0], products_of(own_ref, 0, part))
        total = total + dot(rows_bf[1], products_of(own_ref, 1, part))
        parts.append(total)
    return parts


def bare_of(own_ref, bare_ref, dens):
    pots = []
    for out in range(4):
        total = jnp.zeros((2, 256), F32)
        for part in range(4):
            total = total + dot_t(
                dens[part].astype(BF),
                bare_ref[out * 256 : (out + 1) * 256, part * 256 : (part + 1) * 256],
            )
        pots.append(total.astype(BF))
    terms = []
    for s in range(2):
        total = jnp.zeros((2, 256), F32)
        for part in range(4):
            total = total + dot_t(pots[part], products_of(own_ref, s, part))
        terms.append(total)
    return terms


def info_kernel(
    pair_hbm, slot_hbm, order_hbm, orb_hbm, trial_hbm, trans_hbm,
    info_ref, ids_ref, own_ref, held_ref, pair_ref, slot_ref, order_ref, trial_ref, trans_ref, sem,
):
    moves = [
        (pair_hbm, pair_ref), (slot_hbm, slot_ref), (order_hbm, order_ref),
        (trial_hbm, trial_ref), (trans_hbm, trans_ref),
    ] + [(orb_hbm, own_ref.at[part]) for part in range(4)]
    copies = [pltpu.make_async_copy(a, b, sem.at[k]) for k, (a, b) in enumerate(moves)]
    for copy in copies:
        copy.start()
    for copy in copies[:3]:
        copy.wait()
    position = lax.axis_index(PB)
    lane = lanes(1, 256)
    short = lanes(1, 128)
    order = order_ref[...]
    ids = jnp.where(short == 6, position * 2, jnp.where(short == 7, position * 2 + 1, 0))
    for i in range(3):
        first = pair_ref[i]
        second = first - position * 2 - slot_ref[i]
        second = jnp.where(second < 0, second + 256, second)
        for h, k in enumerate((first, second)):
            row = jnp.sum(jnp.where(order == k, lane, 0))
            info_ref[2 * i + h] = row
            ids = jnp.where(short == 2 * i + h, row, ids)
        info_ref[11 + i] = slot_ref[i]
    info_ref[6] = position * 2
    info_ref[7] = position * 2 + 1
    info_ref[8] = lax.axis_index("z")
    info_ref[9] = lax.axis_index(PLANE)
    info_ref[10] = lax.axis_index("y")
    info_ref[14] = 0
    info_ref[15] = 0
    for peer in range(8):
        ids_ref[peer] = ids
    for copy in copies[3:]:
        copy.wait()
    held_ref[...] = jnp.zeros((8, 256), F32)
    for s in range(2):
        held_ref[2 * s : 2 * s + 2, :] = trial_ref[:, s, :]
    held_ref[4:6, :] = trans_ref[...]


def pack_kernel(info_ref, held_ref, own_ref, out_ref, tail_ref):
    out_ref[0:64, :] = own_ref[info_ref[10]].reshape(64, 256)
    rows = [held_ref[2 * s : 2 * s + 2, :].astype(BF) for s in range(2)]
    parts = density_of(own_ref, rows)
    tail_ref[...] = jnp.zeros((16, 256), F32)
    for s in range(2):
        tail_ref[2 * s : 2 * s + 2, :] = rows[s].astype(F32)
    for part in range(4):
        tail_ref[4 + 2 * part : 6 + 2 * part, :] = parts[part]
    kind = lax.rem(lanes(1, 256), 16) // 2
    ids = jnp.zeros((1, 256), jnp.int32)
    for e in range(8):
        ids = jnp.where(kind == e, info_ref[e], ids)
    tail_ref[12:13, :] = ids.astype(F32)
    out_ref[64:80, :] = tail_ref[...].astype(BF)


def select_kernel(info_ref, plane_ref, gat_ref, twin_ref, out_ref, pick_ref):
    lane = lanes(1, 512)
    core = lax.rem(info_ref[9], 2)
    pick_ref[...] = jnp.zeros((128, 512), F32)
    for peer in range(4):
        for e in range(6):
            row = plane_ref[2 * peer + core, 0, e]
            z = row // 16
            s = lax.rem(row, 2)
            ours = lax.rem(row // 2, 2) == core
            first = z * 16 + 2 * s + jnp.where(ours, 0, 256)
            for n in range(2):
                at = peer * 32 + 2 * e + n
                pick_ref[at : at + 1, :] = (lane == first + n).astype(F32)
            at = pl.multiple_of(s * 32, 32)

            @pl.when(ours)
            def _():
                out_ref[peer, 32 * e : 32 * e + 32, :] = gat_ref[z, pl.ds(at, 32), :]

            @pl.when(jnp.logical_not(ours))
            def _():
                out_ref[peer, 32 * e : 32 * e + 32, :] = twin_ref[z, pl.ds(at, 32), :]

        for d in range(8):
            at = peer * 32 + 16 + d
            pick_ref[at : at + 1, :] = (lax.rem(lane, 16) == 4 + d).astype(F32)
    pick = pick_ref[...].astype(BF)
    picked = dot(pick[:, 0:256], gat_ref[:, 64:80, :].reshape(256, 256))
    picked = picked + dot(pick[:, 256:512], twin_ref[:, 64:80, :].reshape(256, 256))
    out_ref[:, 192:224, :] = picked.astype(BF).reshape(4, 32, 256)


def accept_kernel(info_ref, got_ref, val_ref, cond_ref, dens_ref, tail_ref):
    for e in range(6):
        column = lax.rem(info_ref[e] // 4, 4)
        val = got_ref[column, 32 * e : 32 * e + 16, :]
        for part in range(4):
            val_ref[part, 16 * e : 16 * e + 16, :] = val
        cond_ref[e] = got_ref[column, 32 * e + 16 : 32 * e + 32, :]
        part = got_ref[column, 192:208, :].astype(F32)
        tail_ref[2 * e : 2 * e + 2, :] = part[2 * e : 2 * e + 2, :]
    tail_ref[12:16, :] = jnp.zeros((4, 256), F32)
    for part in range(4):
        val_ref[part, 96:112, :] = tail_ref[...].astype(BF)
    total = got_ref[0, 208:224, :].astype(F32)
    for peer in range(1, 4):
        total = total + got_ref[peer, 208:224, :].astype(F32)
    dens_ref[...] = total[0:8, :]


def base_kernel(
    info_ref, plane_ref, dens_ref, gat_ref, own_ref, bare_ref, held_ref,
    base_ref, route_ref, back_ref, base_s, route_s,
):
    dens = [dens_ref[2 * part : 2 * part + 2, :] for part in range(4)]
    terms = bare_of(own_ref, bare_ref, dens)
    for s in range(2):
        x = held_ref[2 * s : 2 * s + 2, :].astype(BF).astype(F32)
        base_s[2 * s : 2 * s + 2, :] = held_ref[4 + s : 5 + s, :] * x + 2.0 * terms[s]
    base_ref[...] = base_s[...]

    lane = lanes(1, 256)
    held = jnp.zeros((1, 256), F32)
    for z in range(16):
        row = gat_ref[z, 64:80, :].astype(F32)[12:13, :]
        held = jnp.where(lane // 16 == z, row, held)
    held = held.astype(jnp.int32)
    parity = lax.rem(lane, 2)
    z_me = info_ref[8]
    q_me = info_ref[9]
    for peer in range(8):
        for k in range(8):
            row = plane_ref[peer, 0, k] if k < 6 else z_me * 16 + peer * 2 + (k - 6)
            for n in range(2):
                at = peer * 16 + 2 * k + n
                hit = (held == row) & (parity == n)
                route_s[at : at + 1, :] = jnp.where(hit, -1.0 if k < 6 else 1.0, 0.0)
    route_ref[...] = jnp.transpose(route_s[...]).astype(BF)

    wide = lanes(1, 128)
    sent = jnp.full((1, 128), -1, jnp.int32)
    for peer in range(8):
        for e in range(6):
            here = (wide // 16 == peer) & (lax.rem(wide, 16) // 2 == e)
            sent = jnp.where(here, plane_ref[peer, 0, e], sent)
    row = lax.broadcasted_iota(jnp.int32, (64, 128), 0)
    target = (row // 4) * 16 + q_me * 2 + lax.rem(row, 4) // 2
    hit = (sent == target) & (lax.rem(row, 2) == lax.rem(lanes(64, 128), 2))
    back_ref[...] = jnp.where(hit, -1.0, 0.0).astype(BF)


def spread(x):
    rows = jnp.concatenate([x] * 16, axis=0)
    group = lax.broadcasted_iota(jnp.int32, (128, 256), 0) // 8
    return jnp.where(group == lanes(128, 256) // 16, rows, 0.0).astype(BF)


def gathered(full):
    group = lax.broadcasted_iota(jnp.int32, (128, 256), 0) // 8
    kept = jnp.where(group == lanes(128, 256) // 16, full, 0.0)
    total = kept[0:8, :]
    for v in range(1, 16):
        total = total + kept[8 * v : 8 * v + 8, :]
    return total


def apply_pair(i, half_ref, cond_ref, xs_ref, ys_ref, t_ref, u_ref):
    tile_a = jnp.concatenate([cond_ref[2 * i]] * 16, axis=0)
    tile_c = jnp.concatenate([cond_ref[2 * i + 1]] * 16, axis=0)
    t_ref[0] = dot(spread(xs_ref[2 * i]), tile_a)
    t_ref[1] = dot(spread(xs_ref[2 * i + 1]), tile_c)
    for part in range(2):
        at = slice(128 * part, 128 * part + 128)
        t_c = [t_ref[1, 8 * w : 8 * w + 8, at] for w in range(16)]
        u_c = [None] * 16
        for v in range(16):
            t_a = t_ref[0, 8 * v : 8 * v + 8, at]
            sums = [None] * 2
            for w in range(16):
                row = 16 * v + w
                h = jnp.broadcast_to(half_ref[2 * i + part, row : row + 1, :], (8, 128))
                one, two = h * t_c[w], h * t_a
                sums[w % 2] = one if w < 2 else sums[w % 2] + one
                u_c[w] = two if v == 0 else u_c[w] + two
            u_ref[0, 8 * v : 8 * v + 8, at] = sums[0] + sums[1]
        for w in range(16):
            u_ref[1, 8 * w : 8 * w + 8, at] = u_c[w]
    ys_ref[2 * i] = gathered(dot_t(u_ref[0].astype(BF), tile_a))
    ys_ref[2 * i + 1] = gathered(dot_t(u_ref[1].astype(BF), tile_c))


def first_kernel(
    info_ref, wide_ref, cond_ref, scr_ref, base_ref, op_ref, res_ref,
    xs_ref, ys_ref, t_ref, u_ref, rs_ref, half_ref,
):
    for e in range(6):
        op_ref[0, 768 + 16 * e : 784 + 16 * e, :] = cond_ref[e, :, 0:128]
        op_ref[1, 768 + 16 * e : 784 + 16 * e, :] = cond_ref[e, :, 128:256]
    for part in range(4):
        tail = wide_ref[part, 96:112, :].astype(F32)
        for e in range(6):
            xs_ref[e, 2 * part : 2 * part + 2, :] = tail[2 * e : 2 * e + 2, :]

    def one(i, carry):
        slot = info_ref[11 + i]
        total = jnp.zeros((256, 256), F32)
        for part in range(4):
            at = pl.multiple_of(i * 32, 16)
            a = wide_ref[part, pl.ds(at, 16), :].astype(F32)
            b = wide_ref[part, pl.ds(at + 16, 16), :].astype(F32)
            left = jnp.concatenate(
                [(a[v : v + 1, :] * b).astype(BF) for v in range(16)], axis=0
            )
            total = total + dot(left, scr_ref[slot, part * 256 : (part + 1) * 256, :])
        total = total.astype(BF)
        at = pl.multiple_of(i * 256, 256)
        op_ref[0, pl.ds(at, 256), :] = total[:, 0:128]
        op_ref[1, pl.ds(at, 256), :] = total[:, 128:256]
        total = total.astype(F32)
        half_ref[2 * i] = total[:, 0:128]
        half_ref[2 * i + 1] = total[:, 128:256]
        apply_pair(i, half_ref, cond_ref, xs_ref, ys_ref, t_ref, u_ref)
        return carry

    lax.fori_loop(0, 3, one, 0)
    for part in range(4):
        for e in range(6):
            rs_ref[part, 2 * e : 2 * e + 2, :] = ys_ref[e, 2 * part : 2 * part + 2, :]
        mine = (info_ref[10] == part).astype(F32)
        rs_ref[part, 12:16, :] = base_ref[...] * mine
    for peer in range(8):
        for part in range(4):
            res_ref[4 * peer + part] = rs_ref[part].astype(BF)


def middle_kernel(route_ref, got_ref, out_ref):
    peers = []
    for peer in range(8):
        total = got_ref[4 * peer].astype(F32)
        for part in range(1, 4):
            total = total + got_ref[4 * peer + part].astype(F32)
        peers.append(total.astype(BF))
    full = dot(route_ref[...], jnp.concatenate(peers, axis=0))
    out_ref[...] = full.astype(BF).reshape(16, 16, 256)


def picker(rows, columns):
    row = lax.broadcasted_iota(jnp.int32, (rows, columns), 0)
    return (lax.rem(row, 16) == lax.rem(lanes(rows, columns), 16)).astype(BF)


def second_kernel(
    got_ref, own_ref, op_ref, left_ref, right_ref, far_ref, out_ref, own_x_ref,
    x_ref, y_ref, t_ref, ua_ref, uc_ref, rs_ref, ds_ref,
):
    total = got_ref[0].astype(F32)
    for z in range(1, 16):
        total = total + got_ref[z].astype(F32)
    own_x_ref[...] = total[12:16, :]
    parts = density_of(own_ref, [total[12 + 2 * s : 14 + 2 * s, :].astype(BF) for s in range(2)])
    for part in range(4):
        for h in range(2):
            at = 4 * part + 2 * h
            ds_ref[at : at + 2, :] = parts[part][:, 128 * h : 128 * h + 128]

    here = lanes(16, 256) // 16 == lax.broadcasted_iota(jnp.int32, (16, 256), 0)
    rows = [jnp.where(here, total[k : k + 1, :], 0.0).astype(BF) for k in range(12)]
    x_ref[...] = dot(jnp.concatenate(rows, axis=0), picker(256, 16)).astype(BF)

    chunks = [(ref, h) for ref in (op_ref, left_ref, right_ref, far_ref) for h in range(2)]

    def one(p, carry):
        at = pl.multiple_of(p * 64, 64)
        conds = []
        for end in range(2):
            row = pl.multiple_of(768 + p * 32 + end * 16, 16)
            conds.append(
                jnp.concatenate([ref[h, pl.ds(row, 16), :] for ref, h in chunks], axis=1)
            )
            t_ref[end] = dot(x_ref[pl.ds(pl.multiple_of(at + 32 * end, 32), 32), :], conds[end])
        for k, (ref, h) in enumerate(chunks):
            span = slice(128 * k, 128 * k + 128)
            t_c = [t_ref[1, 8 * g : 8 * g + 8, span] for g in range(4)]
            sums = [None] * 4
            for v in range(16):
                tile = ref[h, pl.ds(pl.multiple_of(p * 256 + 16 * v, 16), 16), :].astype(F32)
                lo, hi = tile[0:8, :], tile[8:16, :]
                for n in range(2):
                    ua_ref[128 * n + 8 * v : 128 * n + 8 * v + 8, span] = (
                        lo * t_c[2 * n] + hi * t_c[2 * n + 1]
                    )
                    t_a = jnp.broadcast_to(
                        t_ref[0, 16 * n + v : 16 * n + v + 1, span], (8, 128)
                    )
                    for g, part in ((2 * n, lo * t_a), (2 * n + 1, hi * t_a)):
                        sums[g] = part if v == 0 else sums[g] + part
            for g in range(4):
                uc_ref[8 * g : 8 * g + 8, span] = sums[g]
        first = dot_t(ua_ref[...].astype(BF), conds[0])
        y_ref[pl.ds(at, 32), :] = jnp.sum(first.reshape(32, 8, 16), axis=1)
        y_ref[pl.ds(pl.multiple_of(at + 32, 32), 32), :] = dot_t(uc_ref[...].astype(BF), conds[1])
        return carry

    lax.fori_loop(0, 3, one, 0)
    full = dot(y_ref[...].astype(BF), picker(16, 256)).reshape(12, 16, 256)
    rs_ref[0:12, :] = jnp.sum(jnp.where(here[None], full, 0.0), axis=1)
    rs_ref[12:16, :] = jnp.zeros((4, 256), F32)
    for peer in range(8):
        out_ref[peer, :, 0:256] = rs_ref[...].astype(BF)
        out_ref[peer, :, 256:384] = ds_ref[...].astype(BF)


def return_kernel(back_ref, got_ref, out_ref, buf_ref):
    full = dot(back_ref[...], got_ref[:, :, 0:256].reshape(128, 256))
    total = got_ref[0, :, 256:384].astype(F32)
    for peer in range(1, 8):
        total = total + got_ref[peer, :, 256:384].astype(F32)
    buf_ref[...] = jnp.zeros((16, 16, 256), F32)
    for part in range(4):
        for h in range(2):
            at = 4 * part + 2 * h
            buf_ref[0, 4 + 2 * part : 6 + 2 * part, 128 * h : 128 * h + 128] = total[at : at + 2, :]
    for z in range(16):
        if z:
            buf_ref[z, 4:12, :] = buf_ref[0, 4:12, :]
        buf_ref[z, 0:4, :] = full[4 * z : 4 * z + 4, :]
    out_ref[...] = buf_ref[...].astype(BF)


def last_kernel(cheb_ref, got_ref, own_ref, bare_ref, held_ref, own_x_ref, out_ref):
    total = got_ref[0].astype(F32)
    for z in range(1, 16):
        total = total + got_ref[z].astype(F32)
    dens = [total[4 + 2 * part : 6 + 2 * part, :] for part in range(4)]
    terms = bare_of(own_ref, bare_ref, dens)
    for s in range(2):
        x = own_x_ref[2 * s : 2 * s + 2, :]
        t = held_ref[2 * s : 2 * s + 2, :]
        applied = (
            held_ref[4 + s : 5 + s, :] * x.astype(BF).astype(F32)
            + 2.0 * terms[s]
            + total[2 * s : 2 * s + 2, :]
        )
        second = 2.0 * applied - t
        out_ref[:, s, :] = cheb_ref[0] * t + cheb_ref[1] * x + cheb_ref[2] * second


def body(orbitals, transition, trial, screened, bare, cheb, pair_k, pair_slot, k_order):
    info, ids, copies, held = call(
        info_kernel,
        [
            ((16,), jnp.int32), ((8, 1, 128), jnp.int32), ((4, 2, 32, 256), BF), ((8, 256), F32),
        ],
        (),
        [
            pltpu.SMEM((3,), jnp.int32),
            pltpu.SMEM((3,), jnp.int32),
            pltpu.VMEM((1, 256), jnp.int32),
            pltpu.VMEM((2, 2, 256), F32),
            pltpu.VMEM((2, 256), F32),
            pltpu.SemaphoreType.DMA((9,)),
        ],
        range(6),
        66600000,
    )(pair_k, pair_slot, k_order.reshape(1, -1), orbitals, trial, transition)
    own = exchange(copies, "y")
    plane = exchange(ids, PLANE)
    (packed,) = call(pack_kernel, [((80, 256), BF)], (0,), [pltpu.VMEM((16, 256), F32)])(
        info, held, own
    )
    gat = lax.all_gather(packed, "z")
    twin = swap(gat)
    (chosen,) = call(select_kernel, [((4, 224, 256), BF)], (0, 1), [pltpu.VMEM((128, 512), F32)])(
        info, plane, gat, twin
    )
    got = exchange(chosen, "x")
    val, cond, dens = call(
        accept_kernel,
        [((4, 112, 256), BF), ((6, 16, 256), BF), ((8, 256), F32)],
        (0,),
        [pltpu.VMEM((16, 256), F32)],
    )(info, got)
    wide = exchange(val, "y")
    base, route, back = call(
        base_kernel,
        [((4, 256), F32), ((256, 128), BF), ((64, 128), BF)],
        (0, 1),
        [pltpu.VMEM((4, 256), F32), pltpu.VMEM((128, 256), F32)],
    )(info, plane, dens, gat, own, bare, held)
    work = [
        pltpu.VMEM((6, 8, 256), F32),
        pltpu.VMEM((6, 8, 256), F32),
        pltpu.VMEM((2, 128, 256), F32),
        pltpu.VMEM((2, 128, 256), F32),
        pltpu.VMEM((4, 16, 256), F32),
    ]
    op, res = call(
        first_kernel,
        [((2, 864, 128), BF), ((32, 16, 256), BF)],
        (0,),
        work + [pltpu.VMEM((6, 256, 128), F32)],
    )(info, wide, cond, screened, base)
    mixed = exchange(res, BLOCK)
    left = shift(op, 1)
    right = shift(op, -1)
    (middle,) = call(middle_kernel, [((16, 16, 256), BF)], ())(route, mixed)
    step = exchange(middle, "z")
    far = shift(left, 1)
    out2, own_x = call(
        second_kernel,
        [((8, 16, 384), BF), ((4, 256), F32)],
        (),
        [
            pltpu.VMEM((192, 16), BF),
            pltpu.VMEM((192, 16), F32),
            pltpu.VMEM((2, 32, 1024), F32),
            pltpu.VMEM((256, 1024), F32),
            pltpu.VMEM((32, 1024), F32),
            pltpu.VMEM((16, 256), F32),
            pltpu.VMEM((16, 128), F32),
        ],
    )(step, own, op, left, right, far)
    (final,) = call(return_kernel, [((16, 16, 256), BF)], (), [pltpu.VMEM((16, 16, 256), F32)])(
        back, exchange(out2, PLANE)
    )
    last = exchange(final, "z")
    (result,) = call(last_kernel, [(trial.shape, F32)], (0,))(
        cheb, last, own, bare, held, own_x
    )
    return result


def solution(mesh):
    split = Mesh(mesh.devices.reshape(16, 4, 2, mesh.shape["vert"]), ("z", "x", "c", "y"))
    in_specs = (
        P(PB, None, "y"),
        P(PB, None),
        P("y", PB, None),
        P(PB, None, "y"),
        P(),
        P(),
        P(PB),
        P(PB),
        P(),
    )
    out_specs = P("y", PB, None)
    return jax.shard_map(body, mesh=split, in_specs=in_specs, out_specs=out_specs, check_vma=False)
```

```python
import jax
import jax.numpy as jnp
from jax import lax
from jax.experimental import pallas as pl
from jax.experimental.pallas import tpu as pltpu
from jax.sharding import Mesh
from jax.sharding import PartitionSpec as P


BF = jnp.bfloat16
F32 = jnp.float32
LAST = (((1,), (1,)), ((), ()))
PB = ("z", "x", "c")
PLANE = ("x", "c")
BLOCK = ("x", "c", "y")
LIMIT = 12 << 20


def exchange(blocks, axis):
    return lax.all_to_all(blocks, axis, 0, 0, tiled=True)


def swap(shard):
    return lax.ppermute(shard, "c", [(0, 1), (1, 0)])


def shift(shard, by):
    count = lax.axis_size("y")
    return lax.ppermute(shard, "y", [(k, (k + by) % count) for k in range(count)])


def stay(array):
    return pltpu.with_memory_space_constraint(array, pltpu.HBM)


def dot(a, b):
    return jnp.dot(a, b, preferred_element_type=F32)


def dot_t(a, b):
    return lax.dot_general(a, b, LAST, preferred_element_type=F32)


def call(kernel, outs, smem, scratch=(), far=(), limit=LIMIT):
    def space(k):
        return pltpu.SMEM if k in smem else pltpu.HBM if k in far else pltpu.VMEM

    def run(*args):
        specs = [pl.BlockSpec(memory_space=space(k)) for k in range(len(args))]
        return pl.pallas_call(
            kernel,
            out_shape=[jax.ShapeDtypeStruct(s, d) for s, d in outs],
            in_specs=specs,
            out_specs=[
                pl.BlockSpec(memory_space=pltpu.SMEM if len(s) == 1 else pltpu.VMEM)
                for s, _ in outs
            ],
            scratch_shapes=list(scratch),
            compiler_params=pltpu.CompilerParams(vmem_limit_bytes=limit),
            cost_estimate=pl.CostEstimate(flops=0, transcendentals=0, bytes_accessed=4 << 20),
        )(*args)

    return run


def lanes(rows, width):
    return lax.broadcasted_iota(jnp.int32, (rows, width), 1)


def products_of(own_ref, s, part):
    val = own_ref[part, s, 0:16, :].astype(F32)
    cond = own_ref[part, s, 16:32, :].astype(F32)
    pieces = [(val[v : v + 1, :] * cond).astype(BF) for v in range(16)]
    return jnp.concatenate(pieces, axis=0)


def density_of(own_ref, rows_bf):
    parts = []
    for part in range(4):
        total = dot(rows_bf[0], products_of(own_ref, 0, part))
        total = total + dot(rows_bf[1], products_of(own_ref, 1, part))
        parts.append(total)
    return parts


def bare_of(own_ref, bare_ref, dens):
    pots = []
    for out in range(4):
        total = jnp.zeros((2, 256), F32)
        for part in range(4):
            total = total + dot_t(
                dens[part].astype(BF),
                bare_ref[out * 256 : (out + 1) * 256, part * 256 : (part + 1) * 256],
            )
        pots.append(total.astype(BF))
    terms = []
    for s in range(2):
        total = jnp.zeros((2, 256), F32)
        for part in range(4):
            total = total + dot_t(pots[part], products_of(own_ref, s, part))
        terms.append(total)
    return terms


def info_kernel(
    pair_hbm, slot_hbm, order_hbm, orb_hbm, trial_hbm, trans_hbm,
    ids_ref, own_ref, held_ref, pair_ref, slot_ref, order_ref, trial_ref, trans_ref, sem,
):
    moves = [
        (pair_hbm, pair_ref), (slot_hbm, slot_ref), (order_hbm, order_ref),
        (trial_hbm, trial_ref), (trans_hbm, trans_ref),
    ] + [(orb_hbm, own_ref.at[part]) for part in range(4)]
    copies = [pltpu.make_async_copy(a, b, sem.at[k]) for k, (a, b) in enumerate(moves)]
    for copy in copies:
        copy.start()
    for copy in copies[:3]:
        copy.wait()
    position = lax.axis_index(PB)
    lane = lanes(1, 256)
    short = lanes(1, 128)
    order = order_ref[...]
    ids = jnp.where(short == 6, position * 2, jnp.where(short == 7, position * 2 + 1, 0))
    kind = lax.rem(lane, 16) // 2
    spread_ids = position * 2 + kind - 6
    for i in range(3):
        first = pair_ref[i]
        second = first - position * 2 - slot_ref[i]
        second = jnp.where(second < 0, second + 256, second)
        for h, k in enumerate((first, second)):
            row = jnp.sum(jnp.where(order == k, lane, 0))
            ids = jnp.where(short == 2 * i + h, row, ids)
            spread_ids = jnp.where(kind == 2 * i + h, row, spread_ids)
        ids = jnp.where(short == 8 + i, slot_ref[i], ids)
    for peer in range(8):
        ids_ref[peer] = ids
    for copy in copies[3:]:
        copy.wait()
    held_ref[...] = jnp.zeros((8, 256), F32)
    for s in range(2):
        held_ref[2 * s : 2 * s + 2, :] = trial_ref[:, s, :]
    held_ref[4:6, :] = trans_ref[...]
    held_ref[6:7, :] = spread_ids.astype(F32)


def pack_kernel(held_ref, own_ref, out_ref, tail_ref):
    out_ref[0:64, :] = own_ref[lax.axis_index("y")].reshape(64, 256)
    rows = [held_ref[2 * s : 2 * s + 2, :].astype(BF) for s in range(2)]
    parts = density_of(own_ref, rows)
    tail_ref[...] = jnp.zeros((16, 256), F32)
    for s in range(2):
        tail_ref[2 * s : 2 * s + 2, :] = rows[s].astype(F32)
    for part in range(4):
        tail_ref[4 + 2 * part : 6 + 2 * part, :] = parts[part]
    tail_ref[12:13, :] = held_ref[6:7, :]
    out_ref[64:80, :] = tail_ref[...].astype(BF)


def select_kernel(plane_ref, gat_ref, twin_ref, out_ref, column_ref, pick_ref):
    lane = lanes(1, 512)
    core = lax.axis_index("c")
    held = jnp.zeros((1, 256), F32)
    for z in range(16):
        row = gat_ref[z, 64:80, :].astype(F32)[12:13, :]
        held = jnp.where(lanes(1, 256) // 16 == z, row, held)
    column_ref[...] = jnp.broadcast_to(held, (8, 256))
    pick_ref[...] = jnp.zeros((128, 512), F32)
    for peer in range(4):
        for e in range(6):
            row = plane_ref[2 * peer + core, 0, e]
            z = row // 16
            s = lax.rem(row, 2)
            ours = lax.rem(row // 2, 2) == core
            first = z * 16 + 2 * s + jnp.where(ours, 0, 256)
            for n in range(2):
                at = peer * 32 + 2 * e + n
                pick_ref[at : at + 1, :] = (lane == first + n).astype(F32)
            at = pl.multiple_of(s * 32, 32)

            @pl.when(ours)
            def _():
                out_ref[peer, 32 * e : 32 * e + 32, :] = gat_ref[z, pl.ds(at, 32), :]

            @pl.when(jnp.logical_not(ours))
            def _():
                out_ref[peer, 32 * e : 32 * e + 32, :] = twin_ref[z, pl.ds(at, 32), :]

        for d in range(8):
            at = peer * 32 + 16 + d
            pick_ref[at : at + 1, :] = (lax.rem(lane, 16) == 4 + d).astype(F32)
    pick = pick_ref[...].astype(BF)
    picked = dot(pick[:, 0:256], gat_ref[:, 64:80, :].reshape(256, 256))
    picked = picked + dot(pick[:, 256:512], twin_ref[:, 64:80, :].reshape(256, 256))
    out_ref[:, 192:224, :] = picked.astype(BF).reshape(4, 32, 256)


def accept_kernel(plane_ref, got_ref, val_ref, cond_ref, dens_ref, tail_ref):
    for e in range(6):
        column = lax.rem(plane_ref[lax.axis_index(PLANE), 0, e] // 4, 4)
        val = got_ref[column, 32 * e : 32 * e + 16, :]
        for part in range(4):
            val_ref[part, 16 * e : 16 * e + 16, :] = val
        cond_ref[e] = got_ref[column, 32 * e + 16 : 32 * e + 32, :]
        part = got_ref[column, 192:208, :].astype(F32)
        tail_ref[2 * e : 2 * e + 2, :] = part[2 * e : 2 * e + 2, :]
    tail_ref[12:16, :] = jnp.zeros((4, 256), F32)
    for part in range(4):
        val_ref[part, 96:112, :] = tail_ref[...].astype(BF)
    total = got_ref[0, 208:224, :].astype(F32)
    for peer in range(1, 4):
        total = total + got_ref[peer, 208:224, :].astype(F32)
    dens_ref[...] = total[0:8, :]


def base_kernel(
    plane_ref, dens_ref, column_ref, own_ref, bare_hbm, held_ref,
    base_ref, route_ref, back_ref, base_s, route_s, bare_ref, sem,
):
    copy = pltpu.make_async_copy(bare_hbm, bare_ref, sem)
    copy.start()
    lane = lanes(1, 256)
    held = column_ref[0:1, :].astype(jnp.int32)
    parity = lax.rem(lane, 2)
    z_me = lax.axis_index("z")
    q_me = lax.axis_index(PLANE)
    for peer in range(8):
        for k in range(8):
            row = plane_ref[peer, 0, k] if k < 6 else z_me * 16 + peer * 2 + (k - 6)
            for n in range(2):
                at = peer * 16 + 2 * k + n
                hit = (held == row) & (parity == n)
                route_s[at : at + 1, :] = jnp.where(hit, -1.0 if k < 6 else 1.0, 0.0)
    route_ref[...] = jnp.transpose(route_s[...]).astype(BF)

    wide = lanes(1, 128)
    sent = jnp.full((1, 128), -1, jnp.int32)
    for peer in range(8):
        for e in range(6):
            here = (wide // 16 == peer) & (lax.rem(wide, 16) // 2 == e)
            sent = jnp.where(here, plane_ref[peer, 0, e], sent)
    row = lax.broadcasted_iota(jnp.int32, (64, 128), 0)
    target = (row // 4) * 16 + q_me * 2 + lax.rem(row, 4) // 2
    hit = (sent == target) & (lax.rem(row, 2) == lax.rem(lanes(64, 128), 2))
    back_ref[...] = jnp.where(hit, -1.0, 0.0).astype(BF)

    copy.wait()
    dens = [dens_ref[2 * part : 2 * part + 2, :] for part in range(4)]
    terms = bare_of(own_ref, bare_ref, dens)
    for s in range(2):
        x = held_ref[2 * s : 2 * s + 2, :].astype(BF).astype(F32)
        base_s[2 * s : 2 * s + 2, :] = held_ref[4 + s : 5 + s, :] * x + 2.0 * terms[s]
    base_ref[...] = base_s[...]


def spread(x):
    rows = jnp.concatenate([x] * 16, axis=0)
    group = lax.broadcasted_iota(jnp.int32, (128, 256), 0) // 8
    return jnp.where(group == lanes(128, 256) // 16, rows, 0.0).astype(BF)


def gathered(full):
    group = lax.broadcasted_iota(jnp.int32, (128, 256), 0) // 8
    kept = jnp.where(group == lanes(128, 256) // 16, full, 0.0)
    total = kept[0:8, :]
    for v in range(1, 16):
        total = total + kept[8 * v : 8 * v + 8, :]
    return total


def apply_pair(i, half_ref, cond_ref, xs_ref, ys_ref, t_ref, u_ref):
    tile_a = jnp.concatenate([cond_ref[2 * i]] * 16, axis=0)
    tile_c = jnp.concatenate([cond_ref[2 * i + 1]] * 16, axis=0)
    t_ref[0] = dot(spread(xs_ref[2 * i]), tile_a)
    t_ref[1] = dot(spread(xs_ref[2 * i + 1]), tile_c)
    for part in range(2):
        at = slice(128 * part, 128 * part + 128)
        t_c = [t_ref[1, 8 * w : 8 * w + 8, at] for w in range(16)]
        u_c = [None] * 16
        for v in range(16):
            t_a = t_ref[0, 8 * v : 8 * v + 8, at]
            sums = [None] * 2
            for w in range(16):
                row = 16 * v + w
                h = jnp.broadcast_to(half_ref[2 * i + part, row : row + 1, :], (8, 128))
                one, two = h * t_c[w], h * t_a
                sums[w % 2] = one if w < 2 else sums[w % 2] + one
                u_c[w] = two if v == 0 else u_c[w] + two
            u_ref[0, 8 * v : 8 * v + 8, at] = sums[0] + sums[1]
        for w in range(16):
            u_ref[1, 8 * w : 8 * w + 8, at] = u_c[w]
    ys_ref[2 * i] = gathered(dot_t(u_ref[0].astype(BF), tile_a))
    ys_ref[2 * i + 1] = gathered(dot_t(u_ref[1].astype(BF), tile_c))


def first_kernel(
    plane_ref, wide_ref, cond_ref, scr_hbm, base_ref, op_ref, res_ref,
    xs_ref, ys_ref, t_ref, u_ref, rs_ref, half_ref, scr_ref, sem,
):
    copy = pltpu.make_async_copy(scr_hbm, scr_ref, sem)
    copy.start()
    for e in range(6):
        op_ref[0, 768 + 16 * e : 784 + 16 * e, :] = cond_ref[e, :, 0:128]
        op_ref[1, 768 + 16 * e : 784 + 16 * e, :] = cond_ref[e, :, 128:256]
    for part in range(4):
        tail = wide_ref[part, 96:112, :].astype(F32)
        for e in range(6):
            xs_ref[e, 2 * part : 2 * part + 2, :] = tail[2 * e : 2 * e + 2, :]

    copy.wait()

    def one(i, carry):
        slot = plane_ref[lax.axis_index(PLANE), 0, 8 + i]
        total = jnp.zeros((256, 256), F32)
        for part in range(4):
            at = pl.multiple_of(i * 32, 16)
            a = wide_ref[part, pl.ds(at, 16), :].astype(F32)
            b = wide_ref[part, pl.ds(at + 16, 16), :].astype(F32)
            left = jnp.concatenate(
                [(a[v : v + 1, :] * b).astype(BF) for v in range(16)], axis=0
            )
            total = total + dot(left, scr_ref[slot, part * 256 : (part + 1) * 256, :])
        total = total.astype(BF)
        at = pl.multiple_of(i * 256, 256)
        op_ref[0, pl.ds(at, 256), :] = total[:, 0:128]
        op_ref[1, pl.ds(at, 256), :] = total[:, 128:256]
        total = total.astype(F32)
        half_ref[2 * i] = total[:, 0:128]
        half_ref[2 * i + 1] = total[:, 128:256]
        apply_pair(i, half_ref, cond_ref, xs_ref, ys_ref, t_ref, u_ref)
        return carry

    lax.fori_loop(0, 3, one, 0)
    for part in range(4):
        for e in range(6):
            rs_ref[part, 2 * e : 2 * e + 2, :] = ys_ref[e, 2 * part : 2 * part + 2, :]
        mine = (lax.axis_index("y") == part).astype(F32)
        rs_ref[part, 12:16, :] = base_ref[...] * mine
    for peer in range(8):
        for part in range(4):
            res_ref[4 * peer + part] = rs_ref[part].astype(BF)


def middle_kernel(route_ref, got_ref, out_ref):
    peers = []
    for peer in range(8):
        total = got_ref[4 * peer].astype(F32)
        for part in range(1, 4):
            total = total + got_ref[4 * peer + part].astype(F32)
        peers.append(total.astype(BF))
    full = dot(route_ref[...], jnp.concatenate(peers, axis=0))
    out_ref[...] = full.astype(BF).reshape(16, 16, 256)


def picker(rows, columns):
    row = lax.broadcasted_iota(jnp.int32, (rows, columns), 0)
    return (lax.rem(row, 16) == lax.rem(lanes(rows, columns), 16)).astype(BF)


def second_kernel(
    got_ref, own_ref, op_ref, left_ref, right_ref, far_ref, out_ref, own_x_ref,
    x_ref, y_ref, t_ref, ua_ref, uc_ref, rs_ref, ds_ref,
):
    total = got_ref[0].astype(F32)
    for z in range(1, 16):
        total = total + got_ref[z].astype(F32)
    own_x_ref[...] = total[12:16, :]
    parts = density_of(own_ref, [total[12 + 2 * s : 14 + 2 * s, :].astype(BF) for s in range(2)])
    for part in range(4):
        for h in range(2):
            at = 4 * part + 2 * h
            ds_ref[at : at + 2, :] = parts[part][:, 128 * h : 128 * h + 128]

    here = lanes(16, 256) // 16 == lax.broadcasted_iota(jnp.int32, (16, 256), 0)
    rows = [jnp.where(here, total[k : k + 1, :], 0.0).astype(BF) for k in range(12)]
    x_ref[...] = dot(jnp.concatenate(rows, axis=0), picker(256, 16)).astype(BF)

    chunks = [(ref, h) for ref in (op_ref, left_ref, right_ref, far_ref) for h in range(2)]

    def one(p, carry):
        at = pl.multiple_of(p * 64, 64)
        conds = []
        for end in range(2):
            row = pl.multiple_of(768 + p * 32 + end * 16, 16)
            conds.append(
                jnp.concatenate([ref[h, pl.ds(row, 16), :] for ref, h in chunks], axis=1)
            )
            t_ref[end] = dot(x_ref[pl.ds(pl.multiple_of(at + 32 * end, 32), 32), :], conds[end])
        for k, (ref, h) in enumerate(chunks):
            span = slice(128 * k, 128 * k + 128)
            t_c = [t_ref[1, 8 * g : 8 * g + 8, span] for g in range(4)]
            sums = [None] * 4
            for v in range(16):
                tile = ref[h, pl.ds(pl.multiple_of(p * 256 + 16 * v, 16), 16), :].astype(F32)
                lo, hi = tile[0:8, :], tile[8:16, :]
                for n in range(2):
                    ua_ref[128 * n + 8 * v : 128 * n + 8 * v + 8, span] = (
                        lo * t_c[2 * n] + hi * t_c[2 * n + 1]
                    )
                    t_a = jnp.broadcast_to(
                        t_ref[0, 16 * n + v : 16 * n + v + 1, span], (8, 128)
                    )
                    for g, part in ((2 * n, lo * t_a), (2 * n + 1, hi * t_a)):
                        sums[g] = part if v == 0 else sums[g] + part
            for g in range(4):
                uc_ref[8 * g : 8 * g + 8, span] = sums[g]
        first = dot_t(ua_ref[...].astype(BF), conds[0])
        y_ref[pl.ds(at, 32), :] = jnp.sum(first.reshape(32, 8, 16), axis=1)
        y_ref[pl.ds(pl.multiple_of(at + 32, 32), 32), :] = dot_t(uc_ref[...].astype(BF), conds[1])
        return carry

    lax.fori_loop(0, 3, one, 0)
    full = dot(y_ref[...].astype(BF), picker(16, 256)).reshape(12, 16, 256)
    rs_ref[0:12, :] = jnp.sum(jnp.where(here[None], full, 0.0), axis=1)
    rs_ref[12:16, :] = jnp.zeros((4, 256), F32)
    for peer in range(8):
        out_ref[peer, :, 0:256] = rs_ref[...].astype(BF)
        out_ref[peer, :, 256:384] = ds_ref[...].astype(BF)


def return_kernel(back_ref, got_ref, out_ref, buf_ref):
    full = dot(back_ref[...], got_ref[:, :, 0:256].reshape(128, 256))
    total = got_ref[0, :, 256:384].astype(F32)
    for peer in range(1, 8):
        total = total + got_ref[peer, :, 256:384].astype(F32)
    for part in range(4):
        for h in range(2):
            at = 4 * part + 2 * h
            span = slice(128 * h, 128 * h + 128)
            buf_ref[0, 2 * part : 2 * part + 2, span] = total[at : at + 2, :]
    for z in range(16):
        if z:
            buf_ref[z, :, 0:256] = buf_ref[0, :, 0:256]
        for h in range(2):
            span = slice(128 * h, 128 * h + 128)
            buf_ref[z, 4 * h : 4 * h + 4, 256:384] = full[4 * z : 4 * z + 4, span]
    out_ref[...] = buf_ref[...].astype(BF)


def last_kernel(
    cheb_ref, got_ref, own_ref, bare_hbm, held_ref, own_x_ref, out_ref, bare_ref, sem
):
    copy = pltpu.make_async_copy(bare_hbm, bare_ref, sem)
    copy.start()
    total = got_ref[0].astype(F32)
    for z in range(1, 16):
        total = total + got_ref[z].astype(F32)
    dens = [total[2 * part : 2 * part + 2, 0:256] for part in range(4)]
    rows = jnp.concatenate([total[0:4, 256:384], total[4:8, 256:384]], axis=1)
    copy.wait()
    terms = bare_of(own_ref, bare_ref, dens)
    for s in range(2):
        x = own_x_ref[2 * s : 2 * s + 2, :]
        t = held_ref[2 * s : 2 * s + 2, :]
        applied = (
            held_ref[4 + s : 5 + s, :] * x.astype(BF).astype(F32)
            + 2.0 * terms[s]
            + rows[2 * s : 2 * s + 2, :]
        )
        second = 2.0 * applied - t
        out_ref[:, s, :] = cheb_ref[0] * t + cheb_ref[1] * x + cheb_ref[2] * second


def body(orbitals, transition, trial, screened, bare, cheb, pair_k, pair_slot, k_order):
    ids, copies, held = call(
        info_kernel,
        [((8, 1, 128), jnp.int32), ((4, 2, 32, 256), BF), ((8, 256), F32)],
        (),
        [
            pltpu.SMEM((3,), jnp.int32),
            pltpu.SMEM((3,), jnp.int32),
            pltpu.VMEM((1, 256), jnp.int32),
            pltpu.VMEM((2, 2, 256), F32),
            pltpu.VMEM((2, 256), F32),
            pltpu.SemaphoreType.DMA((9,)),
        ],
        range(6),
    )(*map(stay, (pair_k, pair_slot, k_order.reshape(1, -1), orbitals, trial, transition)))
    far_bare = stay(bare)
    own = exchange(copies, "y")
    plane = exchange(ids, PLANE)
    (packed,) = call(pack_kernel, [((80, 256), BF)], (), [pltpu.VMEM((16, 256), F32)])(held, own)
    gat = lax.all_gather(packed, "z")
    chosen, column = call(
        select_kernel,
        [((4, 224, 256), BF), ((8, 256), F32)],
        (0,),
        [pltpu.VMEM((128, 512), F32)],
    )(plane, gat, swap(gat))
    got = exchange(chosen, "x")
    val, cond, dens = call(
        accept_kernel,
        [((4, 112, 256), BF), ((6, 16, 256), BF), ((8, 256), F32)],
        (0,),
        [pltpu.VMEM((16, 256), F32)],
    )(plane, got)
    wide = exchange(val, "y")
    base, route, back = call(
        base_kernel,
        [((4, 256), F32), ((256, 128), BF), ((64, 128), BF)],
        (0,),
        [
            pltpu.VMEM((4, 256), F32),
            pltpu.VMEM((128, 256), F32),
            pltpu.VMEM(bare.shape, BF),
            pltpu.SemaphoreType.DMA(()),
        ],
        (4,),
    )(plane, dens, column, own, far_bare, held)
    work = [
        pltpu.VMEM((6, 8, 256), F32),
        pltpu.VMEM((6, 8, 256), F32),
        pltpu.VMEM((2, 128, 256), F32),
        pltpu.VMEM((2, 128, 256), F32),
        pltpu.VMEM((4, 16, 256), F32),
    ]
    op, res = call(
        first_kernel,
        [((2, 864, 128), BF), ((32, 16, 256), BF)],
        (0,),
        work
        + [
            pltpu.VMEM((6, 256, 128), F32),
            pltpu.VMEM(screened.shape, BF),
            pltpu.SemaphoreType.DMA(()),
        ],
        (3,),
    )(plane, wide, cond, stay(screened), base)
    mixed = exchange(res, BLOCK)
    left = shift(op, 1)
    right = shift(op, -1)
    (middle,) = call(middle_kernel, [((16, 16, 256), BF)], ())(route, mixed)
    step = exchange(middle, "z")
    far = shift(left, 1)
    out2, own_x = call(
        second_kernel,
        [((8, 16, 384), BF), ((4, 256), F32)],
        (),
        [
            pltpu.VMEM((192, 16), BF),
            pltpu.VMEM((192, 16), F32),
            pltpu.VMEM((2, 32, 1024), F32),
            pltpu.VMEM((256, 1024), F32),
            pltpu.VMEM((32, 1024), F32),
            pltpu.VMEM((16, 256), F32),
            pltpu.VMEM((16, 128), F32),
        ],
    )(step, own, op, left, right, far)
    (final,) = call(return_kernel, [((16, 8, 384), BF)], (), [pltpu.VMEM((16, 8, 384), F32)])(
        back, exchange(out2, PLANE)
    )
    last = exchange(final, "z")
    (result,) = call(
        last_kernel,
        [(trial.shape, F32)],
        (0,),
        [pltpu.VMEM(bare.shape, BF), pltpu.SemaphoreType.DMA(())],
        (3,),
    )(
        cheb, last, own, far_bare, held, own_x
    )
    return result


def solution(mesh):
    split = Mesh(mesh.devices.reshape(16, 4, 2, mesh.shape["vert"]), ("z", "x", "c", "y"))
    in_specs = (
        P(PB, None, "y"),
        P(PB, None),
        P("y", PB, None),
        P(PB, None, "y"),
        P(),
        P(),
        P(PB),
        P(PB),
        P(),
    )
    out_specs = P("y", PB, None)
    return jax.shard_map(body, mesh=split, in_specs=in_specs, out_specs=out_specs, check_vma=False)
```

```python
import jax
import jax.numpy as jnp
from jax import lax
from jax.experimental import pallas as pl
from jax.experimental.pallas import tpu as pltpu
from jax.sharding import Mesh
from jax.sharding import PartitionSpec as P


BF = jnp.bfloat16
F32 = jnp.float32
LAST = (((1,), (1,)), ((), ()))
PB = ("z", "x", "c")
PLANE = ("x", "c")
BLOCK = ("x", "c", "y")
LIMIT = 12 << 20


def exchange(blocks, axis):
    return lax.all_to_all(blocks, axis, 0, 0, tiled=True)


def swap(shard):
    return lax.ppermute(shard, "c", [(0, 1), (1, 0)])


def shift(shard, by):
    count = lax.axis_size("y")
    return lax.ppermute(shard, "y", [(k, (k + by) % count) for k in range(count)])


def stay(array):
    return pltpu.with_memory_space_constraint(array, pltpu.HBM)


def dot(a, b):
    return jnp.dot(a, b, preferred_element_type=F32)


def dot_t(a, b):
    return lax.dot_general(a, b, LAST, preferred_element_type=F32)


def call(kernel, outs, smem, scratch=(), far=(), limit=LIMIT):
    def space(k):
        return pltpu.SMEM if k in smem else pltpu.HBM if k in far else pltpu.VMEM

    def run(*args):
        specs = [pl.BlockSpec(memory_space=space(k)) for k in range(len(args))]
        return pl.pallas_call(
            kernel,
            out_shape=[jax.ShapeDtypeStruct(s, d) for s, d in outs],
            in_specs=specs,
            out_specs=[
                pl.BlockSpec(memory_space=pltpu.SMEM if len(s) == 1 else pltpu.VMEM)
                for s, _ in outs
            ],
            scratch_shapes=list(scratch),
            compiler_params=pltpu.CompilerParams(vmem_limit_bytes=limit),
            cost_estimate=pl.CostEstimate(flops=0, transcendentals=0, bytes_accessed=4 << 20),
        )(*args)

    return run


def lanes(rows, width):
    return lax.broadcasted_iota(jnp.int32, (rows, width), 1)


def products_of(own_ref, s, part):
    val = own_ref[part, s, 0:16, :].astype(F32)
    cond = own_ref[part, s, 16:32, :].astype(F32)
    pieces = [(val[v : v + 1, :] * cond).astype(BF) for v in range(16)]
    return jnp.concatenate(pieces, axis=0)


def density_of(own_ref, rows_bf):
    parts = []
    for part in range(4):
        total = dot(rows_bf[0], products_of(own_ref, 0, part))
        total = total + dot(rows_bf[1], products_of(own_ref, 1, part))
        parts.append(total)
    return parts


def bare_of(own_ref, bare_ref, dens):
    pots = []
    for out in range(4):
        total = jnp.zeros((2, 256), F32)
        for part in range(4):
            total = total + dot_t(
                dens[part].astype(BF),
                bare_ref[out * 256 : (out + 1) * 256, part * 256 : (part + 1) * 256],
            )
        pots.append(total.astype(BF))
    terms = []
    for s in range(2):
        total = jnp.zeros((2, 256), F32)
        for part in range(4):
            total = total + dot_t(pots[part], products_of(own_ref, s, part))
        terms.append(total)
    return terms


def info_kernel(
    pair_hbm, slot_hbm, order_hbm, orb_hbm, trial_hbm, trans_hbm,
    ids_ref, own_ref, held_ref, pair_ref, slot_ref, order_ref, trial_ref, trans_ref, sem,
):
    moves = [
        (pair_hbm, pair_ref), (slot_hbm, slot_ref), (order_hbm, order_ref),
        (trial_hbm, trial_ref), (trans_hbm, trans_ref),
    ] + [(orb_hbm, own_ref.at[part]) for part in range(4)]
    copies = [pltpu.make_async_copy(a, b, sem.at[k]) for k, (a, b) in enumerate(moves)]
    for copy in copies:
        copy.start()
    for copy in copies[:3]:
        copy.wait()
    position = lax.axis_index(PB)
    lane = lanes(1, 256)
    short = lanes(1, 128)
    order = order_ref[...]
    ids = jnp.where(short == 6, position * 2, jnp.where(short == 7, position * 2 + 1, 0))
    kind = lax.rem(lane, 16) // 2
    spread_ids = position * 2 + kind - 6
    for i in range(3):
        first = pair_ref[i]
        second = first - position * 2 - slot_ref[i]
        second = jnp.where(second < 0, second + 256, second)
        for h, k in enumerate((first, second)):
            row = jnp.sum(jnp.where(order == k, lane, 0))
            ids = jnp.where(short == 2 * i + h, row, ids)
            spread_ids = jnp.where(kind == 2 * i + h, row, spread_ids)
        ids = jnp.where(short == 8 + i, slot_ref[i], ids)
    for peer in range(8):
        ids_ref[peer] = ids
    for copy in copies[3:]:
        copy.wait()
    held_ref[...] = jnp.zeros((8, 256), F32)
    for s in range(2):
        held_ref[2 * s : 2 * s + 2, :] = trial_ref[:, s, :]
    held_ref[4:6, :] = trans_ref[...]
    held_ref[6:7, :] = spread_ids.astype(F32)


def pack_kernel(held_ref, own_ref, out_ref, tail_ref):
    out_ref[0:64, :] = own_ref[lax.axis_index("y")].reshape(64, 256)
    rows = [held_ref[2 * s : 2 * s + 2, :].astype(BF) for s in range(2)]
    parts = density_of(own_ref, rows)
    tail_ref[...] = jnp.zeros((16, 256), F32)
    for s in range(2):
        tail_ref[2 * s : 2 * s + 2, :] = rows[s].astype(F32)
    for part in range(4):
        tail_ref[4 + 2 * part : 6 + 2 * part, :] = parts[part]
    tail_ref[12:13, :] = held_ref[6:7, :]
    out_ref[64:80, :] = tail_ref[...].astype(BF)


def select_kernel(plane_ref, gat_ref, twin_ref, out_ref, column_ref, pick_ref):
    lane = lanes(1, 512)
    core = lax.axis_index("c")
    held = jnp.zeros((1, 256), F32)
    for z in range(16):
        row = gat_ref[z, 64:80, :].astype(F32)[12:13, :]
        held = jnp.where(lanes(1, 256) // 16 == z, row, held)
    column_ref[...] = jnp.broadcast_to(held, (8, 256))
    pick_ref[...] = jnp.zeros((128, 512), F32)
    for peer in range(4):
        for e in range(6):
            row = plane_ref[2 * peer + core, 0, e]
            z = row // 16
            s = lax.rem(row, 2)
            ours = lax.rem(row // 2, 2) == core
            first = z * 16 + 2 * s + jnp.where(ours, 0, 256)
            for n in range(2):
                at = peer * 32 + 2 * e + n
                pick_ref[at : at + 1, :] = (lane == first + n).astype(F32)
            at = pl.multiple_of(s * 32, 32)

            @pl.when(ours)
            def _():
                out_ref[peer, 32 * e : 32 * e + 32, :] = gat_ref[z, pl.ds(at, 32), :]

            @pl.when(jnp.logical_not(ours))
            def _():
                out_ref[peer, 32 * e : 32 * e + 32, :] = twin_ref[z, pl.ds(at, 32), :]

        for d in range(8):
            at = peer * 32 + 16 + d
            pick_ref[at : at + 1, :] = (lax.rem(lane, 16) == 4 + d).astype(F32)
    pick = pick_ref[...].astype(BF)
    picked = dot(pick[:, 0:256], gat_ref[:, 64:80, :].reshape(256, 256))
    picked = picked + dot(pick[:, 256:512], twin_ref[:, 64:80, :].reshape(256, 256))
    out_ref[:, 192:224, :] = picked.astype(BF).reshape(4, 32, 256)


def fetch_kernel(far_ref, near_ref, sem):
    copy = pltpu.make_async_copy(far_ref, near_ref, sem)
    copy.start()
    copy.wait()


def accept_kernel(plane_ref, got_ref, val_ref, cond_ref, dens_ref, tail_ref):
    for e in range(6):
        column = lax.rem(plane_ref[lax.axis_index(PLANE), 0, e] // 4, 4)
        val = got_ref[column, 32 * e : 32 * e + 16, :]
        for part in range(4):
            val_ref[part, 16 * e : 16 * e + 16, :] = val
        cond_ref[e] = got_ref[column, 32 * e + 16 : 32 * e + 32, :]
        part = got_ref[column, 192:208, :].astype(F32)
        tail_ref[2 * e : 2 * e + 2, :] = part[2 * e : 2 * e + 2, :]
    tail_ref[12:16, :] = jnp.zeros((4, 256), F32)
    for part in range(4):
        val_ref[part, 96:112, :] = tail_ref[...].astype(BF)
    total = got_ref[0, 208:224, :].astype(F32)
    for peer in range(1, 4):
        total = total + got_ref[peer, 208:224, :].astype(F32)
    dens_ref[...] = total[0:8, :]


def base_kernel(
    plane_ref, dens_ref, column_ref, own_ref, bare_hbm, held_ref,
    base_ref, route_ref, back_ref, base_s, route_s, bare_ref, sem,
):
    copy = pltpu.make_async_copy(bare_hbm, bare_ref, sem)
    copy.start()
    lane = lanes(1, 256)
    held = column_ref[0:1, :].astype(jnp.int32)
    parity = lax.rem(lane, 2)
    z_me = lax.axis_index("z")
    q_me = lax.axis_index(PLANE)
    for peer in range(8):
        for k in range(8):
            row = plane_ref[peer, 0, k] if k < 6 else z_me * 16 + peer * 2 + (k - 6)
            for n in range(2):
                at = peer * 16 + 2 * k + n
                hit = (held == row) & (parity == n)
                route_s[at : at + 1, :] = jnp.where(hit, -1.0 if k < 6 else 1.0, 0.0)
    route_ref[...] = jnp.transpose(route_s[...]).astype(BF)

    wide = lanes(1, 128)
    sent = jnp.full((1, 128), -1, jnp.int32)
    for peer in range(8):
        for e in range(6):
            here = (wide // 16 == peer) & (lax.rem(wide, 16) // 2 == e)
            sent = jnp.where(here, plane_ref[peer, 0, e], sent)
    row = lax.broadcasted_iota(jnp.int32, (64, 128), 0)
    target = (row // 4) * 16 + q_me * 2 + lax.rem(row, 4) // 2
    hit = (sent == target) & (lax.rem(row, 2) == lax.rem(lanes(64, 128), 2))
    back_ref[...] = jnp.where(hit, -1.0, 0.0).astype(BF)

    copy.wait()
    dens = [dens_ref[2 * part : 2 * part + 2, :] for part in range(4)]
    terms = bare_of(own_ref, bare_ref, dens)
    for s in range(2):
        x = held_ref[2 * s : 2 * s + 2, :].astype(BF).astype(F32)
        base_s[2 * s : 2 * s + 2, :] = held_ref[4 + s : 5 + s, :] * x + 2.0 * terms[s]
    base_ref[...] = base_s[...]


def spread(x):
    rows = jnp.concatenate([x] * 16, axis=0)
    group = lax.broadcasted_iota(jnp.int32, (128, 256), 0) // 8
    return jnp.where(group == lanes(128, 256) // 16, rows, 0.0).astype(BF)


def gathered(full):
    group = lax.broadcasted_iota(jnp.int32, (128, 256), 0) // 8
    kept = jnp.where(group == lanes(128, 256) // 16, full, 0.0)
    total = kept[0:8, :]
    for v in range(1, 16):
        total = total + kept[8 * v : 8 * v + 8, :]
    return total


def apply_pair(i, half_ref, cond_ref, xs_ref, ys_ref, t_ref, u_ref):
    tile_a = jnp.concatenate([cond_ref[2 * i]] * 16, axis=0)
    tile_c = jnp.concatenate([cond_ref[2 * i + 1]] * 16, axis=0)
    t_ref[0] = dot(spread(xs_ref[2 * i]), tile_a)
    t_ref[1] = dot(spread(xs_ref[2 * i + 1]), tile_c)
    for part in range(2):
        at = slice(128 * part, 128 * part + 128)
        t_c = [t_ref[1, 8 * w : 8 * w + 8, at] for w in range(16)]
        u_c = [None] * 16
        for v in range(16):
            t_a = t_ref[0, 8 * v : 8 * v + 8, at]
            sums = [None] * 2
            for w in range(16):
                row = 16 * v + w
                h = jnp.broadcast_to(half_ref[2 * i + part, row : row + 1, :], (8, 128))
                one, two = h * t_c[w], h * t_a
                sums[w % 2] = one if w < 2 else sums[w % 2] + one
                u_c[w] = two if v == 0 else u_c[w] + two
            u_ref[0, 8 * v : 8 * v + 8, at] = sums[0] + sums[1]
        for w in range(16):
            u_ref[1, 8 * w : 8 * w + 8, at] = u_c[w]
    ys_ref[2 * i] = gathered(dot_t(u_ref[0].astype(BF), tile_a))
    ys_ref[2 * i + 1] = gathered(dot_t(u_ref[1].astype(BF), tile_c))


def first_kernel(
    plane_ref, wide_ref, cond_ref, scr_ref, base_ref, op_ref, res_ref,
    xs_ref, ys_ref, t_ref, u_ref, rs_ref, half_ref,
):
    for e in range(6):
        op_ref[0, 768 + 16 * e : 784 + 16 * e, :] = cond_ref[e, :, 0:128]
        op_ref[1, 768 + 16 * e : 784 + 16 * e, :] = cond_ref[e, :, 128:256]
    for part in range(4):
        tail = wide_ref[part, 96:112, :].astype(F32)
        for e in range(6):
            xs_ref[e, 2 * part : 2 * part + 2, :] = tail[2 * e : 2 * e + 2, :]

    def one(i, carry):
        slot = plane_ref[lax.axis_index(PLANE), 0, 8 + i]
        total = jnp.zeros((256, 256), F32)
        for part in range(4):
            at = pl.multiple_of(i * 32, 16)
            a = wide_ref[part, pl.ds(at, 16), :].astype(F32)
            b = wide_ref[part, pl.ds(at + 16, 16), :].astype(F32)
            left = jnp.concatenate(
                [(a[v : v + 1, :] * b).astype(BF) for v in range(16)], axis=0
            )
            total = total + dot(left, scr_ref[slot, part * 256 : (part + 1) * 256, :])
        total = total.astype(BF)
        at = pl.multiple_of(i * 256, 256)
        op_ref[0, pl.ds(at, 256), :] = total[:, 0:128]
        op_ref[1, pl.ds(at, 256), :] = total[:, 128:256]
        total = total.astype(F32)
        half_ref[2 * i] = total[:, 0:128]
        half_ref[2 * i + 1] = total[:, 128:256]
        apply_pair(i, half_ref, cond_ref, xs_ref, ys_ref, t_ref, u_ref)
        return carry

    lax.fori_loop(0, 3, one, 0)
    for part in range(4):
        for e in range(6):
            rs_ref[part, 2 * e : 2 * e + 2, :] = ys_ref[e, 2 * part : 2 * part + 2, :]
        mine = (lax.axis_index("y") == part).astype(F32)
        rs_ref[part, 12:16, :] = base_ref[...] * mine
    for peer in range(8):
        for part in range(4):
            res_ref[4 * peer + part] = rs_ref[part].astype(BF)


def middle_kernel(route_ref, got_ref, out_ref):
    peers = []
    for peer in range(8):
        total = got_ref[4 * peer].astype(F32)
        for part in range(1, 4):
            total = total + got_ref[4 * peer + part].astype(F32)
        peers.append(total.astype(BF))
    full = dot(route_ref[...], jnp.concatenate(peers, axis=0))
    out_ref[...] = full.astype(BF).reshape(16, 16, 256)


def picker(rows, columns):
    row = lax.broadcasted_iota(jnp.int32, (rows, columns), 0)
    return (lax.rem(row, 16) == lax.rem(lanes(rows, columns), 16)).astype(BF)


def second_kernel(
    got_ref, own_ref, op_ref, left_ref, right_ref, far_ref, out_ref, own_x_ref,
    x_ref, y_ref, t_ref, ua_ref, uc_ref, rs_ref, ds_ref,
):
    total = got_ref[0].astype(F32)
    for z in range(1, 16):
        total = total + got_ref[z].astype(F32)
    own_x_ref[...] = total[12:16, :]
    parts = density_of(own_ref, [total[12 + 2 * s : 14 + 2 * s, :].astype(BF) for s in range(2)])
    for part in range(4):
        for h in range(2):
            at = 4 * part + 2 * h
            ds_ref[at : at + 2, :] = parts[part][:, 128 * h : 128 * h + 128]

    here = lanes(16, 256) // 16 == lax.broadcasted_iota(jnp.int32, (16, 256), 0)
    rows = [jnp.where(here, total[k : k + 1, :], 0.0).astype(BF) for k in range(12)]
    x_ref[...] = dot(jnp.concatenate(rows, axis=0), picker(256, 16)).astype(BF)

    chunks = [(ref, h) for ref in (op_ref, left_ref, right_ref, far_ref) for h in range(2)]

    def one(p, carry):
        at = pl.multiple_of(p * 64, 64)
        conds = []
        for end in range(2):
            row = pl.multiple_of(768 + p * 32 + end * 16, 16)
            conds.append(
                jnp.concatenate([ref[h, pl.ds(row, 16), :] for ref, h in chunks], axis=1)
            )
            t_ref[end] = dot(x_ref[pl.ds(pl.multiple_of(at + 32 * end, 32), 32), :], conds[end])
        for k, (ref, h) in enumerate(chunks):
            span = slice(128 * k, 128 * k + 128)
            t_c = [t_ref[1, 8 * g : 8 * g + 8, span] for g in range(4)]
            sums = [None] * 4
            for v in range(16):
                tile = ref[h, pl.ds(pl.multiple_of(p * 256 + 16 * v, 16), 16), :].astype(F32)
                lo, hi = tile[0:8, :], tile[8:16, :]
                for n in range(2):
                    ua_ref[128 * n + 8 * v : 128 * n + 8 * v + 8, span] = (
                        lo * t_c[2 * n] + hi * t_c[2 * n + 1]
                    )
                    t_a = jnp.broadcast_to(
                        t_ref[0, 16 * n + v : 16 * n + v + 1, span], (8, 128)
                    )
                    for g, part in ((2 * n, lo * t_a), (2 * n + 1, hi * t_a)):
                        sums[g] = part if v == 0 else sums[g] + part
            for g in range(4):
                uc_ref[8 * g : 8 * g + 8, span] = sums[g]
        first = dot_t(ua_ref[...].astype(BF), conds[0])
        y_ref[pl.ds(at, 32), :] = jnp.sum(first.reshape(32, 8, 16), axis=1)
        y_ref[pl.ds(pl.multiple_of(at + 32, 32), 32), :] = dot_t(uc_ref[...].astype(BF), conds[1])
        return carry

    lax.fori_loop(0, 3, one, 0)
    full = dot(y_ref[...].astype(BF), picker(16, 256)).reshape(12, 16, 256)
    rs_ref[0:12, :] = jnp.sum(jnp.where(here[None], full, 0.0), axis=1)
    rs_ref[12:16, :] = jnp.zeros((4, 256), F32)
    for peer in range(8):
        out_ref[peer, :, 0:256] = rs_ref[...].astype(BF)
        out_ref[peer, :, 256:384] = ds_ref[...].astype(BF)


def return_kernel(back_ref, got_ref, out_ref, buf_ref):
    full = dot(back_ref[...], got_ref[:, :, 0:256].reshape(128, 256))
    total = got_ref[0, :, 256:384].astype(F32)
    for peer in range(1, 8):
        total = total + got_ref[peer, :, 256:384].astype(F32)
    for part in range(4):
        for h in range(2):
            at = 4 * part + 2 * h
            span = slice(128 * h, 128 * h + 128)
            buf_ref[0, 2 * part : 2 * part + 2, span] = total[at : at + 2, :]
    for z in range(16):
        if z:
            buf_ref[z, :, 0:256] = buf_ref[0, :, 0:256]
        for h in range(2):
            span = slice(128 * h, 128 * h + 128)
            buf_ref[z, 4 * h : 4 * h + 4, 256:384] = full[4 * z : 4 * z + 4, span]
    out_ref[...] = buf_ref[...].astype(BF)


def last_kernel(cheb_ref, got_ref, own_ref, bare_ref, held_ref, own_x_ref, out_ref):
    total = got_ref[0].astype(F32)
    for z in range(1, 16):
        total = total + got_ref[z].astype(F32)
    dens = [total[2 * part : 2 * part + 2, 0:256] for part in range(4)]
    rows = jnp.concatenate([total[0:4, 256:384], total[4:8, 256:384]], axis=1)
    terms = bare_of(own_ref, bare_ref, dens)
    for s in range(2):
        x = own_x_ref[2 * s : 2 * s + 2, :]
        t = held_ref[2 * s : 2 * s + 2, :]
        applied = (
            held_ref[4 + s : 5 + s, :] * x.astype(BF).astype(F32)
            + 2.0 * terms[s]
            + rows[2 * s : 2 * s + 2, :]
        )
        second = 2.0 * applied - t
        out_ref[:, s, :] = cheb_ref[0] * t + cheb_ref[1] * x + cheb_ref[2] * second


def body(orbitals, transition, trial, screened, bare, cheb, pair_k, pair_slot, k_order):
    ids, copies, held = call(
        info_kernel,
        [((8, 1, 128), jnp.int32), ((4, 2, 32, 256), BF), ((8, 256), F32)],
        (),
        [
            pltpu.SMEM((3,), jnp.int32),
            pltpu.SMEM((3,), jnp.int32),
            pltpu.VMEM((1, 256), jnp.int32),
            pltpu.VMEM((2, 2, 256), F32),
            pltpu.VMEM((2, 256), F32),
            pltpu.SemaphoreType.DMA((9,)),
        ],
        range(6),
    )(*map(stay, (pair_k, pair_slot, k_order.reshape(1, -1), orbitals, trial, transition)))
    far_bare = stay(bare)
    own = exchange(copies, "y")
    plane = exchange(ids, PLANE)
    (packed,) = call(pack_kernel, [((80, 256), BF)], (), [pltpu.VMEM((16, 256), F32)])(held, own)
    gat = lax.all_gather(packed, "z")
    chosen, column = call(
        select_kernel,
        [((4, 224, 256), BF), ((8, 256), F32)],
        (0,),
        [pltpu.VMEM((128, 512), F32)],
    )(plane, gat, swap(gat))
    got = exchange(chosen, "x")
    (scr,) = call(
        fetch_kernel, [(screened.shape, BF)], (), [pltpu.SemaphoreType.DMA(())], (0,)
    )(stay(screened))
    val, cond, dens = call(
        accept_kernel,
        [((4, 112, 256), BF), ((6, 16, 256), BF), ((8, 256), F32)],
        (0,),
        [pltpu.VMEM((16, 256), F32)],
    )(plane, got)
    wide = exchange(val, "y")
    base, route, back = call(
        base_kernel,
        [((4, 256), F32), ((256, 128), BF), ((64, 128), BF)],
        (0,),
        [
            pltpu.VMEM((4, 256), F32),
            pltpu.VMEM((128, 256), F32),
            pltpu.VMEM(bare.shape, BF),
            pltpu.SemaphoreType.DMA(()),
        ],
        (4,),
    )(plane, dens, column, own, far_bare, held)
    work = [
        pltpu.VMEM((6, 8, 256), F32),
        pltpu.VMEM((6, 8, 256), F32),
        pltpu.VMEM((2, 128, 256), F32),
        pltpu.VMEM((2, 128, 256), F32),
        pltpu.VMEM((4, 16, 256), F32),
    ]
    op, res = call(
        first_kernel,
        [((2, 864, 128), BF), ((32, 16, 256), BF)],
        (0,),
        work + [pltpu.VMEM((6, 256, 128), F32)],
    )(plane, wide, cond, scr, base)
    mixed = exchange(res, BLOCK)
    left = shift(op, 1)
    right = shift(op, -1)
    (middle,) = call(middle_kernel, [((16, 16, 256), BF)], ())(route, mixed)
    step = exchange(middle, "z")
    far = shift(left, 1)
    out2, own_x = call(
        second_kernel,
        [((8, 16, 384), BF), ((4, 256), F32)],
        (),
        [
            pltpu.VMEM((192, 16), BF),
            pltpu.VMEM((192, 16), F32),
            pltpu.VMEM((2, 32, 1024), F32),
            pltpu.VMEM((256, 1024), F32),
            pltpu.VMEM((32, 1024), F32),
            pltpu.VMEM((16, 256), F32),
            pltpu.VMEM((16, 128), F32),
        ],
    )(step, own, op, left, right, far)
    (final,) = call(return_kernel, [((16, 8, 384), BF)], (), [pltpu.VMEM((16, 8, 384), F32)])(
        back, exchange(out2, PLANE)
    )
    last = exchange(final, "z")
    (near_bare,) = call(
        fetch_kernel, [(bare.shape, BF)], (), [pltpu.SemaphoreType.DMA(())], (0,)
    )(far_bare)
    (result,) = call(last_kernel, [(trial.shape, F32)], (0,))(
        cheb, last, own, near_bare, held, own_x
    )
    return result


def solution(mesh):
    split = Mesh(mesh.devices.reshape(16, 4, 2, mesh.shape["vert"]), ("z", "x", "c", "y"))
    in_specs = (
        P(PB, None, "y"),
        P(PB, None),
        P("y", PB, None),
        P(PB, None, "y"),
        P(),
        P(),
        P(PB),
        P(PB),
        P(),
    )
    out_specs = P("y", PB, None)
    return jax.shard_map(body, mesh=split, in_specs=in_specs, out_specs=out_specs, check_vma=False)
```

```python
import jax
import jax.numpy as jnp
from jax import lax
from jax.experimental import pallas as pl
from jax.experimental.pallas import tpu as pltpu
from jax.sharding import Mesh
from jax.sharding import PartitionSpec as P


BF = jnp.bfloat16
F32 = jnp.float32
LAST = (((1,), (1,)), ((), ()))
PB = ("z", "x", "c")
PLANE = ("x", "c")
BLOCK = ("x", "c", "y")
LIMIT = 12 << 20


def exchange(blocks, axis):
    return lax.all_to_all(blocks, axis, 0, 0, tiled=True)


def swap(shard):
    return lax.ppermute(shard, "c", [(0, 1), (1, 0)])


def shift(shard, by):
    count = lax.axis_size("y")
    return lax.ppermute(shard, "y", [(k, (k + by) % count) for k in range(count)])


def stay(array):
    return pltpu.with_memory_space_constraint(array, pltpu.HBM)


def dot(a, b):
    return jnp.dot(a, b, preferred_element_type=F32)


def dot_t(a, b):
    return lax.dot_general(a, b, LAST, preferred_element_type=F32)


def call(kernel, outs, smem, scratch=(), far=(), limit=LIMIT):
    def space(k):
        return pltpu.SMEM if k in smem else pltpu.HBM if k in far else pltpu.VMEM

    def run(*args):
        specs = [pl.BlockSpec(memory_space=space(k)) for k in range(len(args))]
        return pl.pallas_call(
            kernel,
            out_shape=[jax.ShapeDtypeStruct(s, d) for s, d in outs],
            in_specs=specs,
            out_specs=[
                pl.BlockSpec(memory_space=pltpu.SMEM if len(s) == 1 else pltpu.VMEM)
                for s, _ in outs
            ],
            scratch_shapes=list(scratch),
            compiler_params=pltpu.CompilerParams(vmem_limit_bytes=limit),
            cost_estimate=pl.CostEstimate(flops=0, transcendentals=0, bytes_accessed=4 << 20),
        )(*args)

    return run


def lanes(rows, width):
    return lax.broadcasted_iota(jnp.int32, (rows, width), 1)


def products_of(own_ref, s, part):
    val = own_ref[part, s, 0:16, :].astype(F32)
    cond = own_ref[part, s, 16:32, :].astype(F32)
    pieces = [(val[v : v + 1, :] * cond).astype(BF) for v in range(16)]
    return jnp.concatenate(pieces, axis=0)


def density_of(own_ref, rows_bf):
    parts = []
    for part in range(4):
        total = dot(rows_bf[0], products_of(own_ref, 0, part))
        total = total + dot(rows_bf[1], products_of(own_ref, 1, part))
        parts.append(total)
    return parts


def bare_of(own_ref, bare_ref, dens):
    pots = []
    for out in range(4):
        total = jnp.zeros((2, 256), F32)
        for part in range(4):
            total = total + dot_t(
                dens[part].astype(BF),
                bare_ref[out * 256 : (out + 1) * 256, part * 256 : (part + 1) * 256],
            )
        pots.append(total.astype(BF))
    terms = []
    for s in range(2):
        total = jnp.zeros((2, 256), F32)
        for part in range(4):
            total = total + dot_t(pots[part], products_of(own_ref, s, part))
        terms.append(total)
    return terms


def copies_kernel(orb_hbm, own_ref, sem):
    copies = [
        pltpu.make_async_copy(orb_hbm, own_ref.at[part], sem.at[part]) for part in range(4)
    ]
    for copy in copies:
        copy.start()
    for copy in copies:
        copy.wait()


def info_kernel(
    pair_hbm, slot_hbm, order_hbm, trial_hbm, trans_hbm,
    ids_ref, held_ref, pair_ref, slot_ref, order_ref, trial_ref, trans_ref, sem,
):
    moves = [
        (pair_hbm, pair_ref), (slot_hbm, slot_ref), (order_hbm, order_ref),
        (trial_hbm, trial_ref), (trans_hbm, trans_ref),
    ]
    copies = [pltpu.make_async_copy(a, b, sem.at[k]) for k, (a, b) in enumerate(moves)]
    for copy in copies:
        copy.start()
    for copy in copies[:3]:
        copy.wait()
    position = lax.axis_index(PB)
    lane = lanes(1, 256)
    short = lanes(1, 128)
    order = order_ref[...]
    ids = jnp.where(short == 6, position * 2, jnp.where(short == 7, position * 2 + 1, 0))
    kind = lax.rem(lane, 16) // 2
    spread_ids = position * 2 + kind - 6
    for i in range(3):
        first = pair_ref[i]
        second = first - position * 2 - slot_ref[i]
        second = jnp.where(second < 0, second + 256, second)
        for h, k in enumerate((first, second)):
            row = jnp.sum(jnp.where(order == k, lane, 0))
            ids = jnp.where(short == 2 * i + h, row, ids)
            spread_ids = jnp.where(kind == 2 * i + h, row, spread_ids)
        ids = jnp.where(short == 8 + i, slot_ref[i], ids)
    for peer in range(8):
        ids_ref[peer] = ids
    for copy in copies[3:]:
        copy.wait()
    held_ref[...] = jnp.zeros((8, 256), F32)
    for s in range(2):
        held_ref[2 * s : 2 * s + 2, :] = trial_ref[:, s, :]
    held_ref[4:6, :] = trans_ref[...]
    held_ref[6:7, :] = spread_ids.astype(F32)


def pack_kernel(held_ref, own_ref, out_ref, tail_ref):
    out_ref[0:64, :] = own_ref[lax.axis_index("y")].reshape(64, 256)
    rows = [held_ref[2 * s : 2 * s + 2, :].astype(BF) for s in range(2)]
    parts = density_of(own_ref, rows)
    tail_ref[...] = jnp.zeros((16, 256), F32)
    for s in range(2):
        tail_ref[2 * s : 2 * s + 2, :] = rows[s].astype(F32)
    for part in range(4):
        tail_ref[4 + 2 * part : 6 + 2 * part, :] = parts[part]
    tail_ref[12:13, :] = held_ref[6:7, :]
    out_ref[64:80, :] = tail_ref[...].astype(BF)


def select_kernel(plane_ref, gat_ref, twin_ref, out_ref, column_ref, pick_ref):
    lane = lanes(1, 512)
    core = lax.axis_index("c")
    held = jnp.zeros((1, 256), F32)
    for z in range(16):
        row = gat_ref[z, 64:80, :].astype(F32)[12:13, :]
        held = jnp.where(lanes(1, 256) // 16 == z, row, held)
    column_ref[...] = jnp.broadcast_to(held, (8, 256))
    pick_ref[...] = jnp.zeros((128, 512), F32)
    for peer in range(4):
        for e in range(6):
            row = plane_ref[2 * peer + core, 0, e]
            z = row // 16
            s = lax.rem(row, 2)
            ours = lax.rem(row // 2, 2) == core
            first = z * 16 + 2 * s + jnp.where(ours, 0, 256)
            for n in range(2):
                at = peer * 32 + 2 * e + n
                pick_ref[at : at + 1, :] = (lane == first + n).astype(F32)
            at = pl.multiple_of(s * 32, 32)

            @pl.when(ours)
            def _():
                out_ref[peer, 32 * e : 32 * e + 32, :] = gat_ref[z, pl.ds(at, 32), :]

            @pl.when(jnp.logical_not(ours))
            def _():
                out_ref[peer, 32 * e : 32 * e + 32, :] = twin_ref[z, pl.ds(at, 32), :]

        for d in range(8):
            at = peer * 32 + 16 + d
            pick_ref[at : at + 1, :] = (lax.rem(lane, 16) == 4 + d).astype(F32)
    pick = pick_ref[...].astype(BF)
    picked = dot(pick[:, 0:256], gat_ref[:, 64:80, :].reshape(256, 256))
    picked = picked + dot(pick[:, 256:512], twin_ref[:, 64:80, :].reshape(256, 256))
    out_ref[:, 192:224, :] = picked.astype(BF).reshape(4, 32, 256)


def fetch_kernel(far_ref, near_ref, sem):
    copy = pltpu.make_async_copy(far_ref, near_ref, sem)
    copy.start()
    copy.wait()


def accept_kernel(plane_ref, got_ref, val_ref, cond_ref, dens_ref, tail_ref):
    for e in range(6):
        column = lax.rem(plane_ref[lax.axis_index(PLANE), 0, e] // 4, 4)
        val = got_ref[column, 32 * e : 32 * e + 16, :]
        for part in range(4):
            val_ref[part, 16 * e : 16 * e + 16, :] = val
        cond_ref[e] = got_ref[column, 32 * e + 16 : 32 * e + 32, :]
        part = got_ref[column, 192:208, :].astype(F32)
        tail_ref[2 * e : 2 * e + 2, :] = part[2 * e : 2 * e + 2, :]
    tail_ref[12:16, :] = jnp.zeros((4, 256), F32)
    for part in range(4):
        val_ref[part, 96:112, :] = tail_ref[...].astype(BF)
    total = got_ref[0, 208:224, :].astype(F32)
    for peer in range(1, 4):
        total = total + got_ref[peer, 208:224, :].astype(F32)
    dens_ref[...] = total[0:8, :]


def base_kernel(
    plane_ref, dens_ref, column_ref, own_ref, bare_hbm, held_ref,
    base_ref, route_ref, back_ref, base_s, route_s, bare_ref, sem,
):
    copy = pltpu.make_async_copy(bare_hbm, bare_ref, sem)
    copy.start()
    lane = lanes(1, 256)
    held = column_ref[0:1, :].astype(jnp.int32)
    parity = lax.rem(lane, 2)
    z_me = lax.axis_index("z")
    q_me = lax.axis_index(PLANE)
    for peer in range(8):
        for k in range(8):
            row = plane_ref[peer, 0, k] if k < 6 else z_me * 16 + peer * 2 + (k - 6)
            for n in range(2):
                at = peer * 16 + 2 * k + n
                hit = (held == row) & (parity == n)
                route_s[at : at + 1, :] = jnp.where(hit, -1.0 if k < 6 else 1.0, 0.0)
    route_ref[...] = jnp.transpose(route_s[...]).astype(BF)

    wide = lanes(1, 128)
    sent = jnp.full((1, 128), -1, jnp.int32)
    for peer in range(8):
        for e in range(6):
            here = (wide // 16 == peer) & (lax.rem(wide, 16) // 2 == e)
            sent = jnp.where(here, plane_ref[peer, 0, e], sent)
    row = lax.broadcasted_iota(jnp.int32, (64, 128), 0)
    target = (row // 4) * 16 + q_me * 2 + lax.rem(row, 4) // 2
    hit = (sent == target) & (lax.rem(row, 2) == lax.rem(lanes(64, 128), 2))
    back_ref[...] = jnp.where(hit, -1.0, 0.0).astype(BF)

    copy.wait()
    dens = [dens_ref[2 * part : 2 * part + 2, :] for part in range(4)]
    terms = bare_of(own_ref, bare_ref, dens)
    for s in range(2):
        x = held_ref[2 * s : 2 * s + 2, :].astype(BF).astype(F32)
        base_s[2 * s : 2 * s + 2, :] = held_ref[4 + s : 5 + s, :] * x + 2.0 * terms[s]
    base_ref[...] = base_s[...]


def spread(x):
    rows = jnp.concatenate([x] * 16, axis=0)
    group = lax.broadcasted_iota(jnp.int32, (128, 256), 0) // 8
    return jnp.where(group == lanes(128, 256) // 16, rows, 0.0).astype(BF)


def gathered(full):
    group = lax.broadcasted_iota(jnp.int32, (128, 256), 0) // 8
    kept = jnp.where(group == lanes(128, 256) // 16, full, 0.0)
    total = kept[0:8, :]
    for v in range(1, 16):
        total = total + kept[8 * v : 8 * v + 8, :]
    return total


def apply_pair(i, half_ref, cond_ref, xs_ref, ys_ref, t_ref, u_ref):
    tile_a = jnp.concatenate([cond_ref[2 * i]] * 16, axis=0)
    tile_c = jnp.concatenate([cond_ref[2 * i + 1]] * 16, axis=0)
    t_ref[0] = dot(spread(xs_ref[2 * i]), tile_a)
    t_ref[1] = dot(spread(xs_ref[2 * i + 1]), tile_c)
    for part in range(2):
        at = slice(128 * part, 128 * part + 128)
        t_c = [t_ref[1, 8 * w : 8 * w + 8, at] for w in range(16)]
        u_c = [None] * 16
        for v in range(16):
            t_a = t_ref[0, 8 * v : 8 * v + 8, at]
            sums = [None] * 2
            for w in range(16):
                row = 16 * v + w
                h = jnp.broadcast_to(half_ref[2 * i + part, row : row + 1, :], (8, 128))
                one, two = h * t_c[w], h * t_a
                sums[w % 2] = one if w < 2 else sums[w % 2] + one
                u_c[w] = two if v == 0 else u_c[w] + two
            u_ref[0, 8 * v : 8 * v + 8, at] = sums[0] + sums[1]
        for w in range(16):
            u_ref[1, 8 * w : 8 * w + 8, at] = u_c[w]
    ys_ref[2 * i] = gathered(dot_t(u_ref[0].astype(BF), tile_a))
    ys_ref[2 * i + 1] = gathered(dot_t(u_ref[1].astype(BF), tile_c))


def first_kernel(
    plane_ref, wide_ref, cond_ref, scr_ref, base_ref, op_ref, res_ref,
    xs_ref, ys_ref, t_ref, u_ref, rs_ref, half_ref,
):
    for e in range(6):
        op_ref[0, 768 + 16 * e : 784 + 16 * e, :] = cond_ref[e, :, 0:128]
        op_ref[1, 768 + 16 * e : 784 + 16 * e, :] = cond_ref[e, :, 128:256]
    for part in range(4):
        tail = wide_ref[part, 96:112, :].astype(F32)
        for e in range(6):
            xs_ref[e, 2 * part : 2 * part + 2, :] = tail[2 * e : 2 * e + 2, :]

    def one(i, carry):
        slot = plane_ref[lax.axis_index(PLANE), 0, 8 + i]
        total = jnp.zeros((256, 256), F32)
        for part in range(4):
            at = pl.multiple_of(i * 32, 16)
            a = wide_ref[part, pl.ds(at, 16), :].astype(F32)
            b = wide_ref[part, pl.ds(at + 16, 16), :].astype(F32)
            left = jnp.concatenate(
                [(a[v : v + 1, :] * b).astype(BF) for v in range(16)], axis=0
            )
            total = total + dot(left, scr_ref[slot, part * 256 : (part + 1) * 256, :])
        total = total.astype(BF)
        at = pl.multiple_of(i * 256, 256)
        op_ref[0, pl.ds(at, 256), :] = total[:, 0:128]
        op_ref[1, pl.ds(at, 256), :] = total[:, 128:256]
        total = total.astype(F32)
        half_ref[2 * i] = total[:, 0:128]
        half_ref[2 * i + 1] = total[:, 128:256]
        apply_pair(i, half_ref, cond_ref, xs_ref, ys_ref, t_ref, u_ref)
        return carry

    lax.fori_loop(0, 3, one, 0)
    for part in range(4):
        for e in range(6):
            rs_ref[part, 2 * e : 2 * e + 2, :] = ys_ref[e, 2 * part : 2 * part + 2, :]
        mine = (lax.axis_index("y") == part).astype(F32)
        rs_ref[part, 12:16, :] = base_ref[...] * mine
    for peer in range(8):
        for part in range(4):
            res_ref[4 * peer + part] = rs_ref[part].astype(BF)


def middle_kernel(route_ref, got_ref, out_ref):
    peers = []
    for peer in range(8):
        total = got_ref[4 * peer].astype(F32)
        for part in range(1, 4):
            total = total + got_ref[4 * peer + part].astype(F32)
        peers.append(total.astype(BF))
    full = dot(route_ref[...], jnp.concatenate(peers, axis=0))
    out_ref[...] = full.astype(BF).reshape(16, 16, 256)


def picker(rows, columns):
    row = lax.broadcasted_iota(jnp.int32, (rows, columns), 0)
    return (lax.rem(row, 16) == lax.rem(lanes(rows, columns), 16)).astype(BF)


def second_kernel(
    got_ref, own_ref, op_ref, left_ref, right_ref, far_ref, out_ref, own_x_ref,
    x_ref, y_ref, t_ref, ua_ref, uc_ref, rs_ref, ds_ref,
):
    total = got_ref[0].astype(F32)
    for z in range(1, 16):
        total = total + got_ref[z].astype(F32)
    own_x_ref[...] = total[12:16, :]
    parts = density_of(own_ref, [total[12 + 2 * s : 14 + 2 * s, :].astype(BF) for s in range(2)])
    for part in range(4):
        for h in range(2):
            at = 4 * part + 2 * h
            ds_ref[at : at + 2, :] = parts[part][:, 128 * h : 128 * h + 128]

    here = lanes(16, 256) // 16 == lax.broadcasted_iota(jnp.int32, (16, 256), 0)
    rows = [jnp.where(here, total[k : k + 1, :], 0.0).astype(BF) for k in range(12)]
    x_ref[...] = dot(jnp.concatenate(rows, axis=0), picker(256, 16)).astype(BF)

    chunks = [(ref, h) for ref in (op_ref, left_ref, right_ref, far_ref) for h in range(2)]

    def one(p, carry):
        at = pl.multiple_of(p * 64, 64)
        conds = []
        for end in range(2):
            row = pl.multiple_of(768 + p * 32 + end * 16, 16)
            conds.append(
                jnp.concatenate([ref[h, pl.ds(row, 16), :] for ref, h in chunks], axis=1)
            )
            t_ref[end] = dot(x_ref[pl.ds(pl.multiple_of(at + 32 * end, 32), 32), :], conds[end])
        for k, (ref, h) in enumerate(chunks):
            span = slice(128 * k, 128 * k + 128)
            t_c = [t_ref[1, 8 * g : 8 * g + 8, span] for g in range(4)]
            sums = [None] * 4
            for v in range(16):
                tile = ref[h, pl.ds(pl.multiple_of(p * 256 + 16 * v, 16), 16), :].astype(F32)
                lo, hi = tile[0:8, :], tile[8:16, :]
                for n in range(2):
                    ua_ref[128 * n + 8 * v : 128 * n + 8 * v + 8, span] = (
                        lo * t_c[2 * n] + hi * t_c[2 * n + 1]
                    )
                    t_a = jnp.broadcast_to(
                        t_ref[0, 16 * n + v : 16 * n + v + 1, span], (8, 128)
                    )
                    for g, part in ((2 * n, lo * t_a), (2 * n + 1, hi * t_a)):
                        sums[g] = part if v == 0 else sums[g] + part
            for g in range(4):
                uc_ref[8 * g : 8 * g + 8, span] = sums[g]
        first = dot_t(ua_ref[...].astype(BF), conds[0])
        y_ref[pl.ds(at, 32), :] = jnp.sum(first.reshape(32, 8, 16), axis=1)
        y_ref[pl.ds(pl.multiple_of(at + 32, 32), 32), :] = dot_t(uc_ref[...].astype(BF), conds[1])
        return carry

    lax.fori_loop(0, 3, one, 0)
    full = dot(y_ref[...].astype(BF), picker(16, 256)).reshape(12, 16, 256)
    rs_ref[0:12, :] = jnp.sum(jnp.where(here[None], full, 0.0), axis=1)
    rs_ref[12:16, :] = jnp.zeros((4, 256), F32)
    for peer in range(8):
        out_ref[peer, :, 0:256] = rs_ref[...].astype(BF)
        out_ref[peer, :, 256:384] = ds_ref[...].astype(BF)


def return_kernel(back_ref, got_ref, out_ref, buf_ref):
    full = dot(back_ref[...], got_ref[:, :, 0:256].reshape(128, 256))
    total = got_ref[0, :, 256:384].astype(F32)
    for peer in range(1, 8):
        total = total + got_ref[peer, :, 256:384].astype(F32)
    for part in range(4):
        for h in range(2):
            at = 4 * part + 2 * h
            span = slice(128 * h, 128 * h + 128)
            buf_ref[0, 2 * part : 2 * part + 2, span] = total[at : at + 2, :]
    for z in range(16):
        if z:
            buf_ref[z, :, 0:256] = buf_ref[0, :, 0:256]
        for h in range(2):
            span = slice(128 * h, 128 * h + 128)
            buf_ref[z, 4 * h : 4 * h + 4, 256:384] = full[4 * z : 4 * z + 4, span]
    out_ref[...] = buf_ref[...].astype(BF)


def last_kernel(cheb_ref, got_ref, own_ref, bare_ref, held_ref, own_x_ref, out_ref):
    total = got_ref[0].astype(F32)
    for z in range(1, 16):
        total = total + got_ref[z].astype(F32)
    dens = [total[2 * part : 2 * part + 2, 0:256] for part in range(4)]
    rows = jnp.concatenate([total[0:4, 256:384], total[4:8, 256:384]], axis=1)
    terms = bare_of(own_ref, bare_ref, dens)
    for s in range(2):
        x = own_x_ref[2 * s : 2 * s + 2, :]
        t = held_ref[2 * s : 2 * s + 2, :]
        applied = (
            held_ref[4 + s : 5 + s, :] * x.astype(BF).astype(F32)
            + 2.0 * terms[s]
            + rows[2 * s : 2 * s + 2, :]
        )
        second = 2.0 * applied - t
        out_ref[:, s, :] = cheb_ref[0] * t + cheb_ref[1] * x + cheb_ref[2] * second


def body(orbitals, transition, trial, screened, bare, cheb, pair_k, pair_slot, k_order):
    (copies,) = call(
        copies_kernel, [((4, 2, 32, 256), BF)], (), [pltpu.SemaphoreType.DMA((4,))], (0,)
    )(stay(orbitals))
    far_bare = stay(bare)
    own = exchange(copies, "y")
    ids, held = call(
        info_kernel,
        [((8, 1, 128), jnp.int32), ((8, 256), F32)],
        (),
        [
            pltpu.SMEM((3,), jnp.int32),
            pltpu.SMEM((3,), jnp.int32),
            pltpu.VMEM((1, 256), jnp.int32),
            pltpu.VMEM((2, 2, 256), F32),
            pltpu.VMEM((2, 256), F32),
            pltpu.SemaphoreType.DMA((5,)),
        ],
        range(5),
    )(*map(stay, (pair_k, pair_slot, k_order.reshape(1, -1), trial, transition)))
    plane = exchange(ids, PLANE)
    (packed,) = call(pack_kernel, [((80, 256), BF)], (), [pltpu.VMEM((16, 256), F32)])(held, own)
    gat = lax.all_gather(packed, "z")
    twin = swap(gat)
    chosen, column = call(
        select_kernel,
        [((4, 224, 256), BF), ((8, 256), F32)],
        (0,),
        [pltpu.VMEM((128, 512), F32)],
    )(plane, gat, twin)
    got = exchange(chosen, "x")
    (scr,) = call(
        fetch_kernel, [(screened.shape, BF)], (), [pltpu.SemaphoreType.DMA(())], (0,)
    )(stay(screened))
    val, cond, dens = call(
        accept_kernel,
        [((4, 112, 256), BF), ((6, 16, 256), BF), ((8, 256), F32)],
        (0,),
        [pltpu.VMEM((16, 256), F32)],
    )(plane, got)
    wide = exchange(val, "y")
    base, route, back = call(
        base_kernel,
        [((4, 256), F32), ((256, 128), BF), ((64, 128), BF)],
        (0,),
        [
            pltpu.VMEM((4, 256), F32),
            pltpu.VMEM((128, 256), F32),
            pltpu.VMEM(bare.shape, BF),
            pltpu.SemaphoreType.DMA(()),
        ],
        (4,),
    )(plane, dens, column, own, far_bare, held)
    work = [
        pltpu.VMEM((6, 8, 256), F32),
        pltpu.VMEM((6, 8, 256), F32),
        pltpu.VMEM((2, 128, 256), F32),
        pltpu.VMEM((2, 128, 256), F32),
        pltpu.VMEM((4, 16, 256), F32),
    ]
    op, res = call(
        first_kernel,
        [((2, 864, 128), BF), ((32, 16, 256), BF)],
        (0,),
        work + [pltpu.VMEM((6, 256, 128), F32)],
    )(plane, wide, cond, scr, base)
    mixed = exchange(res, BLOCK)
    left = shift(op, 1)
    right = shift(op, -1)
    (middle,) = call(middle_kernel, [((16, 16, 256), BF)], ())(route, mixed)
    step = exchange(middle, "z")
    far = shift(left, 1)
    out2, own_x = call(
        second_kernel,
        [((8, 16, 384), BF), ((4, 256), F32)],
        (),
        [
            pltpu.VMEM((192, 16), BF),
            pltpu.VMEM((192, 16), F32),
            pltpu.VMEM((2, 32, 1024), F32),
            pltpu.VMEM((256, 1024), F32),
            pltpu.VMEM((32, 1024), F32),
            pltpu.VMEM((16, 256), F32),
            pltpu.VMEM((16, 128), F32),
        ],
    )(step, own, op, left, right, far)
    (final,) = call(return_kernel, [((16, 8, 384), BF)], (), [pltpu.VMEM((16, 8, 384), F32)])(
        back, exchange(out2, PLANE)
    )
    last = exchange(final, "z")
    (near_bare,) = call(
        fetch_kernel, [(bare.shape, BF)], (), [pltpu.SemaphoreType.DMA(())], (0,)
    )(far_bare)
    (result,) = call(last_kernel, [(trial.shape, F32)], (0,))(
        cheb, last, own, near_bare, held, own_x
    )
    return result


def solution(mesh):
    split = Mesh(mesh.devices.reshape(16, 4, 2, mesh.shape["vert"]), ("z", "x", "c", "y"))
    in_specs = (
        P(PB, None, "y"),
        P(PB, None),
        P("y", PB, None),
        P(PB, None, "y"),
        P(),
        P(),
        P(PB),
        P(PB),
        P(),
    )
    out_specs = P("y", PB, None)
    return jax.shard_map(body, mesh=split, in_specs=in_specs, out_specs=out_specs, check_vma=False)
```

```python
import jax
import jax.numpy as jnp
from jax import lax
from jax.experimental import pallas as pl
from jax.experimental.pallas import tpu as pltpu
from jax.sharding import Mesh
from jax.sharding import PartitionSpec as P


BF = jnp.bfloat16
F32 = jnp.float32
LAST = (((1,), (1,)), ((), ()))
PB = ("z", "x", "c")
PLANE = ("x", "c")
BLOCK = ("x", "c", "y")
LIMIT = 12 << 20


def exchange(blocks, axis):
    return lax.all_to_all(blocks, axis, 0, 0, tiled=True)


def swap(shard):
    return lax.ppermute(shard, "c", [(0, 1), (1, 0)])


def shift(shard, by):
    count = lax.axis_size("y")
    return lax.ppermute(shard, "y", [(k, (k + by) % count) for k in range(count)])


def stay(array):
    return pltpu.with_memory_space_constraint(array, pltpu.HBM)


def aligned(value, by):
    return value if isinstance(value, int) else pl.multiple_of(value, by)


def dot(a, b):
    return jnp.dot(a, b, preferred_element_type=F32)


def dot_t(a, b):
    return lax.dot_general(a, b, LAST, preferred_element_type=F32)


def call(kernel, outs, smem, scratch=(), far=(), limit=LIMIT):
    def space(k):
        return pltpu.SMEM if k in smem else pltpu.HBM if k in far else pltpu.VMEM

    def run(*args):
        specs = [pl.BlockSpec(memory_space=space(k)) for k in range(len(args))]
        return pl.pallas_call(
            kernel,
            out_shape=[jax.ShapeDtypeStruct(s, d) for s, d in outs],
            in_specs=specs,
            out_specs=[
                pl.BlockSpec(memory_space=pltpu.SMEM if len(s) == 1 else pltpu.VMEM)
                for s, _ in outs
            ],
            scratch_shapes=list(scratch),
            compiler_params=pltpu.CompilerParams(vmem_limit_bytes=limit),
            cost_estimate=pl.CostEstimate(flops=0, transcendentals=0, bytes_accessed=4 << 20),
        )(*args)

    return run


def lanes(rows, width):
    return lax.broadcasted_iota(jnp.int32, (rows, width), 1)


def products_of(own_ref, s, part):
    val = own_ref[part, s, 0:16, :]
    cond = own_ref[part, s, 16:32, :]
    pieces = [val[v : v + 1, :] * cond for v in range(16)]
    return jnp.concatenate(pieces, axis=0)


def density_of(own_ref, rows_bf):
    parts = []
    for part in range(4):
        total = dot(rows_bf[0], products_of(own_ref, 0, part))
        total = total + dot(rows_bf[1], products_of(own_ref, 1, part))
        parts.append(total)
    return parts


def bare_of(own_ref, bare_ref, dens):
    pots = []
    for out in range(4):
        total = jnp.zeros((2, 256), F32)
        for part in range(4):
            total = total + dot_t(
                dens[part].astype(BF),
                bare_ref[out * 256 : (out + 1) * 256, part * 256 : (part + 1) * 256],
            )
        pots.append(total.astype(BF))
    terms = []
    for s in range(2):
        total = jnp.zeros((2, 256), F32)
        for part in range(4):
            total = total + dot_t(pots[part], products_of(own_ref, s, part))
        terms.append(total)
    return terms


def copies_kernel(orb_hbm, own_ref, sem):
    copies = [
        pltpu.make_async_copy(orb_hbm, own_ref.at[part], sem.at[part]) for part in range(4)
    ]
    for copy in copies:
        copy.start()
    for copy in copies:
        copy.wait()


def info_kernel(
    pair_hbm, slot_hbm, order_hbm, trial_hbm, trans_hbm,
    ids_ref, held_ref, pair_ref, slot_ref, order_ref, trial_ref, trans_ref, sem,
):
    moves = [
        (pair_hbm, pair_ref), (slot_hbm, slot_ref), (order_hbm, order_ref),
        (trial_hbm, trial_ref), (trans_hbm, trans_ref),
    ]
    copies = [pltpu.make_async_copy(a, b, sem.at[k]) for k, (a, b) in enumerate(moves)]
    for copy in copies:
        copy.start()
    for copy in copies[:3]:
        copy.wait()
    position = lax.axis_index(PB)
    lane = lanes(1, 256)
    short = lanes(1, 128)
    order = order_ref[...]
    ids = jnp.where(short == 6, position * 2, jnp.where(short == 7, position * 2 + 1, 0))
    kind = lax.rem(lane, 16) // 2
    spread_ids = position * 2 + kind - 6
    for i in range(3):
        first = pair_ref[i]
        second = first - position * 2 - slot_ref[i]
        second = jnp.where(second < 0, second + 256, second)
        for h, k in enumerate((first, second)):
            row = jnp.sum(jnp.where(order == k, lane, 0))
            ids = jnp.where(short == 2 * i + h, row, ids)
            spread_ids = jnp.where(kind == 2 * i + h, row, spread_ids)
        ids = jnp.where(short == 8 + i, slot_ref[i], ids)
    for peer in range(8):
        ids_ref[peer] = ids
    for copy in copies[3:]:
        copy.wait()
    held_ref[...] = jnp.zeros((8, 256), F32)
    for s in range(2):
        held_ref[2 * s : 2 * s + 2, :] = trial_ref[:, s, :]
    held_ref[4:6, :] = trans_ref[...]
    held_ref[6:7, :] = spread_ids.astype(F32)


def pack_kernel(held_ref, own_ref, out_ref, tail_ref):
    out_ref[0:64, :] = own_ref[lax.axis_index("y")].reshape(64, 256)
    rows = [held_ref[2 * s : 2 * s + 2, :].astype(BF) for s in range(2)]
    parts = density_of(own_ref, rows)
    tail_ref[...] = jnp.zeros((16, 256), F32)
    for s in range(2):
        tail_ref[2 * s : 2 * s + 2, :] = rows[s].astype(F32)
    for part in range(4):
        tail_ref[4 + 2 * part : 6 + 2 * part, :] = parts[part]
    tail_ref[12:13, :] = held_ref[6:7, :]
    out_ref[64:80, :] = tail_ref[...].astype(BF)


def select_kernel(plane_ref, gat_ref, twin_ref, out_ref, column_ref, pick_ref):
    lane = lanes(1, 512)
    core = lax.axis_index("c")
    held = jnp.zeros((1, 256), F32)
    for z in range(16):
        row = gat_ref[z, 64:80, :].astype(F32)[12:13, :]
        held = jnp.where(lanes(1, 256) // 16 == z, row, held)
    column_ref[...] = jnp.broadcast_to(held, (8, 256))
    pick_ref[...] = jnp.zeros((128, 512), F32)
    for peer in range(4):
        for e in range(6):
            row = plane_ref[2 * peer + core, 0, e]
            z = row // 16
            s = lax.rem(row, 2)
            ours = lax.rem(row // 2, 2) == core
            first = z * 16 + 2 * s + jnp.where(ours, 0, 256)
            for n in range(2):
                at = peer * 32 + 2 * e + n
                pick_ref[at : at + 1, :] = (lane == first + n).astype(F32)
            at = aligned(s * 32, 32)

            @pl.when(ours)
            def _():
                out_ref[peer, 32 * e : 32 * e + 32, :] = gat_ref[z, pl.ds(at, 32), :]

            @pl.when(jnp.logical_not(ours))
            def _():
                out_ref[peer, 32 * e : 32 * e + 32, :] = twin_ref[z, pl.ds(at, 32), :]

        for d in range(8):
            at = peer * 32 + 16 + d
            pick_ref[at : at + 1, :] = (lax.rem(lane, 16) == 4 + d).astype(F32)
    pick = pick_ref[...].astype(BF)
    picked = dot(pick[:, 0:256], gat_ref[:, 64:80, :].reshape(256, 256))
    picked = picked + dot(pick[:, 256:512], twin_ref[:, 64:80, :].reshape(256, 256))
    out_ref[:, 192:224, :] = picked.astype(BF).reshape(4, 32, 256)


def fetch_kernel(far_ref, near_ref, sem):
    copy = pltpu.make_async_copy(far_ref, near_ref, sem)
    copy.start()
    copy.wait()


def accept_kernel(plane_ref, got_ref, val_ref, cond_ref, dens_ref, tail_ref):
    for e in range(6):
        column = lax.rem(plane_ref[lax.axis_index(PLANE), 0, e] // 4, 4)
        val = got_ref[column, 32 * e : 32 * e + 16, :]
        for part in range(4):
            val_ref[part, 16 * e : 16 * e + 16, :] = val
        cond_ref[e] = got_ref[column, 32 * e + 16 : 32 * e + 32, :]
        part = got_ref[column, 192:208, :].astype(F32)
        tail_ref[2 * e : 2 * e + 2, :] = part[2 * e : 2 * e + 2, :]
    tail_ref[12:16, :] = jnp.zeros((4, 256), F32)
    for part in range(4):
        val_ref[part, 96:112, :] = tail_ref[...].astype(BF)
    total = got_ref[0, 208:224, :].astype(F32)
    for peer in range(1, 4):
        total = total + got_ref[peer, 208:224, :].astype(F32)
    dens_ref[...] = total[0:8, :]


def base_kernel(
    plane_ref, dens_ref, column_ref, own_ref, bare_hbm, held_ref,
    base_ref, route_ref, back_ref, base_s, route_s, bare_ref, sem,
):
    copy = pltpu.make_async_copy(bare_hbm, bare_ref, sem)
    copy.start()
    lane = lanes(1, 256)
    held = column_ref[0:1, :].astype(jnp.int32)
    parity = lax.rem(lane, 2)
    z_me = lax.axis_index("z")
    q_me = lax.axis_index(PLANE)
    for peer in range(8):
        for k in range(8):
            row = plane_ref[peer, 0, k] if k < 6 else z_me * 16 + peer * 2 + (k - 6)
            for n in range(2):
                at = peer * 16 + 2 * k + n
                hit = (held == row) & (parity == n)
                route_s[at : at + 1, :] = jnp.where(hit, -1.0 if k < 6 else 1.0, 0.0)
    route_ref[...] = jnp.transpose(route_s[...]).astype(BF)

    wide = lanes(1, 128)
    sent = jnp.full((1, 128), -1, jnp.int32)
    for peer in range(8):
        for e in range(6):
            here = (wide // 16 == peer) & (lax.rem(wide, 16) // 2 == e)
            sent = jnp.where(here, plane_ref[peer, 0, e], sent)
    row = lax.broadcasted_iota(jnp.int32, (64, 128), 0)
    target = (row // 4) * 16 + q_me * 2 + lax.rem(row, 4) // 2
    hit = (sent == target) & (lax.rem(row, 2) == lax.rem(lanes(64, 128), 2))
    back_ref[...] = jnp.where(hit, -1.0, 0.0).astype(BF)

    copy.wait()
    dens = [dens_ref[2 * part : 2 * part + 2, :] for part in range(4)]
    terms = bare_of(own_ref, bare_ref, dens)
    for s in range(2):
        x = held_ref[2 * s : 2 * s + 2, :].astype(BF).astype(F32)
        base_s[2 * s : 2 * s + 2, :] = held_ref[4 + s : 5 + s, :] * x + 2.0 * terms[s]
    base_ref[...] = base_s[...]


def spread(x):
    rows = jnp.concatenate([x] * 16, axis=0)
    group = lax.broadcasted_iota(jnp.int32, (128, 256), 0) // 8
    return jnp.where(group == lanes(128, 256) // 16, rows, 0.0).astype(BF)


def gathered(full):
    group = lax.broadcasted_iota(jnp.int32, (128, 256), 0) // 8
    kept = jnp.where(group == lanes(128, 256) // 16, full, 0.0)
    total = kept[0:8, :]
    for v in range(1, 16):
        total = total + kept[8 * v : 8 * v + 8, :]
    return total


def apply_pair(i, half_ref, cond_ref, xs_ref, ys_ref, t_ref, u_ref):
    tile_a = jnp.concatenate([cond_ref[2 * i]] * 16, axis=0)
    tile_c = jnp.concatenate([cond_ref[2 * i + 1]] * 16, axis=0)
    t_ref[0] = dot(spread(xs_ref[2 * i]), tile_a)
    t_ref[1] = dot(spread(xs_ref[2 * i + 1]), tile_c)
    for part in range(2):
        at = slice(128 * part, 128 * part + 128)
        t_c = [t_ref[1, 8 * w : 8 * w + 8, at] for w in range(16)]
        u_c = [None] * 16
        for v in range(16):
            t_a = t_ref[0, 8 * v : 8 * v + 8, at]
            sums = [None] * 2
            for w in range(16):
                row = 16 * v + w
                h = jnp.broadcast_to(half_ref[2 * i + part, row : row + 1, :], (8, 128))
                one, two = h * t_c[w], h * t_a
                sums[w % 2] = one if w < 2 else sums[w % 2] + one
                u_c[w] = two if v == 0 else u_c[w] + two
            u_ref[0, 8 * v : 8 * v + 8, at] = sums[0] + sums[1]
        for w in range(16):
            u_ref[1, 8 * w : 8 * w + 8, at] = u_c[w]
    ys_ref[2 * i] = gathered(dot_t(u_ref[0].astype(BF), tile_a))
    ys_ref[2 * i + 1] = gathered(dot_t(u_ref[1].astype(BF), tile_c))


def first_kernel(
    plane_ref, wide_ref, cond_ref, scr_ref, base_ref, op_ref, res_ref,
    xs_ref, ys_ref, t_ref, u_ref, rs_ref, half_ref,
):
    for e in range(6):
        op_ref[0, 768 + 16 * e : 784 + 16 * e, :] = cond_ref[e, :, 0:128]
        op_ref[1, 768 + 16 * e : 784 + 16 * e, :] = cond_ref[e, :, 128:256]
    for part in range(4):
        tail = wide_ref[part, 96:112, :].astype(F32)
        for e in range(6):
            xs_ref[e, 2 * part : 2 * part + 2, :] = tail[2 * e : 2 * e + 2, :]

    def one(i, carry):
        slot = plane_ref[lax.axis_index(PLANE), 0, 8 + i]
        total = jnp.zeros((256, 256), F32)
        for part in range(4):
            at = aligned(i * 32, 16)
            a = wide_ref[part, pl.ds(at, 16), :]
            b = wide_ref[part, pl.ds(at + 16, 16), :]
            left = jnp.concatenate([a[v : v + 1, :] * b for v in range(16)], axis=0)
            total = total + dot(left, scr_ref[slot, part * 256 : (part + 1) * 256, :])
        total = total.astype(BF)
        at = aligned(i * 256, 256)
        op_ref[0, pl.ds(at, 256), :] = total[:, 0:128]
        op_ref[1, pl.ds(at, 256), :] = total[:, 128:256]
        total = total.astype(F32)
        half_ref[2 * i] = total[:, 0:128]
        half_ref[2 * i + 1] = total[:, 128:256]
        apply_pair(i, half_ref, cond_ref, xs_ref, ys_ref, t_ref, u_ref)
        return carry

    for i in range(3):
        one(i, 0)
    for part in range(4):
        for e in range(6):
            rs_ref[part, 2 * e : 2 * e + 2, :] = ys_ref[e, 2 * part : 2 * part + 2, :]
        mine = (lax.axis_index("y") == part).astype(F32)
        rs_ref[part, 12:16, :] = base_ref[...] * mine
    for peer in range(8):
        for part in range(4):
            res_ref[4 * peer + part] = rs_ref[part].astype(BF)


def middle_kernel(route_ref, got_ref, out_ref):
    peers = []
    for peer in range(8):
        total = got_ref[4 * peer].astype(F32)
        for part in range(1, 4):
            total = total + got_ref[4 * peer + part].astype(F32)
        peers.append(total.astype(BF))
    full = dot(route_ref[...], jnp.concatenate(peers, axis=0))
    out_ref[...] = full.astype(BF).reshape(16, 16, 256)


def picker(rows, columns):
    row = lax.broadcasted_iota(jnp.int32, (rows, columns), 0)
    return (lax.rem(row, 16) == lax.rem(lanes(rows, columns), 16)).astype(BF)


def second_kernel(
    got_ref, own_ref, op_ref, left_ref, right_ref, far_ref, out_ref, own_x_ref,
    x_ref, y_ref, t_ref, ua_ref, uc_ref, rs_ref, ds_ref,
):
    total = got_ref[0].astype(F32)
    for z in range(1, 16):
        total = total + got_ref[z].astype(F32)
    own_x_ref[...] = total[12:16, :]
    parts = density_of(own_ref, [total[12 + 2 * s : 14 + 2 * s, :].astype(BF) for s in range(2)])
    for part in range(4):
        for h in range(2):
            at = 4 * part + 2 * h
            ds_ref[at : at + 2, :] = parts[part][:, 128 * h : 128 * h + 128]

    here = lanes(16, 256) // 16 == lax.broadcasted_iota(jnp.int32, (16, 256), 0)
    rows = [jnp.where(here, total[k : k + 1, :], 0.0).astype(BF) for k in range(12)]
    x_ref[...] = dot(jnp.concatenate(rows, axis=0), picker(256, 16)).astype(BF)

    chunks = [(ref, h) for ref in (op_ref, left_ref, right_ref, far_ref) for h in range(2)]

    def one(p, carry):
        at = aligned(p * 64, 64)
        conds = []
        for end in range(2):
            row = aligned(768 + p * 32 + end * 16, 16)
            conds.append(
                jnp.concatenate([ref[h, pl.ds(row, 16), :] for ref, h in chunks], axis=1)
            )
            t_ref[end] = dot(x_ref[pl.ds(aligned(at + 32 * end, 32), 32), :], conds[end])
        for k, (ref, h) in enumerate(chunks):
            span = slice(128 * k, 128 * k + 128)
            t_c = [t_ref[1, 8 * g : 8 * g + 8, span] for g in range(4)]
            sums = [None] * 4
            for v in range(16):
                tile = ref[h, pl.ds(aligned(p * 256 + 16 * v, 16), 16), :].astype(F32)
                lo, hi = tile[0:8, :], tile[8:16, :]
                for n in range(2):
                    ua_ref[128 * n + 8 * v : 128 * n + 8 * v + 8, span] = (
                        lo * t_c[2 * n] + hi * t_c[2 * n + 1]
                    )
                    t_a = jnp.broadcast_to(
                        t_ref[0, 16 * n + v : 16 * n + v + 1, span], (8, 128)
                    )
                    for g, part in ((2 * n, lo * t_a), (2 * n + 1, hi * t_a)):
                        sums[g] = part if v == 0 else sums[g] + part
            for g in range(4):
                uc_ref[8 * g : 8 * g + 8, span] = sums[g]
        first = dot_t(ua_ref[...].astype(BF), conds[0])
        y_ref[pl.ds(at, 32), :] = jnp.sum(first.reshape(32, 8, 16), axis=1)
        y_ref[pl.ds(aligned(at + 32, 32), 32), :] = dot_t(uc_ref[...].astype(BF), conds[1])
        return carry

    for p in range(3):
        one(p, 0)
    full = dot(y_ref[...].astype(BF), picker(16, 256)).reshape(12, 16, 256)
    rs_ref[0:12, :] = jnp.sum(jnp.where(here[None], full, 0.0), axis=1)
    rs_ref[12:16, :] = jnp.zeros((4, 256), F32)
    for peer in range(8):
        out_ref[peer, :, 0:256] = rs_ref[...].astype(BF)
        out_ref[peer, :, 256:384] = ds_ref[...].astype(BF)


def return_kernel(back_ref, got_ref, out_ref, buf_ref):
    full = dot(back_ref[...], got_ref[:, :, 0:256].reshape(128, 256))
    total = got_ref[0, :, 256:384].astype(F32)
    for peer in range(1, 8):
        total = total + got_ref[peer, :, 256:384].astype(F32)
    for part in range(4):
        for h in range(2):
            at = 4 * part + 2 * h
            span = slice(128 * h, 128 * h + 128)
            buf_ref[0, 2 * part : 2 * part + 2, span] = total[at : at + 2, :]
    for z in range(16):
        if z:
            buf_ref[z, :, 0:256] = buf_ref[0, :, 0:256]
        for h in range(2):
            span = slice(128 * h, 128 * h + 128)
            buf_ref[z, 4 * h : 4 * h + 4, 256:384] = full[4 * z : 4 * z + 4, span]
    out_ref[...] = buf_ref[...].astype(BF)


def last_kernel(cheb_ref, got_ref, own_ref, bare_ref, held_ref, own_x_ref, out_ref):
    total = got_ref[0].astype(F32)
    for z in range(1, 16):
        total = total + got_ref[z].astype(F32)
    dens = [total[2 * part : 2 * part + 2, 0:256] for part in range(4)]
    rows = jnp.concatenate([total[0:4, 256:384], total[4:8, 256:384]], axis=1)
    terms = bare_of(own_ref, bare_ref, dens)
    for s in range(2):
        x = own_x_ref[2 * s : 2 * s + 2, :]
        t = held_ref[2 * s : 2 * s + 2, :]
        applied = (
            held_ref[4 + s : 5 + s, :] * x.astype(BF).astype(F32)
            + 2.0 * terms[s]
            + rows[2 * s : 2 * s + 2, :]
        )
        second = 2.0 * applied - t
        out_ref[:, s, :] = cheb_ref[0] * t + cheb_ref[1] * x + cheb_ref[2] * second


def body(orbitals, transition, trial, screened, bare, cheb, pair_k, pair_slot, k_order):
    (copies,) = call(
        copies_kernel, [((4, 2, 32, 256), BF)], (), [pltpu.SemaphoreType.DMA((4,))], (0,)
    )(stay(orbitals))
    far_bare = stay(bare)
    own = exchange(copies, "y")
    ids, held = call(
        info_kernel,
        [((8, 1, 128), jnp.int32), ((8, 256), F32)],
        (),
        [
            pltpu.SMEM((3,), jnp.int32),
            pltpu.SMEM((3,), jnp.int32),
            pltpu.VMEM((1, 256), jnp.int32),
            pltpu.VMEM((2, 2, 256), F32),
            pltpu.VMEM((2, 256), F32),
            pltpu.SemaphoreType.DMA((5,)),
        ],
        range(5),
    )(*map(stay, (pair_k, pair_slot, k_order.reshape(1, -1), trial, transition)))
    plane = exchange(ids, PLANE)
    (packed,) = call(pack_kernel, [((80, 256), BF)], (), [pltpu.VMEM((16, 256), F32)])(held, own)
    gat = lax.all_gather(packed, "z")
    twin = swap(gat)
    chosen, column = call(
        select_kernel,
        [((4, 224, 256), BF), ((8, 256), F32)],
        (0,),
        [pltpu.VMEM((128, 512), F32)],
    )(plane, gat, twin)
    got = exchange(chosen, "x")
    (scr,) = call(
        fetch_kernel, [(screened.shape, BF)], (), [pltpu.SemaphoreType.DMA(())], (0,)
    )(stay(screened))
    val, cond, dens = call(
        accept_kernel,
        [((4, 112, 256), BF), ((6, 16, 256), BF), ((8, 256), F32)],
        (0,),
        [pltpu.VMEM((16, 256), F32)],
    )(plane, got)
    wide = exchange(val, "y")
    base, route, back = call(
        base_kernel,
        [((4, 256), F32), ((256, 128), BF), ((64, 128), BF)],
        (0,),
        [
            pltpu.VMEM((4, 256), F32),
            pltpu.VMEM((128, 256), F32),
            pltpu.VMEM(bare.shape, BF),
            pltpu.SemaphoreType.DMA(()),
        ],
        (4,),
    )(plane, dens, column, own, far_bare, held)
    work = [
        pltpu.VMEM((6, 8, 256), F32),
        pltpu.VMEM((6, 8, 256), F32),
        pltpu.VMEM((2, 128, 256), F32),
        pltpu.VMEM((2, 128, 256), F32),
        pltpu.VMEM((4, 16, 256), F32),
    ]
    op, res = call(
        first_kernel,
        [((2, 864, 128), BF), ((32, 16, 256), BF)],
        (0,),
        work + [pltpu.VMEM((6, 256, 128), F32)],
    )(plane, wide, cond, scr, base)
    mixed = exchange(res, BLOCK)
    left = shift(op, 1)
    right = shift(op, -1)
    (middle,) = call(middle_kernel, [((16, 16, 256), BF)], ())(route, mixed)
    step = exchange(middle, "z")
    far = shift(left, 1)
    out2, own_x = call(
        second_kernel,
        [((8, 16, 384), BF), ((4, 256), F32)],
        (),
        [
            pltpu.VMEM((192, 16), BF),
            pltpu.VMEM((192, 16), F32),
            pltpu.VMEM((2, 32, 1024), F32),
            pltpu.VMEM((256, 1024), F32),
            pltpu.VMEM((32, 1024), F32),
            pltpu.VMEM((16, 256), F32),
            pltpu.VMEM((16, 128), F32),
        ],
    )(step, own, op, left, right, far)
    (final,) = call(return_kernel, [((16, 8, 384), BF)], (), [pltpu.VMEM((16, 8, 384), F32)])(
        back, exchange(out2, PLANE)
    )
    last = exchange(final, "z")
    (near_bare,) = call(
        fetch_kernel, [(bare.shape, BF)], (), [pltpu.SemaphoreType.DMA(())], (0,)
    )(far_bare)
    (result,) = call(last_kernel, [(trial.shape, F32)], (0,))(
        cheb, last, own, near_bare, held, own_x
    )
    return result


def solution(mesh):
    split = Mesh(mesh.devices.reshape(16, 4, 2, mesh.shape["vert"]), ("z", "x", "c", "y"))
    in_specs = (
        P(PB, None, "y"),
        P(PB, None),
        P("y", PB, None),
        P(PB, None, "y"),
        P(),
        P(),
        P(PB),
        P(PB),
        P(),
    )
    out_specs = P("y", PB, None)
    return jax.shard_map(body, mesh=split, in_specs=in_specs, out_specs=out_specs, check_vma=False)
```

```python
import jax
import jax.numpy as jnp
from jax import lax
from jax.experimental import pallas as pl
from jax.experimental.pallas import tpu as pltpu
from jax.sharding import Mesh
from jax.sharding import PartitionSpec as P


BF = jnp.bfloat16
F32 = jnp.float32
LAST = (((1,), (1,)), ((), ()))
PB = ("z", "x", "c")
PLANE = ("x", "c")
BLOCK = ("x", "c", "y")
LIMIT = 12 << 20


def exchange(blocks, axis):
    return lax.all_to_all(blocks, axis, 0, 0, tiled=True)


def swap(shard):
    return lax.ppermute(shard, "c", [(0, 1), (1, 0)])


def shift(shard, by):
    count = lax.axis_size("y")
    return lax.ppermute(shard, "y", [(k, (k + by) % count) for k in range(count)])


def stay(array):
    return pltpu.with_memory_space_constraint(array, pltpu.HBM)


def aligned(value, by):
    return value if isinstance(value, int) else pl.multiple_of(value, by)


def dot(a, b):
    return jnp.dot(a, b, preferred_element_type=F32)


def dot_t(a, b):
    return lax.dot_general(a, b, LAST, preferred_element_type=F32)


def call(kernel, outs, smem, scratch=(), far=(), limit=LIMIT):
    def space(k):
        return pltpu.SMEM if k in smem else pltpu.HBM if k in far else pltpu.VMEM

    def run(*args):
        specs = [pl.BlockSpec(memory_space=space(k)) for k in range(len(args))]
        return pl.pallas_call(
            kernel,
            out_shape=[jax.ShapeDtypeStruct(s, d) for s, d in outs],
            in_specs=specs,
            out_specs=[
                pl.BlockSpec(memory_space=pltpu.SMEM if len(s) == 1 else pltpu.VMEM)
                for s, _ in outs
            ],
            scratch_shapes=list(scratch),
            compiler_params=pltpu.CompilerParams(vmem_limit_bytes=limit),
            cost_estimate=pl.CostEstimate(flops=0, transcendentals=0, bytes_accessed=4 << 20),
        )(*args)

    return run


def lanes(rows, width):
    return lax.broadcasted_iota(jnp.int32, (rows, width), 1)


def products_of(own_ref, s, part):
    val = own_ref[part, s, 0:16, :]
    cond = own_ref[part, s, 16:32, :]
    pieces = [val[v : v + 1, :] * cond for v in range(16)]
    return jnp.concatenate(pieces, axis=0)


def density_of(own_ref, rows_bf):
    parts = []
    for part in range(4):
        total = dot(rows_bf[0], products_of(own_ref, 0, part))
        total = total + dot(rows_bf[1], products_of(own_ref, 1, part))
        parts.append(total)
    return parts


def bare_of(own_ref, bare_ref, dens):
    pots = []
    for out in range(4):
        total = jnp.zeros((2, 256), F32)
        for part in range(4):
            total = total + dot_t(
                dens[part].astype(BF),
                bare_ref[out * 256 : (out + 1) * 256, part * 256 : (part + 1) * 256],
            )
        pots.append(total.astype(BF))
    terms = []
    for s in range(2):
        total = jnp.zeros((2, 256), F32)
        for part in range(4):
            total = total + dot_t(pots[part], products_of(own_ref, s, part))
        terms.append(total)
    return terms


def info_kernel(
    pair_hbm, slot_hbm, order_hbm, trial_hbm, trans_hbm,
    ids_ref, held_ref, pair_ref, slot_ref, order_ref, trial_ref, trans_ref, sem,
):
    moves = [
        (pair_hbm, pair_ref), (slot_hbm, slot_ref), (order_hbm, order_ref),
        (trial_hbm, trial_ref), (trans_hbm, trans_ref),
    ]
    copies = [pltpu.make_async_copy(a, b, sem.at[k]) for k, (a, b) in enumerate(moves)]
    for copy in copies:
        copy.start()
    for copy in copies[:3]:
        copy.wait()
    position = lax.axis_index(PB)
    lane = lanes(1, 256)
    short = lanes(1, 128)
    order = order_ref[...]
    ids = jnp.where(short == 6, position * 2, jnp.where(short == 7, position * 2 + 1, 0))
    kind = lax.rem(lane, 16) // 2
    spread_ids = position * 2 + kind - 6
    for i in range(3):
        first = pair_ref[i]
        second = first - position * 2 - slot_ref[i]
        second = jnp.where(second < 0, second + 256, second)
        for h, k in enumerate((first, second)):
            row = jnp.sum(jnp.where(order == k, lane, 0))
            ids = jnp.where(short == 2 * i + h, row, ids)
            spread_ids = jnp.where(kind == 2 * i + h, row, spread_ids)
        ids = jnp.where(short == 8 + i, slot_ref[i], ids)
    for peer in range(8):
        ids_ref[peer] = ids
    for copy in copies[3:]:
        copy.wait()
    held_ref[...] = jnp.zeros((8, 256), F32)
    for s in range(2):
        held_ref[2 * s : 2 * s + 2, :] = trial_ref[:, s, :]
    held_ref[4:6, :] = trans_ref[...]
    held_ref[6:7, :] = spread_ids.astype(F32)


def pack_kernel(held_ref, own_ref, out_ref, tail_ref):
    out_ref[0:64, :] = own_ref[lax.axis_index("y")].reshape(64, 256)
    rows = [held_ref[2 * s : 2 * s + 2, :].astype(BF) for s in range(2)]
    parts = density_of(own_ref, rows)
    tail_ref[...] = jnp.zeros((16, 256), F32)
    for s in range(2):
        tail_ref[2 * s : 2 * s + 2, :] = rows[s].astype(F32)
    for part in range(4):
        tail_ref[4 + 2 * part : 6 + 2 * part, :] = parts[part]
    tail_ref[12:13, :] = held_ref[6:7, :]
    out_ref[64:80, :] = tail_ref[...].astype(BF)


def select_kernel(plane_ref, gat_ref, twin_ref, out_ref, column_ref, pick_ref):
    lane = lanes(1, 512)
    core = lax.axis_index("c")
    held = jnp.zeros((1, 256), F32)
    for z in range(16):
        row = gat_ref[z, 64:80, :].astype(F32)[12:13, :]
        held = jnp.where(lanes(1, 256) // 16 == z, row, held)
    column_ref[...] = jnp.broadcast_to(held, (8, 256))
    pick_ref[...] = jnp.zeros((128, 512), F32)
    for peer in range(4):
        for e in range(6):
            row = plane_ref[2 * peer + core, 0, e]
            z = row // 16
            s = lax.rem(row, 2)
            ours = lax.rem(row // 2, 2) == core
            first = z * 16 + 2 * s + jnp.where(ours, 0, 256)
            for n in range(2):
                at = peer * 32 + 2 * e + n
                pick_ref[at : at + 1, :] = (lane == first + n).astype(F32)
            at = aligned(s * 32, 32)

            @pl.when(ours)
            def _():
                out_ref[peer, 32 * e : 32 * e + 32, :] = gat_ref[z, pl.ds(at, 32), :]

            @pl.when(jnp.logical_not(ours))
            def _():
                out_ref[peer, 32 * e : 32 * e + 32, :] = twin_ref[z, pl.ds(at, 32), :]

        for d in range(8):
            at = peer * 32 + 16 + d
            pick_ref[at : at + 1, :] = (lax.rem(lane, 16) == 4 + d).astype(F32)
    pick = pick_ref[...].astype(BF)
    picked = dot(pick[:, 0:256], gat_ref[:, 64:80, :].reshape(256, 256))
    picked = picked + dot(pick[:, 256:512], twin_ref[:, 64:80, :].reshape(256, 256))
    out_ref[:, 192:224, :] = picked.astype(BF).reshape(4, 32, 256)


def fetch_kernel(far_ref, near_ref, sem):
    copy = pltpu.make_async_copy(far_ref, near_ref, sem)
    copy.start()
    copy.wait()


def accept_kernel(plane_ref, got_ref, val_ref, cond_ref, dens_ref, tail_ref):
    for e in range(6):
        column = lax.rem(plane_ref[lax.axis_index(PLANE), 0, e] // 4, 4)
        val = got_ref[column, 32 * e : 32 * e + 16, :]
        for part in range(4):
            val_ref[part, 16 * e : 16 * e + 16, :] = val
        cond_ref[e] = got_ref[column, 32 * e + 16 : 32 * e + 32, :]
        part = got_ref[column, 192:208, :].astype(F32)
        tail_ref[2 * e : 2 * e + 2, :] = part[2 * e : 2 * e + 2, :]
    tail_ref[12:16, :] = jnp.zeros((4, 256), F32)
    for part in range(4):
        val_ref[part, 96:112, :] = tail_ref[...].astype(BF)
    total = got_ref[0, 208:224, :].astype(F32)
    for peer in range(1, 4):
        total = total + got_ref[peer, 208:224, :].astype(F32)
    dens_ref[...] = total[0:8, :]


def base_kernel(
    plane_ref, dens_ref, column_ref, own_ref, bare_hbm, held_ref,
    base_ref, route_ref, back_ref, base_s, route_s, bare_ref, sem,
):
    copy = pltpu.make_async_copy(bare_hbm, bare_ref, sem)
    copy.start()
    lane = lanes(1, 256)
    held = column_ref[0:1, :].astype(jnp.int32)
    parity = lax.rem(lane, 2)
    z_me = lax.axis_index("z")
    q_me = lax.axis_index(PLANE)
    for peer in range(8):
        for k in range(8):
            row = plane_ref[peer, 0, k] if k < 6 else z_me * 16 + peer * 2 + (k - 6)
            for n in range(2):
                at = peer * 16 + 2 * k + n
                hit = (held == row) & (parity == n)
                route_s[at : at + 1, :] = jnp.where(hit, -1.0 if k < 6 else 1.0, 0.0)
    route_ref[...] = jnp.transpose(route_s[...]).astype(BF)

    wide = lanes(1, 128)
    sent = jnp.full((1, 128), -1, jnp.int32)
    for peer in range(8):
        for e in range(6):
            here = (wide // 16 == peer) & (lax.rem(wide, 16) // 2 == e)
            sent = jnp.where(here, plane_ref[peer, 0, e], sent)
    row = lax.broadcasted_iota(jnp.int32, (64, 128), 0)
    target = (row // 4) * 16 + q_me * 2 + lax.rem(row, 4) // 2
    hit = (sent == target) & (lax.rem(row, 2) == lax.rem(lanes(64, 128), 2))
    back_ref[...] = jnp.where(hit, -1.0, 0.0).astype(BF)

    copy.wait()
    dens = [dens_ref[2 * part : 2 * part + 2, :] for part in range(4)]
    terms = bare_of(own_ref, bare_ref, dens)
    for s in range(2):
        x = held_ref[2 * s : 2 * s + 2, :].astype(BF).astype(F32)
        base_s[2 * s : 2 * s + 2, :] = held_ref[4 + s : 5 + s, :] * x + 2.0 * terms[s]
    base_ref[...] = base_s[...]


def spread(x):
    rows = jnp.concatenate([x] * 16, axis=0)
    group = lax.broadcasted_iota(jnp.int32, (128, 256), 0) // 8
    return jnp.where(group == lanes(128, 256) // 16, rows, 0.0).astype(BF)


def gathered(full):
    group = lax.broadcasted_iota(jnp.int32, (128, 256), 0) // 8
    kept = jnp.where(group == lanes(128, 256) // 16, full, 0.0)
    total = kept[0:8, :]
    for v in range(1, 16):
        total = total + kept[8 * v : 8 * v + 8, :]
    return total


def apply_pair(i, half_ref, cond_ref, xs_ref, ys_ref, t_ref, u_ref):
    tile_a = jnp.concatenate([cond_ref[2 * i]] * 16, axis=0)
    tile_c = jnp.concatenate([cond_ref[2 * i + 1]] * 16, axis=0)
    t_ref[0] = dot(spread(xs_ref[2 * i]), tile_a)
    t_ref[1] = dot(spread(xs_ref[2 * i + 1]), tile_c)
    for part in range(2):
        at = slice(128 * part, 128 * part + 128)
        t_c = [t_ref[1, 8 * w : 8 * w + 8, at] for w in range(16)]
        u_c = [None] * 16
        for v in range(16):
            t_a = t_ref[0, 8 * v : 8 * v + 8, at]
            sums = [None] * 2
            for w in range(16):
                row = 16 * v + w
                h = jnp.broadcast_to(half_ref[2 * i + part, row : row + 1, :], (8, 128))
                one, two = h * t_c[w], h * t_a
                sums[w % 2] = one if w < 2 else sums[w % 2] + one
                u_c[w] = two if v == 0 else u_c[w] + two
            u_ref[0, 8 * v : 8 * v + 8, at] = sums[0] + sums[1]
        for w in range(16):
            u_ref[1, 8 * w : 8 * w + 8, at] = u_c[w]
    ys_ref[2 * i] = gathered(dot_t(u_ref[0].astype(BF), tile_a))
    ys_ref[2 * i + 1] = gathered(dot_t(u_ref[1].astype(BF), tile_c))


def first_kernel(
    plane_ref, wide_ref, cond_ref, scr_ref, base_ref, op_ref, res_ref,
    xs_ref, ys_ref, t_ref, u_ref, rs_ref, half_ref,
):
    for e in range(6):
        op_ref[0, 768 + 16 * e : 784 + 16 * e, :] = cond_ref[e, :, 0:128]
        op_ref[1, 768 + 16 * e : 784 + 16 * e, :] = cond_ref[e, :, 128:256]
    for part in range(4):
        tail = wide_ref[part, 96:112, :].astype(F32)
        for e in range(6):
            xs_ref[e, 2 * part : 2 * part + 2, :] = tail[2 * e : 2 * e + 2, :]

    def one(i, carry):
        slot = plane_ref[lax.axis_index(PLANE), 0, 8 + i]
        total = jnp.zeros((256, 256), F32)
        for part in range(4):
            at = aligned(i * 32, 16)
            a = wide_ref[part, pl.ds(at, 16), :]
            b = wide_ref[part, pl.ds(at + 16, 16), :]
            left = jnp.concatenate([a[v : v + 1, :] * b for v in range(16)], axis=0)
            total = total + dot(left, scr_ref[slot, part * 256 : (part + 1) * 256, :])
        total = total.astype(BF)
        at = aligned(i * 256, 256)
        op_ref[0, pl.ds(at, 256), :] = total[:, 0:128]
        op_ref[1, pl.ds(at, 256), :] = total[:, 128:256]
        total = total.astype(F32)
        half_ref[2 * i] = total[:, 0:128]
        half_ref[2 * i + 1] = total[:, 128:256]
        apply_pair(i, half_ref, cond_ref, xs_ref, ys_ref, t_ref, u_ref)
        return carry

    for i in range(3):
        one(i, 0)
    for part in range(4):
        for e in range(6):
            rs_ref[part, 2 * e : 2 * e + 2, :] = ys_ref[e, 2 * part : 2 * part + 2, :]
        mine = (lax.axis_index("y") == part).astype(F32)
        rs_ref[part, 12:16, :] = base_ref[...] * mine
    for peer in range(8):
        for part in range(4):
            res_ref[4 * peer + part] = rs_ref[part].astype(BF)


def middle_kernel(route_ref, got_ref, out_ref):
    peers = []
    for peer in range(8):
        total = got_ref[4 * peer].astype(F32)
        for part in range(1, 4):
            total = total + got_ref[4 * peer + part].astype(F32)
        peers.append(total.astype(BF))
    full = dot(route_ref[...], jnp.concatenate(peers, axis=0))
    out_ref[...] = full.astype(BF).reshape(16, 16, 256)


def picker(rows, columns):
    row = lax.broadcasted_iota(jnp.int32, (rows, columns), 0)
    return (lax.rem(row, 16) == lax.rem(lanes(rows, columns), 16)).astype(BF)


def second_kernel(
    got_ref, own_ref, op_ref, left_ref, right_ref, far_ref, rest_ref, out_ref, own_x_ref,
    x_ref, y_ref, t_ref, ua_ref, uc_ref, rs_ref, ds_ref,
):
    total = got_ref[0].astype(F32)
    for z in range(1, 16):
        total = total + got_ref[z].astype(F32)
    own_x_ref[...] = total[12:16, :]
    parts = density_of(own_ref, [total[12 + 2 * s : 14 + 2 * s, :].astype(BF) for s in range(2)])
    for part in range(4):
        for h in range(2):
            at = 4 * part + 2 * h
            ds_ref[at : at + 2, :] = parts[part][:, 128 * h : 128 * h + 128]

    here = lanes(16, 256) // 16 == lax.broadcasted_iota(jnp.int32, (16, 256), 0)
    rows = [jnp.where(here, total[k : k + 1, :], 0.0).astype(BF) for k in range(12)]
    x_ref[...] = dot(jnp.concatenate(rows, axis=0), picker(256, 16)).astype(BF)

    chunks = [(ref, h) for ref in (op_ref, left_ref, right_ref) for h in range(2)]
    chunks += [(far_ref, 0), (rest_ref, 0)]

    def one(p, carry):
        at = aligned(p * 64, 64)
        conds = []
        for end in range(2):
            row = aligned(768 + p * 32 + end * 16, 16)
            conds.append(
                jnp.concatenate([ref[h, pl.ds(row, 16), :] for ref, h in chunks], axis=1)
            )
            t_ref[end] = dot(x_ref[pl.ds(aligned(at + 32 * end, 32), 32), :], conds[end])
        for k, (ref, h) in enumerate(chunks):
            span = slice(128 * k, 128 * k + 128)
            t_c = [t_ref[1, 8 * g : 8 * g + 8, span] for g in range(4)]
            sums = [None] * 4
            for v in range(16):
                tile = ref[h, pl.ds(aligned(p * 256 + 16 * v, 16), 16), :].astype(F32)
                lo, hi = tile[0:8, :], tile[8:16, :]
                for n in range(2):
                    ua_ref[128 * n + 8 * v : 128 * n + 8 * v + 8, span] = (
                        lo * t_c[2 * n] + hi * t_c[2 * n + 1]
                    )
                    t_a = jnp.broadcast_to(
                        t_ref[0, 16 * n + v : 16 * n + v + 1, span], (8, 128)
                    )
                    for g, part in ((2 * n, lo * t_a), (2 * n + 1, hi * t_a)):
                        sums[g] = part if v == 0 else sums[g] + part
            for g in range(4):
                uc_ref[8 * g : 8 * g + 8, span] = sums[g]
        first = dot_t(ua_ref[...].astype(BF), conds[0])
        y_ref[pl.ds(at, 32), :] = jnp.sum(first.reshape(32, 8, 16), axis=1)
        y_ref[pl.ds(aligned(at + 32, 32), 32), :] = dot_t(uc_ref[...].astype(BF), conds[1])
        return carry

    for p in range(3):
        one(p, 0)
    full = dot(y_ref[...].astype(BF), picker(16, 256)).reshape(12, 16, 256)
    rs_ref[0:12, :] = jnp.sum(jnp.where(here[None], full, 0.0), axis=1)
    rs_ref[12:16, :] = jnp.zeros((4, 256), F32)
    for peer in range(8):
        out_ref[peer, :, 0:256] = rs_ref[...].astype(BF)
        out_ref[peer, :, 256:384] = ds_ref[...].astype(BF)


def return_kernel(back_ref, got_ref, out_ref, buf_ref):
    full = dot(back_ref[...], got_ref[:, :, 0:256].reshape(128, 256))
    total = got_ref[0, :, 256:384].astype(F32)
    for peer in range(1, 8):
        total = total + got_ref[peer, :, 256:384].astype(F32)
    for part in range(4):
        for h in range(2):
            at = 4 * part + 2 * h
            span = slice(128 * h, 128 * h + 128)
            buf_ref[0, 2 * part : 2 * part + 2, span] = total[at : at + 2, :]
    for z in range(16):
        if z:
            buf_ref[z, :, 0:256] = buf_ref[0, :, 0:256]
        for h in range(2):
            span = slice(128 * h, 128 * h + 128)
            buf_ref[z, 4 * h : 4 * h + 4, 256:384] = full[4 * z : 4 * z + 4, span]
    out_ref[...] = buf_ref[...].astype(BF)


def last_kernel(cheb_ref, got_ref, own_ref, bare_ref, held_ref, own_x_ref, out_ref):
    total = got_ref[0].astype(F32)
    for z in range(1, 16):
        total = total + got_ref[z].astype(F32)
    dens = [total[2 * part : 2 * part + 2, 0:256] for part in range(4)]
    rows = jnp.concatenate([total[0:4, 256:384], total[4:8, 256:384]], axis=1)
    terms = bare_of(own_ref, bare_ref, dens)
    for s in range(2):
        x = own_x_ref[2 * s : 2 * s + 2, :]
        t = held_ref[2 * s : 2 * s + 2, :]
        applied = (
            held_ref[4 + s : 5 + s, :] * x.astype(BF).astype(F32)
            + 2.0 * terms[s]
            + rows[2 * s : 2 * s + 2, :]
        )
        second = 2.0 * applied - t
        out_ref[:, s, :] = cheb_ref[0] * t + cheb_ref[1] * x + cheb_ref[2] * second


def body(orbitals, transition, trial, screened, bare, cheb, pair_k, pair_slot, k_order):
    far_bare = stay(bare)
    ids, held = call(
        info_kernel,
        [((8, 1, 128), jnp.int32), ((8, 256), F32)],
        (),
        [
            pltpu.SMEM((3,), jnp.int32),
            pltpu.SMEM((3,), jnp.int32),
            pltpu.VMEM((1, 256), jnp.int32),
            pltpu.VMEM((2, 2, 256), F32),
            pltpu.VMEM((2, 256), F32),
            pltpu.SemaphoreType.DMA((5,)),
        ],
        range(5),
    )(*map(stay, (pair_k, pair_slot, k_order.reshape(1, -1), trial, transition)))
    plane = exchange(ids, PLANE)
    own = lax.all_gather(orbitals, "y")
    (packed,) = call(pack_kernel, [((80, 256), BF)], (), [pltpu.VMEM((16, 256), F32)])(held, own)
    gat = lax.all_gather(packed, "z")
    twin = swap(gat)
    chosen, column = call(
        select_kernel,
        [((4, 224, 256), BF), ((8, 256), F32)],
        (0,),
        [pltpu.VMEM((128, 512), F32)],
    )(plane, gat, twin)
    got = exchange(chosen, "x")
    (scr,) = call(
        fetch_kernel, [(screened.shape, BF)], (), [pltpu.SemaphoreType.DMA(())], (0,)
    )(stay(screened))
    val, cond, dens = call(
        accept_kernel,
        [((4, 112, 256), BF), ((6, 16, 256), BF), ((8, 256), F32)],
        (0,),
        [pltpu.VMEM((16, 256), F32)],
    )(plane, got)
    wide = exchange(val, "y")
    base, route, back = call(
        base_kernel,
        [((4, 256), F32), ((256, 128), BF), ((64, 128), BF)],
        (0,),
        [
            pltpu.VMEM((4, 256), F32),
            pltpu.VMEM((128, 256), F32),
            pltpu.VMEM(bare.shape, BF),
            pltpu.SemaphoreType.DMA(()),
        ],
        (4,),
    )(plane, dens, column, own, far_bare, held)
    work = [
        pltpu.VMEM((6, 8, 256), F32),
        pltpu.VMEM((6, 8, 256), F32),
        pltpu.VMEM((2, 128, 256), F32),
        pltpu.VMEM((2, 128, 256), F32),
        pltpu.VMEM((4, 16, 256), F32),
    ]
    op, res = call(
        first_kernel,
        [((2, 864, 128), BF), ((32, 16, 256), BF)],
        (0,),
        work + [pltpu.VMEM((6, 256, 128), F32)],
    )(plane, wide, cond, scr, base)
    mixed = exchange(res, BLOCK)
    left = shift(op, 1)
    right = shift(op, -1)
    (middle,) = call(middle_kernel, [((16, 16, 256), BF)], ())(route, mixed)
    step = exchange(middle, "z")
    far = shift(left[0], 1)
    rest = shift(right[1], -1)
    out2, own_x = call(
        second_kernel,
        [((8, 16, 384), BF), ((4, 256), F32)],
        (),
        [
            pltpu.VMEM((192, 16), BF),
            pltpu.VMEM((192, 16), F32),
            pltpu.VMEM((2, 32, 1024), F32),
            pltpu.VMEM((256, 1024), F32),
            pltpu.VMEM((32, 1024), F32),
            pltpu.VMEM((16, 256), F32),
            pltpu.VMEM((16, 128), F32),
        ],
    )(step, own, op, left, right, far[None], rest[None])
    (final,) = call(return_kernel, [((16, 8, 384), BF)], (), [pltpu.VMEM((16, 8, 384), F32)])(
        back, exchange(out2, PLANE)
    )
    last = exchange(final, "z")
    (near_bare,) = call(
        fetch_kernel, [(bare.shape, BF)], (), [pltpu.SemaphoreType.DMA(())], (0,)
    )(far_bare)
    (result,) = call(last_kernel, [(trial.shape, F32)], (0,))(
        cheb, last, own, near_bare, held, own_x
    )
    return result


def solution(mesh):
    split = Mesh(mesh.devices.reshape(16, 4, 2, mesh.shape["vert"]), ("z", "x", "c", "y"))
    in_specs = (
        P(PB, None, "y"),
        P(PB, None),
        P("y", PB, None),
        P(PB, None, "y"),
        P(),
        P(),
        P(PB),
        P(PB),
        P(),
    )
    out_specs = P("y", PB, None)
    return jax.shard_map(body, mesh=split, in_specs=in_specs, out_specs=out_specs, check_vma=False)
```

```python
import jax
import jax.numpy as jnp
from jax import lax
from jax.experimental import pallas as pl
from jax.experimental.pallas import tpu as pltpu
from jax.sharding import Mesh
from jax.sharding import PartitionSpec as P


BF = jnp.bfloat16
F32 = jnp.float32
LAST = (((1,), (1,)), ((), ()))
PB = ("z", "x", "c")
PLANE = ("x", "c")
BLOCK = ("x", "c", "y")
LIMIT = 12 << 20


def exchange(blocks, axis):
    return lax.all_to_all(blocks, axis, 0, 0, tiled=True)


def swap(shard):
    return lax.ppermute(shard, "c", [(0, 1), (1, 0)])


def shift(shard, by):
    count = lax.axis_size("y")
    return lax.ppermute(shard, "y", [(k, (k + by) % count) for k in range(count)])


def stay(array):
    return pltpu.with_memory_space_constraint(array, pltpu.HBM)


def aligned(value, by):
    return value if isinstance(value, int) else pl.multiple_of(value, by)


def dot(a, b):
    return jnp.dot(a, b, preferred_element_type=F32)


def dot_t(a, b):
    return lax.dot_general(a, b, LAST, preferred_element_type=F32)


def call(kernel, outs, smem, scratch=(), far=(), limit=LIMIT):
    def space(k):
        return pltpu.SMEM if k in smem else pltpu.HBM if k in far else pltpu.VMEM

    def run(*args):
        specs = [pl.BlockSpec(memory_space=space(k)) for k in range(len(args))]
        return pl.pallas_call(
            kernel,
            out_shape=[jax.ShapeDtypeStruct(s, d) for s, d in outs],
            in_specs=specs,
            out_specs=[
                pl.BlockSpec(memory_space=pltpu.SMEM if len(s) == 1 else pltpu.VMEM)
                for s, _ in outs
            ],
            scratch_shapes=list(scratch),
            compiler_params=pltpu.CompilerParams(vmem_limit_bytes=limit),
            cost_estimate=pl.CostEstimate(flops=0, transcendentals=0, bytes_accessed=4 << 20),
        )(*args)

    return run


def lanes(rows, width):
    return lax.broadcasted_iota(jnp.int32, (rows, width), 1)


def products_of(own_ref, s, part):
    val = own_ref[part, s, 0:16, :]
    cond = own_ref[part, s, 16:32, :]
    pieces = [val[v : v + 1, :] * cond for v in range(16)]
    return jnp.concatenate(pieces, axis=0)


def density_of(own_ref, rows_bf):
    parts = []
    for part in range(4):
        total = dot(rows_bf[0], products_of(own_ref, 0, part))
        total = total + dot(rows_bf[1], products_of(own_ref, 1, part))
        parts.append(total)
    return parts


def bare_of(own_ref, bare_ref, dens):
    pots = []
    for out in range(4):
        total = jnp.zeros((2, 256), F32)
        for part in range(4):
            total = total + dot_t(
                dens[part].astype(BF),
                bare_ref[out * 256 : (out + 1) * 256, part * 256 : (part + 1) * 256],
            )
        pots.append(total.astype(BF))
    terms = []
    for s in range(2):
        total = jnp.zeros((2, 256), F32)
        for part in range(4):
            total = total + dot_t(pots[part], products_of(own_ref, s, part))
        terms.append(total)
    return terms


def copies_kernel(orb_hbm, own_ref, sem):
    copies = [
        pltpu.make_async_copy(orb_hbm, own_ref.at[part], sem.at[part]) for part in range(4)
    ]
    for copy in copies:
        copy.start()
    for copy in copies:
        copy.wait()


def info_kernel(
    pair_hbm, slot_hbm, order_hbm, trial_hbm, trans_hbm,
    ids_ref, held_ref, pair_ref, slot_ref, order_ref, trial_ref, trans_ref, sem,
):
    moves = [
        (pair_hbm, pair_ref), (slot_hbm, slot_ref), (order_hbm, order_ref),
        (trial_hbm, trial_ref), (trans_hbm, trans_ref),
    ]
    copies = [pltpu.make_async_copy(a, b, sem.at[k]) for k, (a, b) in enumerate(moves)]
    for copy in copies:
        copy.start()
    for copy in copies[:3]:
        copy.wait()
    position = lax.axis_index(PB)
    lane = lanes(1, 256)
    short = lanes(1, 128)
    order = order_ref[...]
    ids = jnp.where(short == 6, position * 2, jnp.where(short == 7, position * 2 + 1, 0))
    kind = lax.rem(lane, 16) // 2
    spread_ids = position * 2 + kind - 6
    for i in range(3):
        first = pair_ref[i]
        second = first - position * 2 - slot_ref[i]
        second = jnp.where(second < 0, second + 256, second)
        for h, k in enumerate((first, second)):
            row = jnp.sum(jnp.where(order == k, lane, 0))
            ids = jnp.where(short == 2 * i + h, row, ids)
            spread_ids = jnp.where(kind == 2 * i + h, row, spread_ids)
        ids = jnp.where(short == 8 + i, slot_ref[i], ids)
    for peer in range(8):
        ids_ref[peer] = ids
    for copy in copies[3:]:
        copy.wait()
    held_ref[...] = jnp.zeros((8, 256), F32)
    for s in range(2):
        held_ref[2 * s : 2 * s + 2, :] = trial_ref[:, s, :]
    held_ref[4:6, :] = trans_ref[...]
    held_ref[6:7, :] = spread_ids.astype(F32)


def pack_kernel(held_ref, own_ref, out_ref, tail_ref):
    out_ref[0:64, :] = own_ref[lax.axis_index("y")].reshape(64, 256)
    rows = [held_ref[2 * s : 2 * s + 2, :].astype(BF) for s in range(2)]
    parts = density_of(own_ref, rows)
    tail_ref[...] = jnp.zeros((16, 256), F32)
    for s in range(2):
        tail_ref[2 * s : 2 * s + 2, :] = rows[s].astype(F32)
    for part in range(4):
        tail_ref[4 + 2 * part : 6 + 2 * part, :] = parts[part]
    tail_ref[12:13, :] = held_ref[6:7, :]
    out_ref[64:80, :] = tail_ref[...].astype(BF)


def select_kernel(plane_ref, gat_ref, twin_ref, out_ref, column_ref, pick_ref):
    lane = lanes(1, 512)
    core = lax.axis_index("c")
    held = jnp.zeros((1, 256), F32)
    for z in range(16):
        row = gat_ref[z, 64:80, :].astype(F32)[12:13, :]
        held = jnp.where(lanes(1, 256) // 16 == z, row, held)
    column_ref[...] = jnp.broadcast_to(held, (8, 256))
    pick_ref[...] = jnp.zeros((128, 512), F32)
    for peer in range(4):
        for e in range(6):
            row = plane_ref[2 * peer + core, 0, e]
            z = row // 16
            s = lax.rem(row, 2)
            ours = lax.rem(row // 2, 2) == core
            first = z * 16 + 2 * s + jnp.where(ours, 0, 256)
            for n in range(2):
                at = peer * 32 + 2 * e + n
                pick_ref[at : at + 1, :] = (lane == first + n).astype(F32)
            at = aligned(s * 32, 32)

            @pl.when(ours)
            def _():
                out_ref[peer, 32 * e : 32 * e + 32, :] = gat_ref[z, pl.ds(at, 32), :]

            @pl.when(jnp.logical_not(ours))
            def _():
                out_ref[peer, 32 * e : 32 * e + 32, :] = twin_ref[z, pl.ds(at, 32), :]

        for d in range(8):
            at = peer * 32 + 16 + d
            pick_ref[at : at + 1, :] = (lax.rem(lane, 16) == 4 + d).astype(F32)
    pick = pick_ref[...].astype(BF)
    picked = dot(pick[:, 0:256], gat_ref[:, 64:80, :].reshape(256, 256))
    picked = picked + dot(pick[:, 256:512], twin_ref[:, 64:80, :].reshape(256, 256))
    out_ref[:, 192:224, :] = picked.astype(BF).reshape(4, 32, 256)


def fetch_kernel(far_ref, near_ref, sem):
    copy = pltpu.make_async_copy(far_ref, near_ref, sem)
    copy.start()
    copy.wait()


def accept_kernel(plane_ref, got_ref, val_ref, cond_ref, dens_ref, tail_ref):
    for e in range(6):
        column = lax.rem(plane_ref[lax.axis_index(PLANE), 0, e] // 4, 4)
        val = got_ref[column, 32 * e : 32 * e + 16, :]
        for part in range(4):
            val_ref[part, 16 * e : 16 * e + 16, :] = val
        cond_ref[e] = got_ref[column, 32 * e + 16 : 32 * e + 32, :]
        part = got_ref[column, 192:208, :].astype(F32)
        tail_ref[2 * e : 2 * e + 2, :] = part[2 * e : 2 * e + 2, :]
    tail_ref[12:16, :] = jnp.zeros((4, 256), F32)
    for part in range(4):
        val_ref[part, 96:112, :] = tail_ref[...].astype(BF)
    total = got_ref[0, 208:224, :].astype(F32)
    for peer in range(1, 4):
        total = total + got_ref[peer, 208:224, :].astype(F32)
    dens_ref[...] = total[0:8, :]


def base_kernel(
    plane_ref, dens_ref, column_ref, own_ref, bare_hbm, held_ref,
    base_ref, route_ref, back_ref, base_s, route_s, bare_ref, sem,
):
    copy = pltpu.make_async_copy(bare_hbm, bare_ref, sem)
    copy.start()
    lane = lanes(1, 256)
    held = column_ref[0:1, :].astype(jnp.int32)
    parity = lax.rem(lane, 2)
    z_me = lax.axis_index("z")
    q_me = lax.axis_index(PLANE)
    for peer in range(8):
        for k in range(8):
            row = plane_ref[peer, 0, k] if k < 6 else z_me * 16 + peer * 2 + (k - 6)
            for n in range(2):
                at = peer * 16 + 2 * k + n
                hit = (held == row) & (parity == n)
                route_s[at : at + 1, :] = jnp.where(hit, -1.0 if k < 6 else 1.0, 0.0)
    route_ref[...] = jnp.transpose(route_s[...]).astype(BF)

    wide = lanes(1, 128)
    sent = jnp.full((1, 128), -1, jnp.int32)
    for peer in range(8):
        for e in range(6):
            here = (wide // 16 == peer) & (lax.rem(wide, 16) // 2 == e)
            sent = jnp.where(here, plane_ref[peer, 0, e], sent)
    row = lax.broadcasted_iota(jnp.int32, (64, 128), 0)
    target = (row // 4) * 16 + q_me * 2 + lax.rem(row, 4) // 2
    hit = (sent == target) & (lax.rem(row, 2) == lax.rem(lanes(64, 128), 2))
    back_ref[...] = jnp.where(hit, -1.0, 0.0).astype(BF)

    copy.wait()
    dens = [dens_ref[2 * part : 2 * part + 2, :] for part in range(4)]
    terms = bare_of(own_ref, bare_ref, dens)
    for s in range(2):
        x = held_ref[2 * s : 2 * s + 2, :].astype(BF).astype(F32)
        base_s[2 * s : 2 * s + 2, :] = held_ref[4 + s : 5 + s, :] * x + 2.0 * terms[s]
    base_ref[...] = base_s[...]


def spread(x):
    rows = jnp.concatenate([x] * 16, axis=0)
    group = lax.broadcasted_iota(jnp.int32, (128, 256), 0) // 8
    return jnp.where(group == lanes(128, 256) // 16, rows, 0.0).astype(BF)


def gathered(full):
    group = lax.broadcasted_iota(jnp.int32, (128, 256), 0) // 8
    kept = jnp.where(group == lanes(128, 256) // 16, full, 0.0)
    total = kept[0:8, :]
    for v in range(1, 16):
        total = total + kept[8 * v : 8 * v + 8, :]
    return total


def apply_pair(i, half_ref, cond_ref, xs_ref, ys_ref, t_ref, u_ref):
    tile_a = jnp.concatenate([cond_ref[2 * i]] * 16, axis=0)
    tile_c = jnp.concatenate([cond_ref[2 * i + 1]] * 16, axis=0)
    t_ref[0] = dot(spread(xs_ref[2 * i]), tile_a)
    t_ref[1] = dot(spread(xs_ref[2 * i + 1]), tile_c)
    for part in range(2):
        at = slice(128 * part, 128 * part + 128)
        t_c = [t_ref[1, 8 * w : 8 * w + 8, at] for w in range(16)]
        u_c = [None] * 16
        for v in range(16):
            t_a = t_ref[0, 8 * v : 8 * v + 8, at]
            sums = [None] * 2
            for w in range(16):
                row = 16 * v + w
                h = jnp.broadcast_to(half_ref[2 * i + part, row : row + 1, :], (8, 128))
                one, two = h * t_c[w], h * t_a
                sums[w % 2] = one if w < 2 else sums[w % 2] + one
                u_c[w] = two if v == 0 else u_c[w] + two
            u_ref[0, 8 * v : 8 * v + 8, at] = sums[0] + sums[1]
        for w in range(16):
            u_ref[1, 8 * w : 8 * w + 8, at] = u_c[w]
    ys_ref[2 * i] = gathered(dot_t(u_ref[0].astype(BF), tile_a))
    ys_ref[2 * i + 1] = gathered(dot_t(u_ref[1].astype(BF), tile_c))


def first_kernel(
    plane_ref, wide_ref, cond_ref, scr_ref, base_ref, op_ref, res_ref,
    xs_ref, ys_ref, t_ref, u_ref, rs_ref, half_ref,
):
    for e in range(6):
        op_ref[0, 768 + 16 * e : 784 + 16 * e, :] = cond_ref[e, :, 0:128]
        op_ref[1, 768 + 16 * e : 784 + 16 * e, :] = cond_ref[e, :, 128:256]
    for part in range(4):
        tail = wide_ref[part, 96:112, :].astype(F32)
        for e in range(6):
            xs_ref[e, 2 * part : 2 * part + 2, :] = tail[2 * e : 2 * e + 2, :]

    def one(i, carry):
        slot = plane_ref[lax.axis_index(PLANE), 0, 8 + i]
        total = jnp.zeros((256, 256), F32)
        for part in range(4):
            at = aligned(i * 32, 16)
            a = wide_ref[part, pl.ds(at, 16), :]
            b = wide_ref[part, pl.ds(at + 16, 16), :]
            left = jnp.concatenate([a[v : v + 1, :] * b for v in range(16)], axis=0)
            total = total + dot(left, scr_ref[slot, part * 256 : (part + 1) * 256, :])
        total = total.astype(BF)
        at = aligned(i * 256, 256)
        op_ref[0, pl.ds(at, 256), :] = total[:, 0:128]
        op_ref[1, pl.ds(at, 256), :] = total[:, 128:256]
        total = total.astype(F32)
        half_ref[2 * i] = total[:, 0:128]
        half_ref[2 * i + 1] = total[:, 128:256]
        apply_pair(i, half_ref, cond_ref, xs_ref, ys_ref, t_ref, u_ref)
        return carry

    for i in range(3):
        one(i, 0)
    for part in range(4):
        for e in range(6):
            rs_ref[part, 2 * e : 2 * e + 2, :] = ys_ref[e, 2 * part : 2 * part + 2, :]
        mine = (lax.axis_index("y") == part).astype(F32)
        rs_ref[part, 12:16, :] = base_ref[...] * mine
    for peer in range(8):
        for part in range(4):
            res_ref[4 * peer + part] = rs_ref[part].astype(BF)


def middle_kernel(route_ref, got_ref, out_ref):
    peers = []
    for peer in range(8):
        total = got_ref[4 * peer].astype(F32)
        for part in range(1, 4):
            total = total + got_ref[4 * peer + part].astype(F32)
        peers.append(total.astype(BF))
    full = dot(route_ref[...], jnp.concatenate(peers, axis=0))
    out_ref[...] = full.astype(BF).reshape(16, 16, 256)


def picker(rows, columns):
    row = lax.broadcasted_iota(jnp.int32, (rows, columns), 0)
    return (lax.rem(row, 16) == lax.rem(lanes(rows, columns), 16)).astype(BF)


def second_kernel(
    got_ref, own_ref, op_ref, left_ref, right_ref, far_ref, rest_ref, out_ref, own_x_ref,
    x_ref, y_ref, t_ref, ua_ref, uc_ref, rs_ref, ds_ref,
):
    total = got_ref[0].astype(F32)
    for z in range(1, 16):
        total = total + got_ref[z].astype(F32)
    own_x_ref[...] = total[12:16, :]
    parts = density_of(own_ref, [total[12 + 2 * s : 14 + 2 * s, :].astype(BF) for s in range(2)])
    for part in range(4):
        for h in range(2):
            at = 4 * part + 2 * h
            ds_ref[at : at + 2, :] = parts[part][:, 128 * h : 128 * h + 128]

    here = lanes(16, 256) // 16 == lax.broadcasted_iota(jnp.int32, (16, 256), 0)
    rows = [jnp.where(here, total[k : k + 1, :], 0.0).astype(BF) for k in range(12)]
    x_ref[...] = dot(jnp.concatenate(rows, axis=0), picker(256, 16)).astype(BF)

    chunks = [(ref, h) for ref in (op_ref, left_ref, right_ref) for h in range(2)]
    chunks += [(far_ref, 0), (rest_ref, 0)]

    def one(p, carry):
        at = aligned(p * 64, 64)
        conds = []
        for end in range(2):
            row = aligned(768 + p * 32 + end * 16, 16)
            conds.append(
                jnp.concatenate([ref[h, pl.ds(row, 16), :] for ref, h in chunks], axis=1)
            )
            t_ref[end] = dot(x_ref[pl.ds(aligned(at + 32 * end, 32), 32), :], conds[end])
        for k, (ref, h) in enumerate(chunks):
            span = slice(128 * k, 128 * k + 128)
            t_c = [t_ref[1, 8 * g : 8 * g + 8, span] for g in range(4)]
            sums = [None] * 4
            for v in range(16):
                tile = ref[h, pl.ds(aligned(p * 256 + 16 * v, 16), 16), :].astype(F32)
                lo, hi = tile[0:8, :], tile[8:16, :]
                for n in range(2):
                    ua_ref[128 * n + 8 * v : 128 * n + 8 * v + 8, span] = (
                        lo * t_c[2 * n] + hi * t_c[2 * n + 1]
                    )
                    t_a = jnp.broadcast_to(
                        t_ref[0, 16 * n + v : 16 * n + v + 1, span], (8, 128)
                    )
                    for g, part in ((2 * n, lo * t_a), (2 * n + 1, hi * t_a)):
                        sums[g] = part if v == 0 else sums[g] + part
            for g in range(4):
                uc_ref[8 * g : 8 * g + 8, span] = sums[g]
        first = dot_t(ua_ref[...].astype(BF), conds[0])
        y_ref[pl.ds(at, 32), :] = jnp.sum(first.reshape(32, 8, 16), axis=1)
        y_ref[pl.ds(aligned(at + 32, 32), 32), :] = dot_t(uc_ref[...].astype(BF), conds[1])
        return carry

    for p in range(3):
        one(p, 0)
    full = dot(y_ref[...].astype(BF), picker(16, 256)).reshape(12, 16, 256)
    rs_ref[0:12, :] = jnp.sum(jnp.where(here[None], full, 0.0), axis=1)
    rs_ref[12:16, :] = jnp.zeros((4, 256), F32)
    for peer in range(8):
        out_ref[peer, :, 0:256] = rs_ref[...].astype(BF)
        out_ref[peer, :, 256:384] = ds_ref[...].astype(BF)


def return_kernel(back_ref, got_ref, out_ref, buf_ref):
    full = dot(back_ref[...], got_ref[:, :, 0:256].reshape(128, 256))
    total = got_ref[0, :, 256:384].astype(F32)
    for peer in range(1, 8):
        total = total + got_ref[peer, :, 256:384].astype(F32)
    for part in range(4):
        for h in range(2):
            at = 4 * part + 2 * h
            span = slice(128 * h, 128 * h + 128)
            buf_ref[0, 2 * part : 2 * part + 2, span] = total[at : at + 2, :]
    for z in range(16):
        if z:
            buf_ref[z, :, 0:256] = buf_ref[0, :, 0:256]
        for h in range(2):
            span = slice(128 * h, 128 * h + 128)
            buf_ref[z, 4 * h : 4 * h + 4, 256:384] = full[4 * z : 4 * z + 4, span]
    out_ref[...] = buf_ref[...].astype(BF)


def last_kernel(cheb_ref, got_ref, own_ref, bare_ref, held_ref, own_x_ref, out_ref):
    total = got_ref[0].astype(F32)
    for z in range(1, 16):
        total = total + got_ref[z].astype(F32)
    dens = [total[2 * part : 2 * part + 2, 0:256] for part in range(4)]
    rows = jnp.concatenate([total[0:4, 256:384], total[4:8, 256:384]], axis=1)
    terms = bare_of(own_ref, bare_ref, dens)
    for s in range(2):
        x = own_x_ref[2 * s : 2 * s + 2, :]
        t = held_ref[2 * s : 2 * s + 2, :]
        applied = (
            held_ref[4 + s : 5 + s, :] * x.astype(BF).astype(F32)
            + 2.0 * terms[s]
            + rows[2 * s : 2 * s + 2, :]
        )
        second = 2.0 * applied - t
        out_ref[:, s, :] = cheb_ref[0] * t + cheb_ref[1] * x + cheb_ref[2] * second


def body(orbitals, transition, trial, screened, bare, cheb, pair_k, pair_slot, k_order):
    (copies,) = call(
        copies_kernel, [((4, 2, 32, 256), BF)], (), [pltpu.SemaphoreType.DMA((4,))], (0,)
    )(stay(orbitals))
    far_bare = stay(bare)
    own = exchange(copies, "y")
    ids, held = call(
        info_kernel,
        [((8, 1, 128), jnp.int32), ((8, 256), F32)],
        (),
        [
            pltpu.SMEM((3,), jnp.int32),
            pltpu.SMEM((3,), jnp.int32),
            pltpu.VMEM((1, 256), jnp.int32),
            pltpu.VMEM((2, 2, 256), F32),
            pltpu.VMEM((2, 256), F32),
            pltpu.SemaphoreType.DMA((5,)),
        ],
        range(5),
    )(*map(stay, (pair_k, pair_slot, k_order.reshape(1, -1), trial, transition)))
    plane = exchange(ids, PLANE)
    (packed,) = call(pack_kernel, [((80, 256), BF)], (), [pltpu.VMEM((16, 256), F32)])(held, own)
    gat = lax.all_gather(packed, "z")
    twin = swap(gat)
    chosen, column = call(
        select_kernel,
        [((4, 224, 256), BF), ((8, 256), F32)],
        (0,),
        [pltpu.VMEM((128, 512), F32)],
    )(plane, gat, twin)
    got = exchange(chosen, "x")
    (scr,) = call(
        fetch_kernel, [(screened.shape, BF)], (), [pltpu.SemaphoreType.DMA(())], (0,)
    )(stay(screened))
    val, cond, dens = call(
        accept_kernel,
        [((4, 112, 256), BF), ((6, 16, 256), BF), ((8, 256), F32)],
        (0,),
        [pltpu.VMEM((16, 256), F32)],
    )(plane, got)
    wide = exchange(val, "y")
    base, route, back = call(
        base_kernel,
        [((4, 256), F32), ((256, 128), BF), ((64, 128), BF)],
        (0,),
        [
            pltpu.VMEM((4, 256), F32),
            pltpu.VMEM((128, 256), F32),
            pltpu.VMEM(bare.shape, BF),
            pltpu.SemaphoreType.DMA(()),
        ],
        (4,),
    )(plane, dens, column, own, far_bare, held)
    work = [
        pltpu.VMEM((6, 8, 256), F32),
        pltpu.VMEM((6, 8, 256), F32),
        pltpu.VMEM((2, 128, 256), F32),
        pltpu.VMEM((2, 128, 256), F32),
        pltpu.VMEM((4, 16, 256), F32),
    ]
    op, res = call(
        first_kernel,
        [((2, 864, 128), BF), ((32, 16, 256), BF)],
        (0,),
        work + [pltpu.VMEM((6, 256, 128), F32)],
    )(plane, wide, cond, scr, base)
    mixed = exchange(res, BLOCK)
    left = shift(op, 1)
    right = shift(op, -1)
    (middle,) = call(middle_kernel, [((16, 16, 256), BF)], ())(route, mixed)
    step = exchange(middle, "z")
    far = shift(left[0], 1)
    rest = shift(right[1], -1)
    out2, own_x = call(
        second_kernel,
        [((8, 16, 384), BF), ((4, 256), F32)],
        (),
        [
            pltpu.VMEM((192, 16), BF),
            pltpu.VMEM((192, 16), F32),
            pltpu.VMEM((2, 32, 1024), F32),
            pltpu.VMEM((256, 1024), F32),
            pltpu.VMEM((32, 1024), F32),
            pltpu.VMEM((16, 256), F32),
            pltpu.VMEM((16, 128), F32),
        ],
    )(step, own, op, left, right, far[None], rest[None])
    returned = exchange(out2, PLANE)
    (final,) = call(return_kernel, [((16, 8, 384), BF)], (), [pltpu.VMEM((16, 8, 384), F32)])(
        back, returned
    )
    last = exchange(final, "z")
    (near_bare,) = call(
        fetch_kernel, [(bare.shape, BF)], (), [pltpu.SemaphoreType.DMA(())], (0,)
    )(far_bare)
    (result,) = call(last_kernel, [(trial.shape, F32)], (0,))(
        cheb, last, own, near_bare, held, own_x
    )
    return result


def solution(mesh):
    split = Mesh(mesh.devices.reshape(16, 4, 2, mesh.shape["vert"]), ("z", "x", "c", "y"))
    in_specs = (
        P(PB, None, "y"),
        P(PB, None),
        P("y", PB, None),
        P(PB, None, "y"),
        P(),
        P(),
        P(PB),
        P(PB),
        P(),
    )
    out_specs = P("y", PB, None)
    return jax.shard_map(body, mesh=split, in_specs=in_specs, out_specs=out_specs, check_vma=False)
```

```python
import jax
import jax.numpy as jnp
from jax import lax
from jax.experimental import pallas as pl
from jax.experimental.pallas import tpu as pltpu
from jax.sharding import Mesh
from jax.sharding import PartitionSpec as P


BF = jnp.bfloat16
F32 = jnp.float32
LAST = (((1,), (1,)), ((), ()))
PB = ("z", "x", "c")
PLANE = ("x", "c")
BLOCK = ("x", "c", "y")
LIMIT = 12 << 20


def exchange(blocks, axis):
    return lax.all_to_all(blocks, axis, 0, 0, tiled=True)


def swap(shard):
    return lax.ppermute(shard, "c", [(0, 1), (1, 0)])


def shift(shard, by):
    count = lax.axis_size("y")
    return lax.ppermute(shard, "y", [(k, (k + by) % count) for k in range(count)])


def stay(array):
    return pltpu.with_memory_space_constraint(array, pltpu.HBM)


def aligned(value, by):
    return value if isinstance(value, int) else pl.multiple_of(value, by)


def dot(a, b):
    return jnp.dot(a, b, preferred_element_type=F32)


def dot_t(a, b):
    return lax.dot_general(a, b, LAST, preferred_element_type=F32)


def call(kernel, outs, smem, scratch=(), far=(), limit=LIMIT, out_space=pltpu.VMEM):
    def space(k):
        return pltpu.SMEM if k in smem else pltpu.HBM if k in far else pltpu.VMEM

    def run(*args):
        specs = [pl.BlockSpec(memory_space=space(k)) for k in range(len(args))]
        return pl.pallas_call(
            kernel,
            out_shape=[jax.ShapeDtypeStruct(s, d) for s, d in outs],
            in_specs=specs,
            out_specs=[
                pl.BlockSpec(memory_space=pltpu.SMEM if len(s) == 1 else out_space)
                for s, _ in outs
            ],
            scratch_shapes=list(scratch),
            compiler_params=pltpu.CompilerParams(vmem_limit_bytes=limit),
            cost_estimate=pl.CostEstimate(flops=0, transcendentals=0, bytes_accessed=4 << 20),
        )(*args)

    return run


def lanes(rows, width):
    return lax.broadcasted_iota(jnp.int32, (rows, width), 1)


def products_of(own_ref, s, part):
    val = own_ref[part, s, 0:16, :]
    cond = own_ref[part, s, 16:32, :]
    pieces = [val[v : v + 1, :] * cond for v in range(16)]
    return jnp.concatenate(pieces, axis=0)


def density_of(own_ref, rows_bf):
    parts = []
    for part in range(4):
        total = dot(rows_bf[0], products_of(own_ref, 0, part))
        total = total + dot(rows_bf[1], products_of(own_ref, 1, part))
        parts.append(total)
    return parts


def bare_of(own_ref, bare_ref, dens):
    pots = []
    for out in range(4):
        total = jnp.zeros((2, 256), F32)
        for part in range(4):
            total = total + dot_t(
                dens[part].astype(BF),
                bare_ref[out * 256 : (out + 1) * 256, part * 256 : (part + 1) * 256],
            )
        pots.append(total.astype(BF))
    terms = []
    for s in range(2):
        total = jnp.zeros((2, 256), F32)
        for part in range(4):
            total = total + dot_t(pots[part], products_of(own_ref, s, part))
        terms.append(total)
    return terms


def copies_kernel(orb_hbm, own_ref, sem):
    copies = [
        pltpu.make_async_copy(orb_hbm, own_ref.at[part], sem.at[part]) for part in range(4)
    ]
    for copy in copies:
        copy.start()
    for copy in copies:
        copy.wait()


def info_kernel(
    pair_hbm, slot_hbm, order_hbm, trial_hbm, trans_hbm,
    ids_ref, held_ref, pair_ref, slot_ref, order_ref, trial_ref, trans_ref, sem,
):
    moves = [
        (pair_hbm, pair_ref), (slot_hbm, slot_ref), (order_hbm, order_ref),
        (trial_hbm, trial_ref), (trans_hbm, trans_ref),
    ]
    copies = [pltpu.make_async_copy(a, b, sem.at[k]) for k, (a, b) in enumerate(moves)]
    for copy in copies:
        copy.start()
    for copy in copies[:3]:
        copy.wait()
    position = lax.axis_index(PB)
    lane = lanes(1, 256)
    short = lanes(1, 128)
    order = order_ref[...]
    ids = jnp.where(short == 6, position * 2, jnp.where(short == 7, position * 2 + 1, 0))
    kind = lax.rem(lane, 16) // 2
    spread_ids = position * 2 + kind - 6
    for i in range(3):
        first = pair_ref[i]
        second = first - position * 2 - slot_ref[i]
        second = jnp.where(second < 0, second + 256, second)
        for h, k in enumerate((first, second)):
            row = jnp.sum(jnp.where(order == k, lane, 0))
            ids = jnp.where(short == 2 * i + h, row, ids)
            spread_ids = jnp.where(kind == 2 * i + h, row, spread_ids)
        ids = jnp.where(short == 8 + i, slot_ref[i], ids)
    for peer in range(8):
        ids_ref[peer] = ids
    for copy in copies[3:]:
        copy.wait()
    held_ref[...] = jnp.zeros((8, 256), F32)
    for s in range(2):
        held_ref[2 * s : 2 * s + 2, :] = trial_ref[:, s, :]
    held_ref[4:6, :] = trans_ref[...]
    held_ref[6:7, :] = spread_ids.astype(F32)


def pack_kernel(held_ref, own_ref, out_ref, tail_ref):
    out_ref[0:64, :] = own_ref[lax.axis_index("y")].reshape(64, 256)
    rows = [held_ref[2 * s : 2 * s + 2, :].astype(BF) for s in range(2)]
    parts = density_of(own_ref, rows)
    tail_ref[...] = jnp.zeros((16, 256), F32)
    for s in range(2):
        tail_ref[2 * s : 2 * s + 2, :] = rows[s].astype(F32)
    for part in range(4):
        tail_ref[4 + 2 * part : 6 + 2 * part, :] = parts[part]
    tail_ref[12:13, :] = held_ref[6:7, :]
    out_ref[64:80, :] = tail_ref[...].astype(BF)


def select_kernel(plane_ref, gat_ref, twin_ref, out_ref, column_ref, pick_ref):
    lane = lanes(1, 512)
    core = lax.axis_index("c")
    held = jnp.zeros((1, 256), F32)
    for z in range(16):
        row = gat_ref[z, 64:80, :].astype(F32)[12:13, :]
        held = jnp.where(lanes(1, 256) // 16 == z, row, held)
    column_ref[...] = jnp.broadcast_to(held, (8, 256))
    pick_ref[...] = jnp.zeros((128, 512), F32)
    for peer in range(4):
        for e in range(6):
            row = plane_ref[2 * peer + core, 0, e]
            z = row // 16
            s = lax.rem(row, 2)
            ours = lax.rem(row // 2, 2) == core
            first = z * 16 + 2 * s + jnp.where(ours, 0, 256)
            for n in range(2):
                at = peer * 32 + 2 * e + n
                pick_ref[at : at + 1, :] = (lane == first + n).astype(F32)
            at = aligned(s * 32, 32)

            @pl.when(ours)
            def _():
                out_ref[peer, 32 * e : 32 * e + 32, :] = gat_ref[z, pl.ds(at, 32), :]

            @pl.when(jnp.logical_not(ours))
            def _():
                out_ref[peer, 32 * e : 32 * e + 32, :] = twin_ref[z, pl.ds(at, 32), :]

        for d in range(8):
            at = peer * 32 + 16 + d
            pick_ref[at : at + 1, :] = (lax.rem(lane, 16) == 4 + d).astype(F32)
    pick = pick_ref[...].astype(BF)
    picked = dot(pick[:, 0:256], gat_ref[:, 64:80, :].reshape(256, 256))
    picked = picked + dot(pick[:, 256:512], twin_ref[:, 64:80, :].reshape(256, 256))
    out_ref[:, 192:224, :] = picked.astype(BF).reshape(4, 32, 256)


def fetch_kernel(far_ref, near_ref, sem):
    copy = pltpu.make_async_copy(far_ref, near_ref, sem)
    copy.start()
    copy.wait()


def accept_kernel(plane_ref, got_ref, val_ref, cond_ref, dens_ref, tail_ref):
    for e in range(6):
        column = lax.rem(plane_ref[lax.axis_index(PLANE), 0, e] // 4, 4)
        val = got_ref[column, 32 * e : 32 * e + 16, :]
        for part in range(4):
            val_ref[part, 16 * e : 16 * e + 16, :] = val
        cond_ref[e] = got_ref[column, 32 * e + 16 : 32 * e + 32, :]
        part = got_ref[column, 192:208, :].astype(F32)
        tail_ref[2 * e : 2 * e + 2, :] = part[2 * e : 2 * e + 2, :]
    tail_ref[12:16, :] = jnp.zeros((4, 256), F32)
    for part in range(4):
        val_ref[part, 96:112, :] = tail_ref[...].astype(BF)
    total = got_ref[0, 208:224, :].astype(F32)
    for peer in range(1, 4):
        total = total + got_ref[peer, 208:224, :].astype(F32)
    dens_ref[...] = total[0:8, :]


def base_kernel(
    plane_ref, dens_ref, column_ref, own_ref, bare_hbm, held_ref,
    base_ref, route_ref, back_ref, base_s, route_s, bare_ref, sem,
):
    copy = pltpu.make_async_copy(bare_hbm, bare_ref, sem)
    copy.start()
    lane = lanes(1, 256)
    held = column_ref[0:1, :].astype(jnp.int32)
    parity = lax.rem(lane, 2)
    z_me = lax.axis_index("z")
    q_me = lax.axis_index(PLANE)
    for peer in range(8):
        for k in range(8):
            row = plane_ref[peer, 0, k] if k < 6 else z_me * 16 + peer * 2 + (k - 6)
            for n in range(2):
                at = peer * 16 + 2 * k + n
                hit = (held == row) & (parity == n)
                route_s[at : at + 1, :] = jnp.where(hit, -1.0 if k < 6 else 1.0, 0.0)
    route_ref[...] = jnp.transpose(route_s[...]).astype(BF)

    wide = lanes(1, 128)
    sent = jnp.full((1, 128), -1, jnp.int32)
    for peer in range(8):
        for e in range(6):
            here = (wide // 16 == peer) & (lax.rem(wide, 16) // 2 == e)
            sent = jnp.where(here, plane_ref[peer, 0, e], sent)
    row = lax.broadcasted_iota(jnp.int32, (64, 128), 0)
    target = (row // 4) * 16 + q_me * 2 + lax.rem(row, 4) // 2
    hit = (sent == target) & (lax.rem(row, 2) == lax.rem(lanes(64, 128), 2))
    back_ref[...] = jnp.where(hit, -1.0, 0.0).astype(BF)

    copy.wait()
    dens = [dens_ref[2 * part : 2 * part + 2, :] for part in range(4)]
    terms = bare_of(own_ref, bare_ref, dens)
    for s in range(2):
        x = held_ref[2 * s : 2 * s + 2, :].astype(BF).astype(F32)
        base_s[2 * s : 2 * s + 2, :] = held_ref[4 + s : 5 + s, :] * x + 2.0 * terms[s]
    base_ref[...] = base_s[...]


def spread(x):
    rows = jnp.concatenate([x] * 16, axis=0)
    group = lax.broadcasted_iota(jnp.int32, (128, 256), 0) // 8
    return jnp.where(group == lanes(128, 256) // 16, rows, 0.0).astype(BF)


def gathered(full):
    group = lax.broadcasted_iota(jnp.int32, (128, 256), 0) // 8
    kept = jnp.where(group == lanes(128, 256) // 16, full, 0.0)
    total = kept[0:8, :]
    for v in range(1, 16):
        total = total + kept[8 * v : 8 * v + 8, :]
    return total


def apply_pair(i, half_ref, cond_ref, xs_ref, ys_ref, t_ref, u_ref):
    tile_a = jnp.concatenate([cond_ref[2 * i]] * 16, axis=0)
    tile_c = jnp.concatenate([cond_ref[2 * i + 1]] * 16, axis=0)
    t_ref[0] = dot(spread(xs_ref[2 * i]), tile_a)
    t_ref[1] = dot(spread(xs_ref[2 * i + 1]), tile_c)
    for part in range(2):
        at = slice(128 * part, 128 * part + 128)
        t_c = [t_ref[1, 8 * w : 8 * w + 8, at] for w in range(16)]
        u_c = [None] * 16
        for v in range(16):
            t_a = t_ref[0, 8 * v : 8 * v + 8, at]
            sums = [None] * 2
            for w in range(16):
                row = 16 * v + w
                h = jnp.broadcast_to(half_ref[2 * i + part, row : row + 1, :], (8, 128))
                one, two = h * t_c[w], h * t_a
                sums[w % 2] = one if w < 2 else sums[w % 2] + one
                u_c[w] = two if v == 0 else u_c[w] + two
            u_ref[0, 8 * v : 8 * v + 8, at] = sums[0] + sums[1]
        for w in range(16):
            u_ref[1, 8 * w : 8 * w + 8, at] = u_c[w]
    ys_ref[2 * i] = gathered(dot_t(u_ref[0].astype(BF), tile_a))
    ys_ref[2 * i + 1] = gathered(dot_t(u_ref[1].astype(BF), tile_c))


def first_kernel(
    plane_ref, wide_ref, cond_ref, scr_ref, base_ref, op_ref, res_ref,
    xs_ref, ys_ref, t_ref, u_ref, rs_ref, half_ref,
):
    for e in range(6):
        op_ref[0, 768 + 16 * e : 784 + 16 * e, :] = cond_ref[e, :, 0:128]
        op_ref[1, 768 + 16 * e : 784 + 16 * e, :] = cond_ref[e, :, 128:256]
    for part in range(4):
        tail = wide_ref[part, 96:112, :].astype(F32)
        for e in range(6):
            xs_ref[e, 2 * part : 2 * part + 2, :] = tail[2 * e : 2 * e + 2, :]

    def one(i, carry):
        slot = plane_ref[lax.axis_index(PLANE), 0, 8 + i]
        total = jnp.zeros((256, 256), F32)
        for part in range(4):
            at = aligned(i * 32, 16)
            a = wide_ref[part, pl.ds(at, 16), :]
            b = wide_ref[part, pl.ds(at + 16, 16), :]
            left = jnp.concatenate([a[v : v + 1, :] * b for v in range(16)], axis=0)
            total = total + dot(left, scr_ref[slot, part * 256 : (part + 1) * 256, :])
        total = total.astype(BF)
        at = aligned(i * 256, 256)
        op_ref[0, pl.ds(at, 256), :] = total[:, 0:128]
        op_ref[1, pl.ds(at, 256), :] = total[:, 128:256]
        total = total.astype(F32)
        half_ref[2 * i] = total[:, 0:128]
        half_ref[2 * i + 1] = total[:, 128:256]
        apply_pair(i, half_ref, cond_ref, xs_ref, ys_ref, t_ref, u_ref)
        return carry

    for i in range(3):
        one(i, 0)
    for part in range(4):
        for e in range(6):
            rs_ref[part, 2 * e : 2 * e + 2, :] = ys_ref[e, 2 * part : 2 * part + 2, :]
        mine = (lax.axis_index("y") == part).astype(F32)
        rs_ref[part, 12:16, :] = base_ref[...] * mine
    for peer in range(8):
        for part in range(4):
            res_ref[4 * peer + part] = rs_ref[part].astype(BF)


def middle_kernel(route_ref, got_ref, out_ref):
    peers = []
    for peer in range(8):
        total = got_ref[4 * peer].astype(F32)
        for part in range(1, 4):
            total = total + got_ref[4 * peer + part].astype(F32)
        peers.append(total.astype(BF))
    full = dot(route_ref[...], jnp.concatenate(peers, axis=0))
    out_ref[...] = full.astype(BF).reshape(16, 16, 256)


def picker(rows, columns):
    row = lax.broadcasted_iota(jnp.int32, (rows, columns), 0)
    return (lax.rem(row, 16) == lax.rem(lanes(rows, columns), 16)).astype(BF)


def second_kernel(
    got_ref, own_ref, op_ref, left_ref, right_ref, far_ref, rest_ref, out_ref, own_x_ref,
    x_ref, y_ref, t_ref, ua_ref, uc_ref, rs_ref, ds_ref,
):
    total = got_ref[0].astype(F32)
    for z in range(1, 16):
        total = total + got_ref[z].astype(F32)
    own_x_ref[...] = total[12:16, :]
    parts = density_of(own_ref, [total[12 + 2 * s : 14 + 2 * s, :].astype(BF) for s in range(2)])
    for part in range(4):
        for h in range(2):
            at = 4 * part + 2 * h
            ds_ref[at : at + 2, :] = parts[part][:, 128 * h : 128 * h + 128]

    here = lanes(16, 256) // 16 == lax.broadcasted_iota(jnp.int32, (16, 256), 0)
    rows = [jnp.where(here, total[k : k + 1, :], 0.0).astype(BF) for k in range(12)]
    x_ref[...] = dot(jnp.concatenate(rows, axis=0), picker(256, 16)).astype(BF)

    chunks = [(ref, h) for ref in (op_ref, left_ref, right_ref) for h in range(2)]
    chunks += [(far_ref, 0), (rest_ref, 0)]

    def one(p, carry):
        at = aligned(p * 64, 64)
        conds = []
        for end in range(2):
            row = aligned(768 + p * 32 + end * 16, 16)
            conds.append(
                jnp.concatenate([ref[h, pl.ds(row, 16), :] for ref, h in chunks], axis=1)
            )
            t_ref[end] = dot(x_ref[pl.ds(aligned(at + 32 * end, 32), 32), :], conds[end])
        for k, (ref, h) in enumerate(chunks):
            span = slice(128 * k, 128 * k + 128)
            t_c = [t_ref[1, 8 * g : 8 * g + 8, span] for g in range(4)]
            sums = [None] * 4
            for v in range(16):
                tile = ref[h, pl.ds(aligned(p * 256 + 16 * v, 16), 16), :].astype(F32)
                lo, hi = tile[0:8, :], tile[8:16, :]
                for n in range(2):
                    ua_ref[128 * n + 8 * v : 128 * n + 8 * v + 8, span] = (
                        lo * t_c[2 * n] + hi * t_c[2 * n + 1]
                    )
                    t_a = jnp.broadcast_to(
                        t_ref[0, 16 * n + v : 16 * n + v + 1, span], (8, 128)
                    )
                    for g, part in ((2 * n, lo * t_a), (2 * n + 1, hi * t_a)):
                        sums[g] = part if v == 0 else sums[g] + part
            for g in range(4):
                uc_ref[8 * g : 8 * g + 8, span] = sums[g]
        first = dot_t(ua_ref[...].astype(BF), conds[0])
        y_ref[pl.ds(at, 32), :] = jnp.sum(first.reshape(32, 8, 16), axis=1)
        y_ref[pl.ds(aligned(at + 32, 32), 32), :] = dot_t(uc_ref[...].astype(BF), conds[1])
        return carry

    for p in range(3):
        one(p, 0)
    full = dot(y_ref[...].astype(BF), picker(16, 256)).reshape(12, 16, 256)
    rs_ref[0:12, :] = jnp.sum(jnp.where(here[None], full, 0.0), axis=1)
    rs_ref[12:16, :] = jnp.zeros((4, 256), F32)
    for peer in range(8):
        out_ref[peer, :, 0:256] = rs_ref[...].astype(BF)
        out_ref[peer, :, 256:384] = ds_ref[...].astype(BF)


def return_kernel(back_ref, got_ref, out_ref, buf_ref):
    full = dot(back_ref[...], got_ref[:, :, 0:256].reshape(128, 256))
    total = got_ref[0, :, 256:384].astype(F32)
    for peer in range(1, 8):
        total = total + got_ref[peer, :, 256:384].astype(F32)
    for part in range(4):
        for h in range(2):
            at = 4 * part + 2 * h
            span = slice(128 * h, 128 * h + 128)
            buf_ref[0, 2 * part : 2 * part + 2, span] = total[at : at + 2, :]
    for z in range(16):
        if z:
            buf_ref[z, :, 0:256] = buf_ref[0, :, 0:256]
        for h in range(2):
            span = slice(128 * h, 128 * h + 128)
            buf_ref[z, 4 * h : 4 * h + 4, 256:384] = full[4 * z : 4 * z + 4, span]
    out_ref[...] = buf_ref[...].astype(BF)


def last_kernel(cheb_ref, got_ref, own_ref, bare_ref, held_ref, own_x_ref, out_ref):
    total = got_ref[0].astype(F32)
    for z in range(1, 16):
        total = total + got_ref[z].astype(F32)
    dens = [total[2 * part : 2 * part + 2, 0:256] for part in range(4)]
    rows = jnp.concatenate([total[0:4, 256:384], total[4:8, 256:384]], axis=1)
    terms = bare_of(own_ref, bare_ref, dens)
    for s in range(2):
        x = own_x_ref[2 * s : 2 * s + 2, :]
        t = held_ref[2 * s : 2 * s + 2, :]
        applied = (
            held_ref[4 + s : 5 + s, :] * x.astype(BF).astype(F32)
            + 2.0 * terms[s]
            + rows[2 * s : 2 * s + 2, :]
        )
        second = 2.0 * applied - t
        out_ref[:, s, :] = cheb_ref[0] * t + cheb_ref[1] * x + cheb_ref[2] * second


def body(orbitals, transition, trial, screened, bare, cheb, pair_k, pair_slot, k_order):
    (copies,) = call(
        copies_kernel, [((4, 2, 32, 256), BF)], (), [pltpu.SemaphoreType.DMA((4,))], (0,),
        out_space=pltpu.HBM,
    )(stay(orbitals))
    far_bare = stay(bare)
    own = exchange(copies, "y")
    ids, held = call(
        info_kernel,
        [((8, 1, 128), jnp.int32), ((8, 256), F32)],
        (),
        [
            pltpu.SMEM((3,), jnp.int32),
            pltpu.SMEM((3,), jnp.int32),
            pltpu.VMEM((1, 256), jnp.int32),
            pltpu.VMEM((2, 2, 256), F32),
            pltpu.VMEM((2, 256), F32),
            pltpu.SemaphoreType.DMA((5,)),
        ],
        range(5),
    )(*map(stay, (pair_k, pair_slot, k_order.reshape(1, -1), trial, transition)))
    plane = exchange(ids, PLANE)
    (packed,) = call(pack_kernel, [((80, 256), BF)], (), [pltpu.VMEM((16, 256), F32)])(held, own)
    gat = lax.all_gather(packed, "z")
    twin = swap(gat)
    chosen, column = call(
        select_kernel,
        [((4, 224, 256), BF), ((8, 256), F32)],
        (0,),
        [pltpu.VMEM((128, 512), F32)],
    )(plane, gat, twin)
    got = exchange(chosen, "x")
    (scr,) = call(
        fetch_kernel, [(screened.shape, BF)], (), [pltpu.SemaphoreType.DMA(())], (0,)
    )(stay(screened))
    val, cond, dens = call(
        accept_kernel,
        [((4, 112, 256), BF), ((6, 16, 256), BF), ((8, 256), F32)],
        (0,),
        [pltpu.VMEM((16, 256), F32)],
    )(plane, got)
    wide = exchange(val, "y")
    base, route, back = call(
        base_kernel,
        [((4, 256), F32), ((256, 128), BF), ((64, 128), BF)],
        (0,),
        [
            pltpu.VMEM((4, 256), F32),
            pltpu.VMEM((128, 256), F32),
            pltpu.VMEM(bare.shape, BF),
            pltpu.SemaphoreType.DMA(()),
        ],
        (4,),
    )(plane, dens, column, own, far_bare, held)
    work = [
        pltpu.VMEM((6, 8, 256), F32),
        pltpu.VMEM((6, 8, 256), F32),
        pltpu.VMEM((2, 128, 256), F32),
        pltpu.VMEM((2, 128, 256), F32),
        pltpu.VMEM((4, 16, 256), F32),
    ]
    op, res = call(
        first_kernel,
        [((2, 864, 128), BF), ((32, 16, 256), BF)],
        (0,),
        work + [pltpu.VMEM((6, 256, 128), F32)],
    )(plane, wide, cond, scr, base)
    mixed = exchange(res, BLOCK)
    left = shift(op, 1)
    right = shift(op, -1)
    (middle,) = call(middle_kernel, [((16, 16, 256), BF)], ())(route, mixed)
    step = exchange(middle, "z")
    far = shift(left[0], 1)
    rest = shift(right[1], -1)
    out2, own_x = call(
        second_kernel,
        [((8, 16, 384), BF), ((4, 256), F32)],
        (),
        [
            pltpu.VMEM((192, 16), BF),
            pltpu.VMEM((192, 16), F32),
            pltpu.VMEM((2, 32, 1024), F32),
            pltpu.VMEM((256, 1024), F32),
            pltpu.VMEM((32, 1024), F32),
            pltpu.VMEM((16, 256), F32),
            pltpu.VMEM((16, 128), F32),
        ],
    )(step, own, op, left, right, far[None], rest[None])
    returned = exchange(out2, PLANE)
    (final,) = call(return_kernel, [((16, 8, 384), BF)], (), [pltpu.VMEM((16, 8, 384), F32)])(
        back, returned
    )
    last = exchange(final, "z")
    (near_bare,) = call(
        fetch_kernel, [(bare.shape, BF)], (), [pltpu.SemaphoreType.DMA(())], (0,)
    )(far_bare)
    (result,) = call(last_kernel, [(trial.shape, F32)], (0,))(
        cheb, last, own, near_bare, held, own_x
    )
    return result


def solution(mesh):
    split = Mesh(mesh.devices.reshape(16, 4, 2, mesh.shape["vert"]), ("z", "x", "c", "y"))
    in_specs = (
        P(PB, None, "y"),
        P(PB, None),
        P("y", PB, None),
        P(PB, None, "y"),
        P(),
        P(),
        P(PB),
        P(PB),
        P(),
    )
    out_specs = P("y", PB, None)
    return jax.shard_map(body, mesh=split, in_specs=in_specs, out_specs=out_specs, check_vma=False)
```
